32 devices in a mesh: tile: 2 (over core), level: 2 (over x), member: 8 (over z, y).
Axes of the slice: x: 2, y: 2, z: 4, core: 2. Of those that a mesh axis runs over, the one named last changes fastest.
Arguments:
- temp_salt: float32 [16, 2, 2, 128, 1024], P('member', None, 'level', None, 'tile'), may hold values from -6 to 6
- diffusivity: float32 [3, 128, 1024], P(None, None, 'tile'), may hold values from -0.1 to 0.2, as said below
- wet_rank: int32 [8], P('tile'), may hold values from -1 to 3, as said below
- land_rows: int32 [1024], P('tile'), may hold values from 0 to 42
- obs_cell: int32 [1024], P(('tile', 'level')), may hold values from 0 to 65022, as said below
- obs_frac: float32 [2, 1024], P(None, ('tile', 'level')), may hold values from 0 to 1
Outputs:
- final_field: float32 [16, 2, 2, 128, 1024], P('member', None, 'level', None, 'tile')
- obs_anomaly: float32 [16, 2, 1024], P('member', None, ('tile', 'level'))
- obs_variance: float32 [2, 1024], P(None, ('tile', 'level'))
The draws below stay inside these ranges and needn't reach their ends.
Inputs may be any that keep to these rules, and one draw needn't show every extreme that they name: `wet_rank`: -1 marks a land tile; the wet tiles carry the ranks 0 to 3 in increasing order of tile index, so exactly half of the tiles are wet. `diffusivity`: kxx and kyy positive, kxy at most half of sqrt(kxx kyy) in magnitude. `obs_cell`: indices are local to the observation's block as in the reference program, with row below 127 and column offset below 511.
All inputs are finite; a program needn't handle non-finite values.
Results may differ from the reference program's by a relative error of at most 0.00002.
Values sent between devices are 32-bit elements; how exact they have to be, the bound alone decides.
No kernel may reach another device: no remote copies, remote signals or barrier semaphores. Data moves between devices by JAX's collectives and lax.ppermute only.
A program may use at most 192 MiB of HBM per device.

```python
import jax
import jax.numpy as jnp
from jax import lax

TILE = 128
TD = 4
LV_DEV = 1
STEPS = 6
OBS_DEV = 256
TILES = 8
LEVELS = 2
MEMBERS = 16
NOBS = 1024


def draw_diffusivity(key, part):
    key_xx, key_yy, key_xy = jax.random.split(key, 3)
    shape_now = (TILE, TILES * TILE)
    kappa_xx = jnp.exp(jax.random.uniform(key_xx, shape_now, jnp.float32, jnp.log(0.02), jnp.log(0.2)))
    kappa_yy = jnp.exp(jax.random.uniform(key_yy, shape_now, jnp.float32, jnp.log(0.02), jnp.log(0.2)))
    tilt = jax.random.uniform(key_xy, shape_now, jnp.float32, -0.5, 0.5)
    kappa_xy = tilt * jnp.sqrt(kappa_xx * kappa_yy)
    return jnp.stack([kappa_xx, kappa_yy, kappa_xy], axis=0).astype(jnp.float32)


def draw_wet_rank(key, part):
    groups = TILES // TD
    run_length = TILES // 2 - 1
    lowest_offset = max(1, TD - run_length + 1)
    key_group, key_offset, key_extra = jax.random.split(key, 3)
    start_group = jax.random.randint(key_group, (), 0, groups)
    start_offset = jax.random.randint(key_offset, (), lowest_offset, TD)
    run_start = start_group * TD + start_offset
    tile_numbers = jnp.arange(TILES, dtype=jnp.int32)
    in_run = jnp.mod(tile_numbers - run_start, TILES) < run_length
    scores = jax.random.permutation(key_extra, tile_numbers)
    masked_scores = jnp.where(in_run, -1, scores)
    extra_tile = jnp.argmax(masked_scores).astype(jnp.int32)
    wet_flags = in_run | (tile_numbers == extra_tile)
    wet_ranks = jnp.cumsum(wet_flags.astype(jnp.int32)) - 1
    return jnp.where(wet_flags, wet_ranks, -1).astype(jnp.int32)


def draw_obs_cell(key, part):
    key_level, key_row, key_column = jax.random.split(key, 3)
    level_pick = jax.random.randint(key_level, (NOBS,), 0, LV_DEV)
    row_pick = jax.random.randint(key_row, (NOBS,), 0, TILE - 1)
    column_pick = jax.random.randint(key_column, (NOBS,), 0, TD * TILE - 1)
    flat_cells = ((level_pick * TILE + row_pick) * (TD * TILE) + column_pick).astype(jnp.int32)
    top_cell = (LV_DEV * TILE - 1) * TD * TILE - 2
    flat_cells = flat_cells.at[0].set(top_cell)
    flat_cells = flat_cells.at[1].set(0)
    return flat_cells.astype(jnp.int32)


def place_ends(array, own_key, least, high):
    extent = array.shape
    place = [jax.random.randint(jax.random.fold_in(own_key, axis), (), 0, extent[axis]) for axis in range(len(extent))]
    array = array.at[tuple(place)].set(least)
    longest = extent.index(max(extent))
    place[longest] = (place[longest] + 1) % extent[longest]
    return array.at[tuple(place)].set(high)


def block_levels(key, dims, shards, low, top_value):
    level = 1.0
    for position, parts in shards:
        heights = jax.random.uniform(jax.random.fold_in(jax.random.fold_in(key, 6), position), (parts,), jnp.float32, low / len(shards), top_value / len(shards))
        level = level * jnp.repeat(jnp.exp(heights), dims[position] // parts).reshape((-1,) + (1,) * (len(dims) - 1 - position))
    return level


def gaussian(key, dims, scale, limit, cuts=(), held_as=jnp.bfloat16):
    array = scale * jax.random.normal(key, dims, jnp.float32)
    if cuts:
        array = array * block_levels(key, dims, cuts, -0.22, 0.18)
    return jnp.clip(array, -limit, limit).astype(held_as)


def setup_inputs(seed: int = 0) -> dict:
    key_list = jax.random.split(jax.random.key(seed), 7)
    return {
        "temp_salt": gaussian(key_list[0], (MEMBERS, 2, LEVELS, TILE, TILES * TILE), 1.0, 6.0, ((0, 8), (2, 2), (4, 2)), jnp.float32),
        "diffusivity": draw_diffusivity(jax.random.fold_in(key_list[6], 71), 0),
        "wet_rank": draw_wet_rank(jax.random.fold_in(key_list[6], 71), 0),
        "land_rows": place_ends(jax.random.randint(key_list[3], (TILES * TILE,), 0, TILE // 3 + 1), jax.random.fold_in(key_list[3], 1), 0, (TILE // 3 + 1) - 1).astype(jnp.int32),
        "obs_cell": draw_obs_cell(jax.random.fold_in(key_list[6], 71), 0),
        "obs_frac": jnp.clip(1.0 * jax.random.uniform(key_list[5], (2, NOBS), jnp.float32) ** block_levels(key_list[5], (2, NOBS), ((1, 4),), -0.2, 0.2), 0.0, 1.0),
    }


def east_of(values):
    return jnp.roll(values, -1, axis=-1)


def west_of(values):
    return jnp.roll(values, 1, axis=-1)


def north_of(values):
    return jnp.concatenate([values[..., 1:, :], jnp.zeros_like(values[..., :1, :])], axis=-2)


def south_of(values):
    return jnp.concatenate([jnp.zeros_like(values[..., :1, :]), values[..., :-1, :]], axis=-2)


def face_terms(kappa_xx, kappa_yy, kappa_xy, wet_cells):
    x_gate = wet_cells * east_of(wet_cells)
    y_gate = wet_cells * north_of(wet_cells)
    along_x = 0.5 * (kappa_xx + east_of(kappa_xx)) * x_gate
    cross_x = 0.125 * (kappa_xy + east_of(kappa_xy)) * x_gate
    along_y = 0.5 * (kappa_yy + north_of(kappa_yy)) * y_gate
    cross_y = 0.125 * (kappa_xy + north_of(kappa_xy)) * y_gate
    return along_x, cross_x, along_y, cross_y, wet_cells


def diffuse(field_now, face_set):
    along_x, cross_x, along_y, cross_y, wet_cells = face_set
    east_vals = east_of(field_now)
    north_vals = north_of(field_now)
    pair_x = field_now + east_vals
    flux_x = along_x * (east_vals - field_now) + cross_x * (north_of(pair_x) - south_of(pair_x))
    pair_y = field_now + north_vals
    flux_y = along_y * (north_vals - field_now) + cross_y * (east_of(pair_y) - west_of(pair_y))
    return field_now + wet_cells * (flux_x - west_of(flux_x) + flux_y - south_of(flux_y))


def reference(temp_salt, diffusivity, wet_rank, land_rows, obs_cell, obs_frac):
    members, fields, levels, rows_count, columns = temp_salt.shape
    tiles_total = wet_rank.shape[0]
    tile_cells = columns // tiles_total
    wet_column = jnp.repeat(wet_rank >= 0, tile_cells)
    row_numbers = jnp.arange(rows_count, dtype=jnp.int32)
    wet_cells = ((row_numbers[:, None] >= land_rows[None, :]) & wet_column[None, :]).astype(jnp.float32)
    face_set = face_terms(diffusivity[0], diffusivity[1], diffusivity[2], wet_cells)

    def evolve(member_block):
        field_now = member_block * wet_cells
        for step_index in range(STEPS):
            field_now = diffuse(field_now, face_set)
        return field_now

    stepped = lax.map(evolve, temp_salt.reshape(members * fields, levels, rows_count, columns))
    stepped = stepped.reshape(members, fields, levels, rows_count, columns)
    sample_count = members * levels
    column_mean = jnp.sum(stepped, axis=(0, 2)) / sample_count
    final_field = stepped - column_mean[None, :, None]

    total_obs = obs_cell.shape[0]
    level_groups = LEVELS // LV_DEV
    block_index = jnp.arange(total_obs, dtype=jnp.int32) // OBS_DEV
    block_columns = TD * TILE
    column_pick = (block_index // level_groups) * block_columns + obs_cell % block_columns
    row_pick = (obs_cell // block_columns) % TILE
    level_pick = (block_index % level_groups) * LV_DEV + obs_cell // (block_columns * TILE)
    south_west = final_field[:, :, level_pick, row_pick, column_pick]
    south_east = final_field[:, :, level_pick, row_pick, column_pick + 1]
    north_west = final_field[:, :, level_pick, row_pick + 1, column_pick]
    north_east = final_field[:, :, level_pick, row_pick + 1, column_pick + 1]
    east_weight = obs_frac[0]
    north_weight = obs_frac[1]
    observed = ((1.0 - east_weight) * (1.0 - north_weight) * south_west + east_weight * (1.0 - north_weight) * south_east
                + (1.0 - east_weight) * north_weight * north_west + east_weight * north_weight * north_east)
    centre = jnp.sum(observed, axis=0) / members
    obs_anomaly = observed - centre[None]
    obs_variance = jnp.sum(obs_anomaly * obs_anomaly, axis=0) / members
    return final_field, obs_anomaly, obs_variance
```

```python
import functools

import jax
import jax.numpy as jnp
from jax import lax
from jax.experimental import pallas as pl
from jax.experimental.pallas import tpu as pltpu
from jax.sharding import PartitionSpec as P

STEPS = 6
LANES = 128
PAD = 8
ALL_AXES = ("tile", "level", "member")
VMEM = pl.BlockSpec(memory_space=pltpu.VMEM)
SMEM = pl.BlockSpec(memory_space=pltpu.SMEM)
HIGHEST = lax.Precision.HIGHEST


def chunk_number():
    member = lax.axis_index("member")
    core = lax.axis_index("tile")
    low = lax.rem(member, 2)
    high = lax.rem(member // 2, 2)
    mine = jnp.where(core == 0, 2 * high + low, 2 * low + high)
    other = jnp.where(core == 0, 2 * low + high, 2 * high + low)
    return core, mine, other


def wet_mask(land_ref, rank_ref, tile, rows):
    row = lax.broadcasted_iota(jnp.int32, (rows, LANES), 0)
    land = land_ref[pl.ds(tile, 1), :]
    dry = jnp.where(rank_ref[tile] >= 0, 0, rows)
    return (row >= jnp.maximum(land, dry)).astype(jnp.float32)


def edge_block(first, last):
    lane = lax.broadcasted_iota(jnp.int32, first.shape, len(first.shape) - 1)
    return jnp.where(lane < LANES // 2, first, last)


def prepare_kernel(sizes, rank_ref, temp_ref, kappa_ref, land_ref, send_ref, keep_ref, edge_ref):
    members, fields, rows, tiles = sizes
    core, mine, other = chunk_number()
    planes = members * fields
    send_ref[...] = jnp.zeros_like(send_ref)
    keep_ref[...] = jnp.zeros_like(keep_ref)
    for tile in range(tiles):
        lanes = slice(tile * LANES, (tile + 1) * LANES)

        @pl.when(rank_ref[tile] >= 0)
        def _():
            rank = rank_ref[tile]
            wet = wet_mask(land_ref, rank_ref, tile, rows)
            for ref, slot, field in ((keep_ref, mine, core), (send_ref, other, 1 - core)):
                total = temp_ref[field, :, lanes] * wet
                for member in range(1, members):
                    total = total + temp_ref[member * fields + field, :, lanes] * wet
                ref[jnp.bitwise_xor(slot, rank)] = total

    wet_first = wet_mask(land_ref, rank_ref, 0, rows)
    wet_last = wet_mask(land_ref, rank_ref, tiles - 1, rows)
    last = (tiles - 1) * LANES
    for plane in range(planes):
        edge_ref[plane] = edge_block(
            temp_ref[plane, :, :LANES] * wet_first, temp_ref[plane, :, last:] * wet_last
        )
    for part in range(3):
        edge_ref[planes + part] = edge_block(kappa_ref[part, :, :LANES], kappa_ref[part, :, last:])
    edge_ref[planes + 3] = edge_block(wet_first, wet_last)


def weights_kernel(sizes, rank_ref, kappa_ref, kappa_edge_ref, land_ref, weight_ref):
    members, fields, rows, tiles = sizes
    width = (tiles + 1) * LANES
    base = members * fields
    row = lax.broadcasted_iota(jnp.int32, (rows, width), 0)

    def east(x):
        return pltpu.roll(x, width - 1, axis=1)

    def west(x):
        return pltpu.roll(x, 1, axis=1)

    def north(x):
        return jnp.where(row == rows - 1, 0.0, pltpu.roll(x, rows - 1, axis=0))

    def south(x):
        return jnp.where(row == 0, 0.0, pltpu.roll(x, 1, axis=0))

    kappas = [
        jnp.concatenate([kappa_ref[part], kappa_edge_ref[base + part]], axis=1) for part in range(3)
    ]
    wet = jnp.concatenate(
        [wet_mask(land_ref, rank_ref, tile, rows) for tile in range(tiles)]
        + [kappa_edge_ref[base + 3]],
        axis=1,
    )
    kxx, kyy, kxy = kappas
    x_gate = wet * east(wet)
    y_gate = wet * north(wet)
    ax = 0.5 * (kxx + east(kxx)) * x_gate
    cx = 0.125 * (kxy + east(kxy)) * x_gate
    ay = 0.5 * (kyy + north(kyy)) * y_gate
    cy = 0.125 * (kxy + north(kxy)) * y_gate
    axw, cxw, ays, cys = west(ax), west(cx), south(ay), south(cy)
    groups = (
        (lambda x: x, (1.0 - wet * (ax + axw + ay + ays), wet * (ay + cx - cxw), wet * (ays - cx + cxw))),
        (west, (wet * (ax + cy - cys), wet * (cx + cy), wet * (-cx - cys))),
        (east, (wet * (axw - cy + cys), wet * (-cxw - cy), wet * (cxw + cys))),
    )
    for group, (move, terms) in enumerate(groups):
        for part, term in enumerate(terms):
            held = move(term)
            for tile in range(tiles + 1):
                weight_ref[3 * group + part, tile] = held[:, tile * LANES : (tile + 1) * LANES]


def run_steps(planes, rows, tiles, weight_ref, u_ref):
    lane = lax.broadcasted_iota(jnp.int32, (8, LANES), 1)
    is_first, is_last = lane == 0, lane == LANES - 1

    def one_step(source, target):
        for block in range(rows // 8):
            base = PAD + 8 * block
            row0 = 8 * block
            parts = [[] for _ in range(planes)]
            for tile in range(tiles + 1):
                weights = [weight_ref[k, tile, row0 : row0 + 8, :] for k in range(9)]
                for plane in range(planes):
                    here = u_ref[source, plane, tile, base : base + 8, :]
                    up = u_ref[source, plane, tile, base + 1 : base + 9, :]
                    down = u_ref[source, plane, tile, base - 1 : base + 7, :]
                    group = [
                        weights[3 * g] * here + weights[3 * g + 1] * up + weights[3 * g + 2] * down
                        for g in range(3)
                    ]
                    parts[plane].append(
                        (group[0], pltpu.roll(group[1], LANES - 1, axis=1), pltpu.roll(group[2], 1, axis=1))
                    )
            for plane in range(planes):
                for tile in range(tiles + 1):
                    centre, from_east, from_west = parts[plane][tile]
                    after = parts[plane][(tile + 1) % (tiles + 1)][1]
                    before = parts[plane][tile - 1][2]
                    u_ref[target, plane, tile, base : base + 8, :] = (
                        centre
                        + jnp.where(is_last, after, from_east)
                        + jnp.where(is_first, before, from_west)
                    )

    def two_steps(_, carry):
        one_step(0, 1)
        one_step(1, 0)
        return carry

    lax.fori_loop(0, STEPS // 2, two_steps, 0)


def clear_pads(planes, rows, tiles, u_ref):
    zeros = jnp.zeros((PAD, LANES), jnp.float32)
    for slot in range(2):
        for plane in range(planes):
            for tile in range(tiles + 1):
                u_ref[slot, plane, tile, :PAD, :] = zeros
                u_ref[slot, plane, tile, PAD + rows :, :] = zeros


def bilinear(field, cell, frac_east, frac_north):
    columns = field.shape[1]
    count = cell.shape[1]
    column = jnp.bitwise_and(cell, columns - 1) if columns & (columns - 1) == 0 else lax.rem(cell, columns)
    at = lax.broadcasted_iota(jnp.int32, (columns, count), 0)
    pick = jnp.where(at == column, 1.0 - frac_east, 0.0) + jnp.where(at == column + 1, frac_east, 0.0)
    return jnp.dot(field, pick, precision=HIGHEST, preferred_element_type=jnp.float32)


def row_pick(picked, planes, rows, columns, cell, frac_north):
    count = cell.shape[1]
    row = lax.rem(cell // columns, rows)
    at = lax.broadcasted_iota(jnp.int32, (rows, count), 0)
    pick = jnp.where(at == row, 1.0 - frac_north, 0.0) + jnp.where(at == row + 1, frac_north, 0.0)
    return [
        jnp.sum(picked[plane * rows : (plane + 1) * rows] * pick, axis=0, keepdims=True)
        for plane in range(planes)
    ]


def member_kernel(
    sizes, first, count, rank_ref, temp_ref, edge_ref, land_ref, weight_ref, cell_ref, frac_ref,
    stepped_ref, seen_ref, u_ref,
):
    members, fields, rows, tiles = sizes
    clear_pads(count, rows, tiles, u_ref)
    for tile in range(tiles):
        wet = wet_mask(land_ref, rank_ref, tile, rows)
        for plane in range(count):
            u_ref[0, plane, tile, PAD : PAD + rows, :] = (
                temp_ref[first + plane, :, tile * LANES : (tile + 1) * LANES] * wet
            )
    for plane in range(count):
        u_ref[0, plane, tiles, PAD : PAD + rows, :] = edge_ref[first + plane]
    run_steps(count, rows, tiles, weight_ref, u_ref)
    for plane in range(count):
        for tile in range(tiles):
            stepped_ref[plane, :, tile * LANES : (tile + 1) * LANES] = u_ref[0, plane, tile, PAD : PAD + rows, :]
    observe_planes(count, rows, tiles, stepped_ref, cell_ref, frac_ref, seen_ref)


def observe_planes(count, rows, tiles, field_ref, cell_ref, frac_ref, seen_ref):
    cell = cell_ref[...]
    frac_east, frac_north = frac_ref[0:1, :], frac_ref[1:2, :]
    field = field_ref[...].reshape(count * rows, tiles * LANES)
    picked = bilinear(field, cell, frac_east, frac_north)
    seen = row_pick(picked, count, rows, tiles * LANES, cell, frac_north)
    for plane in range(count):
        seen_ref[plane : plane + 1, :] = seen[plane]


def final_kernel(
    sizes, samples, ensemble, slots,
    rank_ref, mine_ref, other_ref, edge_ref, land_ref, weight_ref, cell_ref, frac_ref, stepped_refs, seen_ref,
    field_ref, anomaly_ref, variance_ref, u_ref, mean_ref, mean_seen_ref,
):
    members, fields, rows, tiles = sizes
    core, mine, other = chunk_number()
    owned = jnp.int32(0)
    for tile in range(tiles):
        owned = owned + (rank_ref[tile] >= 0).astype(jnp.int32)
    first_rank = jnp.clip(jnp.where(core == 0, owned, 0), 0, slots - 1)
    last_rank = jnp.clip(jnp.where(core == 0, slots - 1, slots - owned - 1), 0, slots - 1)
    clear_pads(fields, rows, tiles, u_ref)
    wet_edge = edge_ref[members * fields + 3]
    scale = 1.0 / samples

    def total(field, rank):
        own = mine_ref[jnp.bitwise_xor(mine, rank)]
        theirs = other_ref[jnp.bitwise_xor(other, rank)]
        return jnp.where(core == field, own, theirs) * scale

    for field in range(fields):
        for tile in range(tiles):
            rank = rank_ref[tile]
            wet = wet_mask(land_ref, rank_ref, tile, rows)
            u_ref[0, field, tile, PAD : PAD + rows, :] = total(field, jnp.maximum(rank, 0)) * wet
        u_ref[0, field, tiles, PAD : PAD + rows, :] = (
            edge_block(total(field, first_rank), total(field, last_rank)) * wet_edge
        )
    run_steps(fields, rows, tiles, weight_ref, u_ref)
    for field in range(fields):
        for tile in range(tiles):
            lanes = slice(tile * LANES, (tile + 1) * LANES)
            mean = u_ref[0, field, tile, PAD : PAD + rows, :]
            mean_ref[field, :, lanes] = mean
            for member in range(members):
                plane = member * fields + field
                per_ref = field_ref.shape[0] // len(stepped_refs)
                field_ref[plane, :, lanes] = stepped_refs[plane // per_ref][plane % per_ref, :, lanes] - mean
    observe_planes(fields, rows, tiles, mean_ref, cell_ref, frac_ref, mean_seen_ref)
    planes = members * fields
    count = cell_ref.shape[1]
    sets = seen_ref.shape[0] // planes

    def tree(values):
        while len(values) > 1:
            values = [a + b for a, b in zip(values[0::2], values[1::2], strict=True)]
        return values[0]

    for field in range(fields):
        mean_seen = mean_seen_ref[field : field + 1, :]
        observed = []
        for part in range(sets):
            for member in range(members):
                at = part * planes + member * fields + field
                observed.append(seen_ref[at : at + 1, :] - mean_seen)
        centre = tree(observed) / ensemble
        anomaly = [value - centre for value in observed]
        variance_ref[field : field + 1, :] = tree([value * value for value in anomaly]) / ensemble
        for member in range(members):
            at = member * fields + field
            anomaly_ref[at : at + 1, :] = anomaly[member]


def local(temp_salt, diffusivity, wet_rank, land_rows, obs_cell, obs_frac):
    members, fields, levels, rows, columns = temp_salt.shape
    tiles = wet_rank.shape[0]
    cores, level_count, member_count = (lax.axis_size(axis) for axis in ALL_AXES)
    slots = tiles * cores // 2
    chips = level_count * member_count
    bits = chips.bit_length() - 1
    assert cores == 2 and fields == 2 and levels == 1 and slots == 4
    assert columns == tiles * LANES and chips == 1 << bits and bits >= 3
    count = obs_cell.shape[0]
    planes = members * fields
    sizes = (members, fields, rows, tiles)
    samples = members * levels * chips
    level_bit = bits - 1

    def device(core, chip):
        return core * chips + chip

    swap_pairs = [(device(core, chip), device(1 - core, chip)) for core in range(2) for chip in range(chips)]

    def pairs(bit_of_core):
        return [
            (device(core, chip), device(core, chip ^ (1 << bit_of_core[core])))
            for core in range(2)
            for chip in range(chips)
        ]

    def exchange(value, bit_of_core):
        return lax.ppermute(value, ALL_AXES, pairs(bit_of_core))

    def struct(*shape):
        return jax.ShapeDtypeStruct(shape, jnp.float32)

    temp = temp_salt.reshape(planes, rows, columns)
    land = land_rows.reshape(tiles, LANES)
    cell = obs_cell.reshape(1, count)

    send, keep, edge = pl.pallas_call(
        functools.partial(prepare_kernel, sizes),
        out_shape=(struct(slots, rows, LANES), struct(slots, rows, LANES), struct(planes + 4, rows, LANES)),
        in_specs=[SMEM, VMEM, VMEM, VMEM],
        out_specs=(VMEM, VMEM, VMEM),
        name="prepare",
    )(wet_rank, temp, diffusivity, land)

    arrived = lax.ppermute(send, ALL_AXES, swap_pairs)
    edges = lax.ppermute(edge, ALL_AXES, swap_pairs)
    total = keep + arrived
    total = total[:2] + exchange(total[2:], (1, 0))

    weights = pl.pallas_call(
        functools.partial(weights_kernel, sizes),
        out_shape=struct(9, tiles + 1, rows, LANES),
        in_specs=[SMEM, VMEM, VMEM, VMEM],
        out_specs=VMEM,
        cost_estimate=pl.CostEstimate(flops=6_000_000, bytes_accessed=4 << 20, transcendentals=0),
        name="weights",
    )(wet_rank, diffusivity, edges, land)

    per_call = 2
    stepped, seen = [], []
    for first in range(0, planes, per_call):
        out, looked = pl.pallas_call(
            functools.partial(member_kernel, sizes, first, per_call),
            out_shape=(struct(per_call, rows, columns), struct(per_call, count)),
            in_specs=[SMEM] + [VMEM] * 6,
            out_specs=(VMEM, VMEM),
            scratch_shapes=[pltpu.VMEM((2, per_call, tiles + 1, rows + 2 * PAD, LANES), jnp.float32)],
            cost_estimate=pl.CostEstimate(flops=20_000_000, bytes_accessed=8 << 20, transcendentals=0),
            name=f"member_steps_{first}",
        )(wet_rank, temp, edges, land, weights, cell, obs_frac)
        stepped.append(out)
        seen.append(looked)

    total = total[0] + exchange(total[1], (0, 1))
    seen = jnp.concatenate(seen, axis=0).reshape(planes * count // LANES, LANES)
    carried = False
    for bit in [level_bit] + list(range(2, level_bit)):
        if bit == level_bit:
            total = total + exchange(total, (bit, bit))
        else:
            got = exchange(jnp.concatenate([total, seen], axis=0), (bit, bit))
            total = total + got[:rows]
            seen = jnp.concatenate([seen, got[rows:]], axis=0)
    for bit_of_core in ((0, 1), (1, 0)):
        got = exchange(jnp.concatenate([total, seen], axis=0), bit_of_core)
        size = total.shape[0]
        total = jnp.concatenate([total, got[:size]], axis=0)
        seen = jnp.concatenate([seen, got[size:]], axis=0)
    mine = total.reshape(slots, rows, LANES)
    theirs = lax.ppermute(mine, ALL_AXES, swap_pairs)
    seen = seen.reshape(member_count * planes, count)

    def last_kernel(*refs):
        fixed, rest = refs[:8], refs[8:]
        stepped_refs, rest = rest[: len(stepped)], rest[len(stepped) :]
        final_kernel(sizes, samples, members * member_count, slots, *fixed, stepped_refs, *rest)

    field, anomaly, variance = pl.pallas_call(
        last_kernel,
        out_shape=(struct(planes, rows, columns), struct(planes, count), struct(fields, count)),
        in_specs=[SMEM] + [VMEM] * (8 + len(stepped)),
        out_specs=(VMEM, VMEM, VMEM),
        scratch_shapes=[
            pltpu.VMEM((2, fields, tiles + 1, rows + 2 * PAD, LANES), jnp.float32),
            pltpu.VMEM((fields, rows, columns), jnp.float32),
            pltpu.VMEM((fields, count), jnp.float32),
        ],
        name="recentre",
    )(wet_rank, mine, theirs, edges, land, weights, cell, obs_frac, *stepped, seen)
    return (
        field.reshape(members, fields, levels, rows, columns),
        anomaly.reshape(members, fields, count),
        variance,
    )


def solution(mesh):
    placed = (
        P("member", None, "level", None, "tile"),
        P(None, None, "tile"),
        P("tile"),
        P("tile"),
        P(("tile", "level")),
        P(None, ("tile", "level")),
    )
    return jax.shard_map(
        local,
        mesh=mesh,
        in_specs=placed,
        out_specs=(
            P("member", None, "level", None, "tile"),
            P("member", None, ("tile", "level")),
            P(None, ("tile", "level")),
        ),
        check_vma=False,
    )
```

```python
import functools

import jax
import jax.numpy as jnp
from jax import lax
from jax.experimental import pallas as pl
from jax.experimental.pallas import tpu as pltpu
from jax.sharding import PartitionSpec as P


STEPS = 6
LANES = 128
PAD = 8
ALL_AXES = ("tile", "level", "member")
VMEM = pl.BlockSpec(memory_space=pltpu.VMEM)
SMEM = pl.BlockSpec(memory_space=pltpu.SMEM)
HIGHEST = lax.Precision.HIGHEST
PARAMS = pltpu.CompilerParams(vmem_limit_bytes=20 << 20)


def chunk_number():
    member = lax.axis_index("member")
    core = lax.axis_index("tile")
    low = lax.rem(member, 2)
    high = lax.rem(member // 2, 2)
    mine = jnp.where(core == 0, 2 * high + low, 2 * low + high)
    other = jnp.where(core == 0, 2 * low + high, 2 * high + low)
    return core, mine, other


def wet_mask(land_ref, rank_ref, tile, rows):
    row = lax.broadcasted_iota(jnp.int32, (rows, LANES), 0)
    land = land_ref[pl.ds(tile, 1), :]
    dry = jnp.where(rank_ref[tile] >= 0, 0, rows)
    return (row >= jnp.maximum(land, dry)).astype(jnp.float32)


def edge_block(first, last):
    lane = lax.broadcasted_iota(jnp.int32, first.shape, len(first.shape) - 1)
    return jnp.where(lane < LANES // 2, first, last)


def sums_kernel(sizes, rank_ref, temp_ref, land_ref, send_ref, keep_ref):
    members, fields, rows, tiles = sizes
    core, mine, other = chunk_number()
    send_ref[...] = jnp.zeros_like(send_ref)
    keep_ref[...] = jnp.zeros_like(keep_ref)
    for tile in range(tiles):
        lanes = slice(tile * LANES, (tile + 1) * LANES)

        @pl.when(rank_ref[tile] >= 0)
        def _():
            rank = rank_ref[tile]
            wet = wet_mask(land_ref, rank_ref, tile, rows)
            for ref, slot, field in ((keep_ref, mine, core), (send_ref, other, 1 - core)):
                total = temp_ref[field, :, lanes] * wet
                for member in range(1, members):
                    total = total + temp_ref[member * fields + field, :, lanes] * wet
                ref[jnp.bitwise_xor(slot, rank)] = total


def edges_kernel(sizes, rank_ref, temp_ref, kappa_ref, land_ref, edge_ref):
    members, fields, rows, tiles = sizes
    planes = members * fields
    wet_first = wet_mask(land_ref, rank_ref, 0, rows)
    wet_last = wet_mask(land_ref, rank_ref, tiles - 1, rows)
    last = (tiles - 1) * LANES
    for plane in range(planes):
        edge_ref[plane] = edge_block(
            temp_ref[plane, :, :LANES] * wet_first, temp_ref[plane, :, last:] * wet_last
        )
    for part in range(3):
        edge_ref[planes + part] = edge_block(kappa_ref[part, :, :LANES], kappa_ref[part, :, last:])
    edge_ref[planes + 3] = edge_block(wet_first, wet_last)


def weights_kernel(sizes, rank_ref, kappa_ref, edge_ref, land_ref, weight_ref, pad_ref):
    members, fields, rows, tiles = sizes
    base = members * fields
    ring = tiles + 1
    zeros = jnp.zeros((PAD, LANES), jnp.float32)
    inside = slice(PAD, PAD + rows)
    for part in range(4):
        for tile in range(ring):
            pad_ref[part, tile, :PAD, :] = zeros
            pad_ref[part, tile, PAD + rows :, :] = zeros
            if tile == tiles:
                pad_ref[part, tile, inside, :] = edge_ref[base + part]
            elif part == 3:
                pad_ref[part, tile, inside, :] = wet_mask(land_ref, rank_ref, tile, rows)
            else:
                pad_ref[part, tile, inside, :] = kappa_ref[part, :, tile * LANES : (tile + 1) * LANES]
    lane = lax.broadcasted_iota(jnp.int32, (8, LANES), 1)
    is_first, is_last = lane == 0, lane == LANES - 1

    def east(values):
        rolled = [pltpu.roll(x, LANES - 1, axis=1) for x in values]
        return [jnp.where(is_last, rolled[(t + 1) % ring], rolled[t]) for t in range(ring)]

    def west(values):
        rolled = [pltpu.roll(x, 1, axis=1) for x in values]
        return [jnp.where(is_first, rolled[t - 1], rolled[t]) for t in range(ring)]

    def same(values):
        return values

    def each(f, *lists):
        return [f(*values) for values in zip(*lists, strict=True)]

    def block_rows(block, carry):
        start = pl.multiple_of(PAD + 8 * block, 8)
        row0 = pl.multiple_of(8 * block, 8)

        def load(part, shift):
            return [pad_ref[part, tile, pl.ds(start + shift, 8), :] for tile in range(ring)]

        kxx, kyy, kxy, wet = (load(part, 0) for part in range(4))
        kyy_n, kxy_n, wet_n = (load(part, 1) for part in (1, 2, 3))
        kyy_s, kxy_s, wet_s = (load(part, -1) for part in (1, 2, 3))
        x_gate = each(lambda w, e: w * e, wet, east(wet))
        y_gate = each(lambda w, n: w * n, wet, wet_n)
        s_gate = each(lambda w, n: w * n, wet_s, wet)
        ax = each(lambda k, e, g: 0.5 * (k + e) * g, kxx, east(kxx), x_gate)
        cx = each(lambda k, e, g: 0.125 * (k + e) * g, kxy, east(kxy), x_gate)
        ay = each(lambda k, n, g: 0.5 * (k + n) * g, kyy, kyy_n, y_gate)
        cy = each(lambda k, n, g: 0.125 * (k + n) * g, kxy, kxy_n, y_gate)
        ays = each(lambda k, n, g: 0.5 * (k + n) * g, kyy_s, kyy, s_gate)
        cys = each(lambda k, n, g: 0.125 * (k + n) * g, kxy_s, kxy, s_gate)
        axw, cxw = west(ax), west(cx)
        groups = (
            (same, each(lambda w, a, b, c, d: 1.0 - w * (a + b + c + d), wet, ax, axw, ay, ays)),
            (same, each(lambda w, a, b, c: w * (a + b - c), wet, ay, cx, cxw)),
            (same, each(lambda w, a, b, c: w * (a - b + c), wet, ays, cx, cxw)),
            (west, each(lambda w, a, b, c: w * (a + b - c), wet, ax, cy, cys)),
            (west, each(lambda w, a, b: w * (a + b), wet, cx, cy)),
            (west, each(lambda w, a, b: w * (-a - b), wet, cx, cys)),
            (east, each(lambda w, a, b, c: w * (a - b + c), wet, axw, cy, cys)),
            (east, each(lambda w, a, b: w * (-a - b), wet, cxw, cy)),
            (east, each(lambda w, a, b: w * (a + b), wet, cxw, cys)),
        )
        for number, (move, terms) in enumerate(groups):
            for tile, term in enumerate(move(terms)):
                weight_ref[number, tile, pl.ds(row0, 8), :] = term
        return carry

    lax.fori_loop(0, rows // 8, block_rows, 0)


def run_steps(planes, rows, tiles, rank_ref, weight_ref, u_ref, part_ref):
    lane = lax.broadcasted_iota(jnp.int32, (8, LANES), 1)
    is_first, is_last = lane == 0, lane == LANES - 1
    ring = tiles + 1
    part_ref[...] = jnp.zeros_like(part_ref)

    def on_wet(tile, work):
        if tile == tiles:
            work()
        else:
            pl.when(rank_ref[tile] >= 0)(work)

    def one_step(source, target):
        for tile in range(ring):

            def spread(tile=tile):
                for block in range(rows // 8):
                    base, row0 = PAD + 8 * block, 8 * block
                    weights = [weight_ref[k, tile, row0 : row0 + 8, :] for k in range(9)]
                    for plane in range(planes):
                        here = u_ref[source, plane, tile, base : base + 8, :]
                        up = u_ref[source, plane, tile, base + 1 : base + 9, :]
                        down = u_ref[source, plane, tile, base - 1 : base + 7, :]
                        centre, to_west, to_east = (
                            weights[3 * g] * here + weights[3 * g + 1] * up + weights[3 * g + 2] * down
                            for g in range(3)
                        )
                        u_ref[target, plane, tile, base : base + 8, :] = centre
                        part_ref[0, plane, tile, row0 : row0 + 8, :] = pltpu.roll(to_west, LANES - 1, axis=1)
                        part_ref[1, plane, tile, row0 : row0 + 8, :] = pltpu.roll(to_east, 1, axis=1)

            on_wet(tile, spread)
        for tile in range(ring):

            def collect(tile=tile):
                for block in range(rows // 8):
                    base, row0 = PAD + 8 * block, 8 * block
                    at = slice(row0, row0 + 8)
                    for plane in range(planes):
                        from_east = jnp.where(
                            is_last, part_ref[0, plane, (tile + 1) % ring, at, :], part_ref[0, plane, tile, at, :]
                        )
                        from_west = jnp.where(
                            is_first, part_ref[1, plane, (tile - 1) % ring, at, :], part_ref[1, plane, tile, at, :]
                        )
                        u_ref[target, plane, tile, base : base + 8, :] = (
                            u_ref[target, plane, tile, base : base + 8, :] + from_east + from_west
                        )

            on_wet(tile, collect)

    def two_steps(_, carry):
        one_step(0, 1)
        one_step(1, 0)
        return carry

    lax.fori_loop(0, STEPS // 2, two_steps, 0)


def step_scratch(planes, rows, tiles):
    return [
        pltpu.VMEM((2, planes, tiles + 1, rows + 2 * PAD, LANES), jnp.float32),
        pltpu.VMEM((2, planes, tiles + 1, rows, LANES), jnp.float32),
    ]


def clear_pads(planes, rows, tiles, u_ref):
    zeros = jnp.zeros((PAD, LANES), jnp.float32)
    for slot in range(2):
        for plane in range(planes):
            for tile in range(tiles + 1):
                u_ref[slot, plane, tile, :PAD, :] = zeros
                u_ref[slot, plane, tile, PAD + rows :, :] = zeros


def member_kernel(sizes, first, count, rank_ref, temp_ref, edge_ref, land_ref, weight_ref, stepped_ref, u_ref, part_ref):
    _, _, rows, tiles = sizes
    clear_pads(count, rows, tiles, u_ref)
    inside = slice(PAD, PAD + rows)
    for tile in range(tiles):
        wet = wet_mask(land_ref, rank_ref, tile, rows)
        for plane in range(count):
            u_ref[0, plane, tile, inside, :] = temp_ref[first + plane, :, tile * LANES : (tile + 1) * LANES] * wet
    for plane in range(count):
        u_ref[0, plane, tiles, inside, :] = edge_ref[first + plane]
    run_steps(count, rows, tiles, rank_ref, weight_ref, u_ref, part_ref)
    for plane in range(count):
        for tile in range(tiles):
            stepped_ref[plane, :, tile * LANES : (tile + 1) * LANES] = u_ref[0, plane, tile, inside, :]


def observe_planes(fields, cell, frac):
    rows, columns = fields[0].shape
    count = cell.shape[1]
    frac_east, frac_north = frac[0:1, :], frac[1:2, :]
    column, row = lax.rem(cell, columns), lax.rem(cell // columns, rows)
    at = lax.broadcasted_iota(jnp.int32, (columns, count), 0) - column
    pick = jnp.where(at == 0, 1.0 - frac_east, jnp.where(at == 1, frac_east, 0.0))
    values = jnp.concatenate(fields, axis=0)
    picked = jnp.dot(values, pick, precision=HIGHEST, preferred_element_type=jnp.float32)
    at = lax.broadcasted_iota(jnp.int32, (rows, count), 0) - row
    pick = jnp.where(at == 0, 1.0 - frac_north, jnp.where(at == 1, frac_north, 0.0))
    return [
        jnp.sum(picked[number * rows : (number + 1) * rows] * pick, axis=0, keepdims=True)
        for number in range(len(fields))
    ]


def observe_kernel(cell_ref, frac_ref, *refs):
    stepped_refs, seen_ref = refs[:-1], refs[-1]
    fields = [ref[plane] for ref in stepped_refs for plane in range(ref.shape[0])]
    halves = cell_ref.shape[1] // LANES
    for plane, seen in enumerate(observe_planes(fields, cell_ref[...], frac_ref[...])):
        for half in range(halves):
            at = plane * halves + half
            seen_ref[at : at + 1, :] = seen[:, half * LANES : (half + 1) * LANES]


def final_kernel(
    sizes, samples, ensemble, slots,
    rank_ref, mine_ref, other_ref, edge_ref, land_ref, weight_ref, cell_ref, frac_ref, seen_ref, stepped_refs,
    field_ref, anomaly_ref, variance_ref, u_ref, part_ref, mean_ref,
):
    members, fields, rows, tiles = sizes
    core, mine, other = chunk_number()
    owned = jnp.int32(0)
    for tile in range(tiles):
        owned = owned + (rank_ref[tile] >= 0).astype(jnp.int32)
    first_rank = jnp.clip(jnp.where(core == 0, owned, 0), 0, slots - 1)
    last_rank = jnp.clip(jnp.where(core == 0, slots - 1, slots - owned - 1), 0, slots - 1)
    clear_pads(fields, rows, tiles, u_ref)
    wet_edge = edge_ref[members * fields + 3]
    scale = 1.0 / samples

    def total(field, rank):
        own = mine_ref[jnp.bitwise_xor(mine, rank)]
        theirs = other_ref[jnp.bitwise_xor(other, rank)]
        return jnp.where(core == field, own, theirs) * scale

    inside = slice(PAD, PAD + rows)
    for tile in range(tiles):
        rank = rank_ref[tile]
        wet = wet_mask(land_ref, rank_ref, tile, rows)
        for field in range(fields):
            u_ref[0, field, tile, inside, :] = total(field, jnp.maximum(rank, 0)) * wet
    for field in range(fields):
        u_ref[0, field, tiles, inside, :] = (
            edge_block(total(field, first_rank), total(field, last_rank)) * wet_edge
        )
    run_steps(fields, rows, tiles, rank_ref, weight_ref, u_ref, part_ref)
    per_ref = field_ref.shape[0] // len(stepped_refs)
    for field in range(fields):
        for tile in range(tiles):
            lanes = slice(tile * LANES, (tile + 1) * LANES)
            mean = u_ref[0, field, tile, inside, :]
            mean_ref[field, :, lanes] = mean
            for member in range(members):
                plane = member * fields + field
                field_ref[plane, :, lanes] = stepped_refs[plane // per_ref][plane % per_ref, :, lanes] - mean
    mean_seen = observe_planes([mean_ref[field] for field in range(fields)], cell_ref[...], frac_ref[...])
    halves = cell_ref.shape[1] // LANES
    stride = members * fields * halves
    sets = seen_ref.shape[0] // stride

    def tree(values):
        while len(values) > 1:
            values = [a + b for a, b in zip(values[0::2], values[1::2], strict=True)]
        return values[0]

    for field in range(fields):
        for half in range(halves):
            lanes = slice(half * LANES, (half + 1) * LANES)
            mean = mean_seen[field][:, lanes]
            observed = []
            for part in range(sets):
                for member in range(members):
                    at = part * stride + (member * fields + field) * halves + half
                    observed.append(seen_ref[at : at + 1, :] - mean)
            centre = tree(observed) / ensemble
            anomaly = [value - centre for value in observed]
            variance_ref[field : field + 1, lanes] = tree([value * value for value in anomaly]) / ensemble
            for member in range(members):
                anomaly_ref[member, field : field + 1, lanes] = anomaly[member]


def local(temp_salt, diffusivity, wet_rank, land_rows, obs_cell, obs_frac):
    members, fields, levels, rows, columns = temp_salt.shape
    tiles = wet_rank.shape[0]
    cores, level_count, member_count = (lax.axis_size(axis) for axis in ALL_AXES)
    slots = tiles * cores // 2
    chips = level_count * member_count
    bits = chips.bit_length() - 1
    assert cores == 2 and fields == 2 and levels == 1 and slots == 4
    assert columns == tiles * LANES and chips == 1 << bits and bits >= 3
    count = obs_cell.shape[0]
    planes = members * fields
    sizes = (members, fields, rows, tiles)
    samples = members * levels * chips
    level_bit = bits - 1

    def device(core, chip):
        return core * chips + chip

    def exchange(value, masks):
        if masks is None:
            to = lambda core, chip: (1 - core, chip)
        else:
            to = lambda core, chip: (core, chip ^ masks[core])
        pairs = [(device(core, chip), device(*to(core, chip))) for core in range(2) for chip in range(chips)]
        return lax.ppermute(value, ALL_AXES, pairs)

    def struct(*shape):
        return jax.ShapeDtypeStruct(shape, jnp.float32)

    def call(kernel, out_shape, operands, scratch=(), cycles=1000):
        out_specs = jax.tree.map(lambda _: VMEM, out_shape)
        return pl.pallas_call(
            kernel,
            out_shape=out_shape,
            in_specs=[SMEM if x is wet_rank else VMEM for x in operands],
            out_specs=out_specs,
            scratch_shapes=list(scratch),
            compiler_params=PARAMS,
            cost_estimate=pl.CostEstimate(flops=cycles * 4096, bytes_accessed=1 << 20, transcendentals=0),
        )(*operands)

    temp = temp_salt.reshape(planes, rows, columns)
    land = land_rows.reshape(tiles, LANES)
    cell = obs_cell.reshape(1, count)
    masks = {1: (1, 2), 2: (2, 1), 3: (3, 3)}

    send, keep = call(
        functools.partial(sums_kernel, sizes),
        (struct(slots, rows, LANES), struct(slots, rows, LANES)), (wet_rank, temp, land),
    )
    arrived = exchange(send, None)
    edge = call(
        functools.partial(edges_kernel, sizes),
        struct(planes + 4, rows, LANES), (wet_rank, temp, diffusivity, land),
    )
    edges = exchange(edge, None)
    total = keep + arrived
    got = [exchange(total[k], masks[k]) for k in (1, 2, 3)]
    total = (total[0] + got[0]) + (got[1] + got[2])

    weights = call(
        functools.partial(weights_kernel, sizes),
        struct(9, tiles + 1, rows, LANES), (wet_rank, diffusivity, edges, land),
        [pltpu.VMEM((4, tiles + 1, rows + 2 * PAD, LANES), jnp.float32)],
    )
    per_call = 2
    stepped = [
        call(
            functools.partial(member_kernel, sizes, first, per_call),
            struct(per_call, rows, columns), (wet_rank, temp, edges, land, weights),
            step_scratch(per_call, rows, tiles), cycles=4000,
        )
        for first in range(0, planes, per_call)
    ]
    seen = call(
        observe_kernel,
        struct(planes * count // LANES, LANES), (cell, obs_frac, *stepped), cycles=2000,
    )

    for bit in [level_bit] + list(range(2, level_bit)):
        mask = (1 << bit, 1 << bit)
        if bit == level_bit:
            total = total + exchange(total, mask)
        else:
            got = exchange(jnp.concatenate([total, seen], axis=0), mask)
            total = total + got[:rows]
            seen = jnp.concatenate([seen, got[rows:]], axis=0)
    payload = jnp.concatenate([total, seen], axis=0)
    got = [payload] + [exchange(payload, masks[k]) for k in (1, 2, 3)]
    mine = jnp.stack([x[:rows] for x in got])
    theirs = exchange(mine, None)
    seen = jnp.concatenate([x[rows:] for x in got], axis=0)

    def last_kernel(*refs):
        fixed, rest = refs[:9], refs[9:]
        final_kernel(
            sizes, samples, members * member_count, slots, *fixed, rest[: len(stepped)], *rest[len(stepped) :]
        )

    field, anomaly, variance = call(
        last_kernel,
        (struct(planes, rows, columns), struct(members, fields, count), struct(fields, count)),
        (wet_rank, mine, theirs, edges, land, weights, cell, obs_frac, seen, *stepped),
        step_scratch(fields, rows, tiles) + [pltpu.VMEM((fields, rows, columns), jnp.float32)],
    )
    return field.reshape(members, fields, levels, rows, columns), anomaly, variance


def solution(mesh):
    placed = (
        P("member", None, "level", None, "tile"),
        P(None, None, "tile"),
        P("tile"),
        P("tile"),
        P(("tile", "level")),
        P(None, ("tile", "level")),
    )

    return jax.shard_map(
        local,
        mesh=mesh,
        in_specs=placed,
        out_specs=(
            P("member", None, "level", None, "tile"),
            P("member", None, ("tile", "level")),
            P(None, ("tile", "level")),
        ),
        check_vma=False,
    )
```

```python
import functools

import jax
import jax.numpy as jnp
from jax import lax
from jax.experimental import pallas as pl
from jax.experimental.pallas import tpu as pltpu
from jax.sharding import PartitionSpec as P


STEPS = 6
LANES = 128
PAD = 8
ALL_AXES = ("tile", "level", "member")
VMEM = pl.BlockSpec(memory_space=pltpu.VMEM)
SMEM = pl.BlockSpec(memory_space=pltpu.SMEM)
HBM = pl.BlockSpec(memory_space=pltpu.HBM)
HIGHEST = lax.Precision.HIGHEST
PARAMS = pltpu.CompilerParams(vmem_limit_bytes=20 << 20)


def chunk_number():
    member = lax.axis_index("member")
    core = lax.axis_index("tile")
    low = lax.rem(member, 2)
    high = lax.rem(member // 2, 2)
    mine = jnp.where(core == 0, 2 * high + low, 2 * low + high)
    other = jnp.where(core == 0, 2 * low + high, 2 * high + low)
    return core, mine, other


def wet_mask(land_ref, rank_ref, tile, rows):
    row = lax.broadcasted_iota(jnp.int32, (rows, LANES), 0)
    land = land_ref[pl.ds(tile, 1), :]
    dry = jnp.where(rank_ref[tile] >= 0, 0, rows)
    return (row >= jnp.maximum(land, dry)).astype(jnp.float32)


def slot_owner(rank_ref, slot, tiles):
    tile, owned = jnp.int32(0), jnp.int32(0)
    for t in range(tiles):
        here = (rank_ref[t] == slot).astype(jnp.int32)
        owned, tile = owned + here, tile + t * here
    return owned > 0, tile


def tile_lanes(tile):
    return pl.ds(pl.multiple_of(tile * LANES, LANES), LANES)


def signed_number(land_ref, rank_ref, core, tile, rows, tiles):
    number = (core * tiles + tile + 1).astype(jnp.float32)
    return (2.0 * wet_mask(land_ref, rank_ref, tile, rows) - 1.0) * number


def sums_kernel(sizes, rank_hbm, temp_hbm, land_hbm, send_ref, keep_ref, rank_ref, temp_ref, land_ref, sem):
    members, fields, rows, tiles, _ = sizes
    core, mine, other = chunk_number()
    copies = [
        pltpu.make_async_copy(rank_hbm, rank_ref, sem.at[0]),
        pltpu.make_async_copy(land_hbm, land_ref, sem.at[1]),
        pltpu.make_async_copy(temp_hbm, temp_ref, sem.at[2]),
    ]
    for copy in copies:
        copy.start()
    send_ref[...] = jnp.zeros_like(send_ref)
    keep_ref[...] = jnp.zeros_like(keep_ref)
    for copy in copies:
        copy.wait()
    for tile in range(tiles):
        lanes = slice(tile * LANES, (tile + 1) * LANES)

        @pl.when(rank_ref[tile] >= 0)
        def _():
            rank = rank_ref[tile]
            wet = wet_mask(land_ref, rank_ref, tile, rows)
            for ref, slot, field in ((send_ref, other, 1 - core), (keep_ref, mine, core)):
                total = temp_ref[field, :, lanes] * wet
                for member in range(1, members):
                    total = total + temp_ref[member * fields + field, :, lanes] * wet
                ref[jnp.bitwise_xor(slot, rank)] = total


def pack_kernel(sizes, rank_ref, temp_ref, kappa_ref, land_ref, pack_ref):
    _, fields, rows, tiles, _ = sizes
    core, _, _ = chunk_number()
    for tile in range(tiles):
        lanes = slice(tile * LANES, (tile + 1) * LANES)

        @pl.when(rank_ref[tile] >= 0)
        def _():
            rank = rank_ref[tile]
            wet = wet_mask(land_ref, rank_ref, tile, rows)
            for field in range(fields):
                pack_ref[field, rank] = temp_ref[(1 - core) * fields + field, :, lanes] * wet
            for part in range(3):
                pack_ref[fields + part, rank] = kappa_ref[part, :, lanes]
            pack_ref[fields + 3, rank] = signed_number(land_ref, rank_ref, core, tile, rows, tiles)


def weights_kernel(sizes, rank_ref, kappa_ref, land_ref, pack_ref, weight_ref, pad_ref):
    _, fields, rows, tiles, slots = sizes
    core, _, _ = chunk_number()
    band = float(2 * tiles)
    zeros = jnp.zeros((PAD, LANES), jnp.float32)
    inside = slice(PAD, PAD + rows)
    for slot in range(slots):
        owned, tile = slot_owner(rank_ref, slot, tiles)
        for part in range(4):
            pad_ref[part, slot, :PAD, :] = zeros
            pad_ref[part, slot, PAD + rows :, :] = zeros

        @pl.when(owned)
        def _():
            for part in range(3):
                pad_ref[part, slot, inside, :] = kappa_ref[part, :, tile_lanes(tile)]
            pad_ref[3, slot, inside, :] = signed_number(land_ref, rank_ref, core, tile, rows, tiles)

        @pl.when(jnp.logical_not(owned))
        def _():
            for part in range(4):
                pad_ref[part, slot, inside, :] = pack_ref[fields + part, slot]

    lane = lax.broadcasted_iota(jnp.int32, (8, LANES), 1)
    is_first, is_last = lane == 0, lane == LANES - 1
    numbers = [jnp.abs(pad_ref[3, slot, PAD : PAD + 8, :]) for slot in range(slots)]
    joined = []
    for slot in range(slots):
        here, following = numbers[slot], numbers[(slot + 1) % slots]
        expected = jnp.where(here == band, 1.0, here + 1.0)
        joined.append((following == expected).astype(jnp.float32))

    def east(values):
        rolled = [pltpu.roll(x, LANES - 1, axis=1) for x in values]
        return [
            jnp.where(is_last, joined[t] * rolled[(t + 1) % slots], rolled[t]) for t in range(slots)
        ]

    def west(values):
        rolled = [pltpu.roll(x, 1, axis=1) for x in values]
        return [jnp.where(is_first, joined[t - 1] * rolled[t - 1], rolled[t]) for t in range(slots)]

    def same(values):
        return values

    def each(f, *lists):
        return [f(*values) for values in zip(*lists, strict=True)]

    def load(part, start):
        values = [pad_ref[part, slot, start : start + 8, :] for slot in range(slots)]
        return [(x > 0.0).astype(jnp.float32) for x in values] if part == 3 else values

    for block in range(rows // 8):
        start = PAD + 8 * block
        kxx, kyy, kxy, wet = (load(part, start) for part in range(4))
        kyy_n, kxy_n, wet_n = (load(part, start + 1) for part in (1, 2, 3))
        kyy_s, kxy_s, wet_s = (load(part, start - 1) for part in (1, 2, 3))
        x_gate = each(lambda w, e: w * e, wet, east(wet))
        y_gate = each(lambda w, n: w * n, wet, wet_n)
        s_gate = each(lambda w, n: w * n, wet_s, wet)
        ax = each(lambda k, e, g: 0.5 * (k + e) * g, kxx, east(kxx), x_gate)
        cx = each(lambda k, e, g: 0.125 * (k + e) * g, kxy, east(kxy), x_gate)
        ay = each(lambda k, n, g: 0.5 * (k + n) * g, kyy, kyy_n, y_gate)
        cy = each(lambda k, n, g: 0.125 * (k + n) * g, kxy, kxy_n, y_gate)
        ays = each(lambda k, n, g: 0.5 * (k + n) * g, kyy_s, kyy, s_gate)
        cys = each(lambda k, n, g: 0.125 * (k + n) * g, kxy_s, kxy, s_gate)
        axw, cxw = west(ax), west(cx)
        groups = (
            (same, lambda: each(lambda w, a, b, c, d: 1.0 - w * (a + b + c + d), wet, ax, axw, ay, ays)),
            (same, lambda: each(lambda w, a, b, c: w * (a + b - c), wet, ay, cx, cxw)),
            (same, lambda: each(lambda w, a, b, c: w * (a - b + c), wet, ays, cx, cxw)),
            (west, lambda: each(lambda w, a, b, c: w * (a + b - c), wet, ax, cy, cys)),
            (west, lambda: each(lambda w, a, b: w * (a + b), wet, cx, cy)),
            (west, lambda: each(lambda w, a, b: w * (-a - b), wet, cx, cys)),
            (east, lambda: each(lambda w, a, b, c: w * (a - b + c), wet, axw, cy, cys)),
            (east, lambda: each(lambda w, a, b: w * (-a - b), wet, cxw, cy)),
            (east, lambda: each(lambda w, a, b: w * (a + b), wet, cxw, cys)),
        )
        for number, (move, terms) in enumerate(groups):
            for slot, term in enumerate(move(terms())):
                weight_ref[number, slot, 8 * block : 8 * block + 8, :] = term


def run_steps(planes, rows, slots, weight_ref, u_ref):
    lane = lax.broadcasted_iota(jnp.int32, (8, LANES), 1)
    is_first, is_last = lane == 0, lane == LANES - 1

    def one_step(source, target):
        for block in range(rows // 8):
            base, row0 = PAD + 8 * block, 8 * block
            parts = [[] for _ in range(planes)]
            for slot in range(slots):
                weights = [weight_ref[k, slot, row0 : row0 + 8, :] for k in range(9)]
                for plane in range(planes):
                    here = u_ref[source, plane, slot, base : base + 8, :]
                    up = u_ref[source, plane, slot, base + 1 : base + 9, :]
                    down = u_ref[source, plane, slot, base - 1 : base + 7, :]
                    centre, to_west, to_east = (
                        weights[3 * g] * here + weights[3 * g + 1] * up + weights[3 * g + 2] * down
                        for g in range(3)
                    )
                    parts[plane].append(
                        (centre, pltpu.roll(to_west, LANES - 1, axis=1), pltpu.roll(to_east, 1, axis=1))
                    )
            for plane in range(planes):
                for slot in range(slots):
                    centre, from_east, from_west = parts[plane][slot]
                    after = parts[plane][(slot + 1) % slots][1]
                    before = parts[plane][slot - 1][2]
                    u_ref[target, plane, slot, base : base + 8, :] = (
                        centre
                        + jnp.where(is_last, after, from_east)
                        + jnp.where(is_first, before, from_west)
                    )

    def two_steps(_, carry):
        one_step(0, 1)
        one_step(1, 0)
        return carry

    lax.fori_loop(0, STEPS // 2, two_steps, 0)


def clear_pads(planes, rows, slots, u_ref):
    zeros = jnp.zeros((PAD, LANES), jnp.float32)
    for half in range(2):
        for plane in range(planes):
            for slot in range(slots):
                u_ref[half, plane, slot, :PAD, :] = zeros
                u_ref[half, plane, slot, PAD + rows :, :] = zeros


def member_kernel(sizes, rank_ref, temp_ref, land_ref, pack_ref, weight_ref, stepped_ref, u_ref):
    _, fields, rows, tiles, slots = sizes
    core, _, _ = chunk_number()
    clear_pads(fields, rows, slots, u_ref)
    inside = slice(PAD, PAD + rows)
    for slot in range(slots):
        owned, tile = slot_owner(rank_ref, slot, tiles)

        @pl.when(owned)
        def _():
            wet = wet_mask(land_ref, rank_ref, tile, rows)
            for field in range(fields):
                u_ref[0, field, slot, inside, :] = temp_ref[core * fields + field, :, tile_lanes(tile)] * wet

        @pl.when(jnp.logical_not(owned))
        def _():
            for field in range(fields):
                u_ref[0, field, slot, inside, :] = pack_ref[field, slot]

    run_steps(fields, rows, slots, weight_ref, u_ref)
    for field in range(fields):
        for slot in range(slots):
            stepped_ref[field, slot] = u_ref[0, field, slot, inside, :]


def mean_kernel(sizes, samples, gathered_ref, weight_ref, stepped_ref, u_ref):
    _, _, rows, _, slots = sizes
    _, mine, _ = chunk_number()
    clear_pads(1, rows, slots, u_ref)
    inside = slice(PAD, PAD + rows)
    for slot in range(slots):
        u_ref[0, 0, slot, inside, :] = gathered_ref[jnp.bitwise_xor(mine, slot)] * (1.0 / samples)
    run_steps(1, rows, slots, weight_ref, u_ref)
    for slot in range(slots):
        stepped_ref[slot] = u_ref[0, 0, slot, inside, :]


def observe_planes(fields, cell, frac):
    rows, columns = fields[0].shape
    count = cell.shape[1]
    frac_east, frac_north = frac[0:1, :], frac[1:2, :]
    column, row = lax.rem(cell, columns), lax.rem(cell // columns, rows)
    at = lax.broadcasted_iota(jnp.int32, (columns, count), 0) - column
    pick = jnp.where(at == 0, 1.0 - frac_east, jnp.where(at == 1, frac_east, 0.0))
    values = jnp.concatenate(fields, axis=0)
    picked = jnp.dot(values, pick, precision=HIGHEST, preferred_element_type=jnp.float32)
    at = lax.broadcasted_iota(jnp.int32, (rows, count), 0) - row
    pick = jnp.where(at == 0, 1.0 - frac_north, jnp.where(at == 1, frac_north, 0.0))
    return [
        jnp.sum(picked[number * rows : (number + 1) * rows] * pick, axis=0, keepdims=True)
        for number in range(len(fields))
    ]


def observe_kernel(sizes, rank_ref, own_ref, other_ref, cell_ref, frac_ref, stepped_ref, seen_ref):
    members, fields, rows, tiles, _ = sizes
    core, _, _ = chunk_number()
    for tile in range(tiles):
        lanes = slice(tile * LANES, (tile + 1) * LANES)
        rank = rank_ref[tile]

        @pl.when(rank >= 0)
        def _():
            for field in range(fields):
                stepped_ref[core * fields + field, :, lanes] = own_ref[field, rank]
                stepped_ref[(1 - core) * fields + field, :, lanes] = other_ref[field, rank]

        @pl.when(rank < 0)
        def _():
            for plane in range(members * fields):
                stepped_ref[plane, :, lanes] = jnp.zeros((rows, LANES), jnp.float32)

    planes = [stepped_ref[plane] for plane in range(members * fields)]
    halves = cell_ref.shape[1] // LANES
    for plane, seen in enumerate(observe_planes(planes, cell_ref[...], frac_ref[...])):
        for half in range(halves):
            at = plane * halves + half
            seen_ref[at : at + 1, :] = seen[:, half * LANES : (half + 1) * LANES]


def final_kernel(
    sizes, ensemble, rank_ref, own_ref, other_ref, cell_ref, frac_ref, seen_ref, stepped_ref,
    field_hbm, anomaly_ref, variance_ref, field_ref, mean_ref, sem,
):
    members, fields, rows, tiles, _ = sizes
    core, _, _ = chunk_number()
    for tile in range(tiles):
        lanes = slice(tile * LANES, (tile + 1) * LANES)
        rank = rank_ref[tile]

        @pl.when(rank >= 0)
        def _():
            mean_ref[core, :, lanes] = own_ref[rank]
            mean_ref[1 - core, :, lanes] = other_ref[rank]

        @pl.when(rank < 0)
        def _():
            for field in range(fields):
                mean_ref[field, :, lanes] = jnp.zeros((rows, LANES), jnp.float32)

    for member in range(members):
        for field in range(fields):
            plane = member * fields + field
            field_ref[plane] = stepped_ref[plane] - mean_ref[field]
    copy = pltpu.make_async_copy(field_ref, field_hbm, sem)
    copy.start()
    mean_seen = observe_planes([mean_ref[field] for field in range(fields)], cell_ref[...], frac_ref[...])
    halves = cell_ref.shape[1] // LANES
    stride = members * fields * halves
    sets = seen_ref.shape[0] // stride

    def tree(values):
        while len(values) > 1:
            values = [a + b for a, b in zip(values[0::2], values[1::2], strict=True)]
        return values[0]

    for field in range(fields):
        for half in range(halves):
            lanes = slice(half * LANES, (half + 1) * LANES)
            mean = mean_seen[field][:, lanes]
            observed = []
            for part in range(sets):
                for member in range(members):
                    at = part * stride + (member * fields + field) * halves + half
                    observed.append(seen_ref[at : at + 1, :] - mean)
            centre = tree(observed) / ensemble
            anomaly = [value - centre for value in observed]
            variance_ref[field : field + 1, lanes] = tree([value * value for value in anomaly]) / ensemble
            for member in range(members):
                anomaly_ref[member, field : field + 1, lanes] = anomaly[member]
    copy.wait()


def local(temp_salt, diffusivity, wet_rank, land_rows, obs_cell, obs_frac):
    members, fields, levels, rows, columns = temp_salt.shape
    tiles = wet_rank.shape[0]
    cores, level_count, member_count = (lax.axis_size(axis) for axis in ALL_AXES)
    slots = tiles * cores // 2
    chips = level_count * member_count
    bits = chips.bit_length() - 1
    assert cores == 2 and fields == 2 and members == 2 and levels == 1 and slots == 4
    assert columns == tiles * LANES and chips == 1 << bits and bits >= 3
    count = obs_cell.shape[0]
    planes = members * fields
    sizes = (members, fields, rows, tiles, slots)
    samples = members * levels * chips
    level_bit = bits - 1

    def device(core, chip):
        return core * chips + chip

    def exchange(value, masks):
        if masks is None:
            to = lambda core, chip: (1 - core, chip)
        else:
            to = lambda core, chip: (core, chip ^ masks[core])
        pairs = [(device(core, chip), device(*to(core, chip))) for core in range(2) for chip in range(chips)]
        return lax.ppermute(value, ALL_AXES, pairs)

    def struct(*shape):
        return jax.ShapeDtypeStruct(shape, jnp.float32)

    def call(kernel, out_shape, operands, scratch=(), cycles=1000, in_specs=None, out_specs=None):
        return pl.pallas_call(
            functools.partial(kernel, sizes),
            out_shape=out_shape,
            in_specs=in_specs or [SMEM if x is wet_rank else VMEM for x in operands],
            out_specs=out_specs or jax.tree.map(lambda _: VMEM, out_shape),
            scratch_shapes=list(scratch),
            compiler_params=PARAMS,
            cost_estimate=pl.CostEstimate(flops=cycles * 4096, bytes_accessed=1 << 20, transcendentals=0),
        )(*operands)

    def halo(count):
        return pltpu.VMEM((2, count, slots, rows + 2 * PAD, LANES), jnp.float32)

    temp = temp_salt.reshape(planes, rows, columns)
    land = land_rows.reshape(tiles, LANES)
    cell = obs_cell.reshape(1, count)
    masks = {1: (1, 2), 2: (2, 1), 3: (3, 3)}

    send, keep = call(
        sums_kernel, (struct(slots, rows, LANES), struct(slots, rows, LANES)), (wet_rank, temp, land),
        scratch=[
            pltpu.SMEM((tiles,), jnp.int32),
            pltpu.VMEM((planes, rows, columns), jnp.float32),
            pltpu.VMEM((tiles, LANES), jnp.int32),
            pltpu.SemaphoreType.DMA((3,)),
        ],
        in_specs=[HBM] * 3,
    )
    arrived = exchange(send, None)
    pack = call(pack_kernel, struct(fields + 4, slots, rows, LANES), (wet_rank, temp, diffusivity, land))
    packed = exchange(pack, None)
    total = keep + arrived
    got = [exchange(total[k], masks[k]) for k in (1, 2, 3)]
    total = (total[0] + got[0]) + (got[1] + got[2])

    weights = call(
        weights_kernel, struct(9, slots, rows, LANES), (wet_rank, diffusivity, land, packed),
        [pltpu.VMEM((4, slots, rows + 2 * PAD, LANES), jnp.float32)],
    )
    own = call(
        member_kernel, struct(fields, slots, rows, LANES), (wet_rank, temp, land, packed, weights),
        [halo(fields)], cycles=4000,
    )
    other = exchange(own, None)
    stepped, seen = call(
        observe_kernel, (struct(planes, rows, columns), struct(planes * count // LANES, LANES)),
        (wet_rank, own, other, cell, obs_frac), cycles=2000,
    )

    for bit in [level_bit] + list(range(2, level_bit)):
        mask = (1 << bit, 1 << bit)
        if bit == level_bit:
            total = total + exchange(total, mask)
        else:
            got = exchange(jnp.concatenate([total, seen], axis=0), mask)
            total = total + got[:rows]
            seen = jnp.concatenate([seen, got[rows:]], axis=0)
    payload = jnp.concatenate([total, seen], axis=0)
    got = [payload] + [exchange(payload, masks[k]) for k in (1, 2, 3)]
    gathered = jnp.stack([x[:rows] for x in got])
    seen = jnp.concatenate([x[rows:] for x in got], axis=0)

    def step_mean(sizes, *refs):
        mean_kernel(sizes, samples, *refs)

    own_mean = call(step_mean, struct(slots, rows, LANES), (gathered, weights), [halo(1)], cycles=2000)
    other_mean = exchange(own_mean, None)

    def last_kernel(sizes, *refs):
        final_kernel(sizes, members * member_count, *refs)

    field, anomaly, variance = call(
        last_kernel,
        (struct(planes, rows, columns), struct(members, fields, count), struct(fields, count)),
        (wet_rank, own_mean, other_mean, cell, obs_frac, seen, stepped),
        [
            pltpu.VMEM((planes, rows, columns), jnp.float32),
            pltpu.VMEM((fields, rows, columns), jnp.float32),
            pltpu.SemaphoreType.DMA,
        ],
        out_specs=(HBM, VMEM, VMEM),
    )
    return field.reshape(members, fields, levels, rows, columns), anomaly, variance


def solution(mesh):
    placed = (
        P("member", None, "level", None, "tile"),
        P(None, None, "tile"),
        P("tile"),
        P("tile"),
        P(("tile", "level")),
        P(None, ("tile", "level")),
    )

    return jax.shard_map(
        local,
        mesh=mesh,
        in_specs=placed,
        out_specs=(
            P("member", None, "level", None, "tile"),
            P("member", None, ("tile", "level")),
            P(None, ("tile", "level")),
        ),
        check_vma=False,
    )
```

```python
import functools

import jax
import jax.numpy as jnp
from jax import lax
from jax.experimental import pallas as pl
from jax.experimental.pallas import tpu as pltpu
from jax.sharding import PartitionSpec as P


STEPS = 6
LANES = 128
PAD = 8
ALL_AXES = ("tile", "level", "member")
VMEM = pl.BlockSpec(memory_space=pltpu.VMEM)
SMEM = pl.BlockSpec(memory_space=pltpu.SMEM)
HBM = pl.BlockSpec(memory_space=pltpu.HBM)
HIGHEST = lax.Precision.HIGHEST
PARAMS = pltpu.CompilerParams(vmem_limit_bytes=20 << 20)


def chunk_number():
    member = lax.axis_index("member")
    core = lax.axis_index("tile")
    low = lax.rem(member, 2)
    high = lax.rem(member // 2, 2)
    mine = jnp.where(core == 0, 2 * high + low, 2 * low + high)
    other = jnp.where(core == 0, 2 * low + high, 2 * high + low)
    return core, mine, other


def wet_mask(land_ref, rank_ref, tile, rows):
    row = lax.broadcasted_iota(jnp.int32, (rows, LANES), 0)
    land = land_ref[pl.ds(tile, 1), :]
    dry = jnp.where(rank_ref[tile] >= 0, 0, rows)
    return (row >= jnp.maximum(land, dry)).astype(jnp.float32)


def slot_owner(rank_ref, slot, tiles):
    tile, owned = jnp.int32(0), jnp.int32(0)
    for t in range(tiles):
        here = (rank_ref[t] == slot).astype(jnp.int32)
        owned, tile = owned + here, tile + t * here
    return owned > 0, tile


def tile_lanes(tile):
    return pl.ds(pl.multiple_of(tile * LANES, LANES), LANES)


def signed_number(land_ref, rank_ref, core, tile, rows, tiles):
    number = (core * tiles + tile + 1).astype(jnp.float32)
    return (2.0 * wet_mask(land_ref, rank_ref, tile, rows) - 1.0) * number


def sums_kernel(
    sizes, rank_hbm, temp_hbm, kappa_hbm, land_hbm, send_ref, keep_ref, temp_ref, kappa_ref, land_ref, rank_ref, sem
):
    members, fields, rows, tiles, _ = sizes
    core, mine, other = chunk_number()
    pairs = ((rank_hbm, rank_ref), (land_hbm, land_ref), (temp_hbm, temp_ref), (kappa_hbm, kappa_ref))
    copies = [pltpu.make_async_copy(*pair, sem.at[number]) for number, pair in enumerate(pairs)]
    for copy in copies:
        copy.start()
    send_ref[...] = jnp.zeros_like(send_ref)
    keep_ref[...] = jnp.zeros_like(keep_ref)
    for copy in copies[:3]:
        copy.wait()
    for tile in range(tiles):
        lanes = slice(tile * LANES, (tile + 1) * LANES)

        @pl.when(rank_ref[tile] >= 0)
        def _():
            rank = rank_ref[tile]
            wet = wet_mask(land_ref, rank_ref, tile, rows)
            for ref, slot, field in ((send_ref, other, 1 - core), (keep_ref, mine, core)):
                total = temp_ref[field, :, lanes] * wet
                for member in range(1, members):
                    total = total + temp_ref[member * fields + field, :, lanes] * wet
                ref[jnp.bitwise_xor(slot, rank)] = total

    copies[3].wait()


def pack_kernel(sizes, rank_ref, temp_ref, kappa_ref, land_ref, pack_ref):
    _, fields, rows, tiles, _ = sizes
    core, _, _ = chunk_number()
    for tile in range(tiles):
        lanes = slice(tile * LANES, (tile + 1) * LANES)

        @pl.when(rank_ref[tile] >= 0)
        def _():
            rank = rank_ref[tile]
            wet = wet_mask(land_ref, rank_ref, tile, rows)
            for field in range(fields):
                pack_ref[field, rank] = temp_ref[(1 - core) * fields + field, :, lanes] * wet
            for part in range(3):
                pack_ref[fields + part, rank] = kappa_ref[part, :, lanes]
            pack_ref[fields + 3, rank] = signed_number(land_ref, rank_ref, core, tile, rows, tiles)


def weights_kernel(sizes, rank_ref, kappa_ref, land_ref, pack_ref, weight_ref, pad_ref, face_ref):
    _, fields, rows, tiles, slots = sizes
    core, _, _ = chunk_number()
    band = float(2 * tiles)
    zeros = jnp.zeros((PAD, LANES), jnp.float32)
    inside = slice(PAD, PAD + rows)
    for slot in range(slots):
        owned, tile = slot_owner(rank_ref, slot, tiles)
        for part in range(4):
            pad_ref[part, slot, :PAD, :] = zeros
            pad_ref[part, slot, PAD + rows :, :] = zeros

        @pl.when(owned)
        def _():
            for part in range(3):
                pad_ref[part, slot, inside, :] = kappa_ref[part, :, tile_lanes(tile)]
            pad_ref[3, slot, inside, :] = signed_number(land_ref, rank_ref, core, tile, rows, tiles)

        @pl.when(jnp.logical_not(owned))
        def _():
            for part in range(4):
                pad_ref[part, slot, inside, :] = pack_ref[fields + part, slot]

    lane = lax.broadcasted_iota(jnp.int32, (8, LANES), 1)
    is_first, is_last = lane == 0, lane == LANES - 1
    numbers = [jnp.abs(pad_ref[3, slot, PAD : PAD + 8, :]) for slot in range(slots)]
    joined = []
    for slot in range(slots):
        here, following = numbers[slot], numbers[(slot + 1) % slots]
        expected = jnp.where(here == band, 1.0, here + 1.0)
        joined.append((following == expected).astype(jnp.float32))

    def east(values):
        rolled = [pltpu.roll(x, LANES - 1, axis=1) for x in values]
        return [
            jnp.where(is_last, joined[t] * rolled[(t + 1) % slots], rolled[t]) for t in range(slots)
        ]

    def west(values):
        rolled = [pltpu.roll(x, 1, axis=1) for x in values]
        return [jnp.where(is_first, joined[t - 1] * rolled[t - 1], rolled[t]) for t in range(slots)]

    def each(f, *lists):
        return [f(*values) for values in zip(*lists, strict=True)]

    def load(ref, part, start):
        return [ref[part, slot, start : start + 8, :] for slot in range(slots)]

    def flags(start):
        return [(x > 0.0).astype(jnp.float32) for x in load(pad_ref, 3, start)]

    for part in range(4):
        for slot in range(slots):
            face_ref[part, slot, :PAD, :] = zeros
    for block in range(rows // 8):
        start = PAD + 8 * block
        kyy, kxy, wet = load(pad_ref, 1, start), load(pad_ref, 2, start), flags(start)
        kyy_n, kxy_n, wet_n = load(pad_ref, 1, start + 1), load(pad_ref, 2, start + 1), flags(start + 1)
        y_gate = each(lambda w, n: w * n, wet, wet_n)
        ay = each(lambda k, n, g: 0.5 * (k + n) * g, kyy, kyy_n, y_gate)
        cy = each(lambda k, n, g: 0.125 * (k + n) * g, kxy, kxy_n, y_gate)
        for part, values in enumerate((cy, west(cy), east(cy), ay)):
            for slot in range(slots):
                face_ref[part, slot, start : start + 8, :] = values[slot]
    for block in range(rows // 8):
        start = PAD + 8 * block
        kxx, kxy, wet = load(pad_ref, 0, start), load(pad_ref, 2, start), flags(start)
        wet_e, wet_w = east(wet), west(wet)
        x_gate = each(lambda w, e: w * e, wet, wet_e)
        ax = each(lambda k, e, g: 0.5 * (k + e) * g, kxx, east(kxx), x_gate)
        cx = each(lambda k, e, g: 0.125 * (k + e) * g, kxy, east(kxy), x_gate)
        axw, cxw = west(ax), west(cx)
        cy, cyw, cye, ay = (load(face_ref, part, start) for part in range(4))
        cysw, cyse, ays = (load(face_ref, part, start - 1) for part in (1, 2, 3))
        terms = (
            each(lambda w, a, b, c, d: 1.0 - w * (a + b + c + d), wet, ax, axw, ay, ays),
            each(lambda w, a, b, c: w * (a + b - c), wet, ay, cx, cxw),
            each(lambda w, a, b, c: w * (a - b + c), wet, ays, cx, cxw),
            each(lambda w, a, b, c: w * (a + b - c), wet_w, axw, cyw, cysw),
            each(lambda w, a, b: w * (a + b), wet_w, cxw, cyw),
            each(lambda w, a, b: w * (-a - b), wet_w, cxw, cysw),
            each(lambda w, a, b, c: w * (a - b + c), wet_e, ax, cye, cyse),
            each(lambda w, a, b: w * (-a - b), wet_e, cx, cye),
            each(lambda w, a, b: w * (a + b), wet_e, cx, cyse),
        )
        for number, values in enumerate(terms):
            for slot in range(slots):
                weight_ref[number, slot, 8 * block : 8 * block + 8, :] = values[slot]


def run_steps(planes, rows, slots, weight_ref, u_ref):
    lane = lax.broadcasted_iota(jnp.int32, (8, LANES), 1)
    is_first, is_last = lane == 0, lane == LANES - 1

    def one_step(source, target):
        for block in range(rows // 8):
            base, row0 = PAD + 8 * block, 8 * block
            parts = [[] for _ in range(planes)]
            for slot in range(slots):
                weights = [weight_ref[k, slot, row0 : row0 + 8, :] for k in range(9)]
                for plane in range(planes):
                    here = u_ref[source, plane, slot, base : base + 8, :]
                    up = u_ref[source, plane, slot, base + 1 : base + 9, :]
                    down = u_ref[source, plane, slot, base - 1 : base + 7, :]
                    centre, to_west, to_east = (
                        weights[3 * g] * here + weights[3 * g + 1] * up + weights[3 * g + 2] * down
                        for g in range(3)
                    )
                    parts[plane].append(
                        (centre, pltpu.roll(to_west, LANES - 1, axis=1), pltpu.roll(to_east, 1, axis=1))
                    )
            for plane in range(planes):
                for slot in range(slots):
                    centre, from_east, from_west = parts[plane][slot]
                    after = parts[plane][(slot + 1) % slots][1]
                    before = parts[plane][slot - 1][2]
                    u_ref[target, plane, slot, base : base + 8, :] = (
                        centre
                        + jnp.where(is_last, after, from_east)
                        + jnp.where(is_first, before, from_west)
                    )

    def two_steps(_, carry):
        one_step(0, 1)
        one_step(1, 0)
        return carry

    lax.fori_loop(0, STEPS // 2, two_steps, 0)


def clear_pads(planes, rows, slots, u_ref):
    zeros = jnp.zeros((PAD, LANES), jnp.float32)
    for half in range(2):
        for plane in range(planes):
            for slot in range(slots):
                u_ref[half, plane, slot, :PAD, :] = zeros
                u_ref[half, plane, slot, PAD + rows :, :] = zeros


def member_kernel(sizes, rank_ref, temp_ref, land_ref, pack_ref, weight_ref, stepped_ref, u_ref):
    _, fields, rows, tiles, slots = sizes
    core, _, _ = chunk_number()
    clear_pads(fields, rows, slots, u_ref)
    inside = slice(PAD, PAD + rows)
    for slot in range(slots):
        owned, tile = slot_owner(rank_ref, slot, tiles)

        @pl.when(owned)
        def _():
            wet = wet_mask(land_ref, rank_ref, tile, rows)
            for field in range(fields):
                u_ref[0, field, slot, inside, :] = temp_ref[core * fields + field, :, tile_lanes(tile)] * wet

        @pl.when(jnp.logical_not(owned))
        def _():
            for field in range(fields):
                u_ref[0, field, slot, inside, :] = pack_ref[field, slot]

    run_steps(fields, rows, slots, weight_ref, u_ref)
    for field in range(fields):
        for slot in range(slots):
            stepped_ref[field, slot] = u_ref[0, field, slot, inside, :]


def mean_kernel(sizes, samples, gathered_ref, weight_ref, stepped_ref, u_ref):
    _, _, rows, _, slots = sizes
    _, mine, _ = chunk_number()
    clear_pads(1, rows, slots, u_ref)
    inside = slice(PAD, PAD + rows)
    for slot in range(slots):
        u_ref[0, 0, slot, inside, :] = gathered_ref[jnp.bitwise_xor(mine, slot)] * (1.0 / samples)
    run_steps(1, rows, slots, weight_ref, u_ref)
    for slot in range(slots):
        stepped_ref[slot] = u_ref[0, 0, slot, inside, :]


def observe_planes(fields, cell, frac):
    rows, columns = fields[0].shape
    count = cell.shape[1]
    frac_east, frac_north = frac[0:1, :], frac[1:2, :]
    column, row = lax.rem(cell, columns), lax.rem(cell // columns, rows)
    at = lax.broadcasted_iota(jnp.int32, (columns, count), 0) - column
    pick = jnp.where(at == 0, 1.0 - frac_east, jnp.where(at == 1, frac_east, 0.0))
    values = jnp.concatenate(fields, axis=0)
    picked = jnp.dot(values, pick, precision=HIGHEST, preferred_element_type=jnp.float32)
    at = lax.broadcasted_iota(jnp.int32, (rows, count), 0) - row
    pick = jnp.where(at == 0, 1.0 - frac_north, jnp.where(at == 1, frac_north, 0.0))
    return [
        jnp.sum(picked[number * rows : (number + 1) * rows] * pick, axis=0, keepdims=True)
        for number in range(len(fields))
    ]


def observe_kernel(sizes, rank_ref, own_ref, other_ref, cell_ref, frac_ref, stepped_ref, seen_ref):
    members, fields, rows, tiles, _ = sizes
    core, _, _ = chunk_number()
    for tile in range(tiles):
        lanes = slice(tile * LANES, (tile + 1) * LANES)
        rank = rank_ref[tile]

        @pl.when(rank >= 0)
        def _():
            for field in range(fields):
                stepped_ref[core * fields + field, :, lanes] = own_ref[field, rank]
                stepped_ref[(1 - core) * fields + field, :, lanes] = other_ref[field, rank]

        @pl.when(rank < 0)
        def _():
            for plane in range(members * fields):
                stepped_ref[plane, :, lanes] = jnp.zeros((rows, LANES), jnp.float32)

    planes = [stepped_ref[plane] for plane in range(members * fields)]
    halves = cell_ref.shape[1] // LANES
    for plane, seen in enumerate(observe_planes(planes, cell_ref[...], frac_ref[...])):
        for half in range(halves):
            at = plane * halves + half
            seen_ref[at : at + 1, :] = seen[:, half * LANES : (half + 1) * LANES]


def final_kernel(
    sizes, ensemble, rank_ref, own_ref, other_ref, cell_ref, frac_ref, seen_ref, stepped_ref,
    field_hbm, anomaly_ref, variance_ref, field_ref, mean_ref, sem,
):
    members, fields, rows, tiles, _ = sizes
    core, _, _ = chunk_number()
    for tile in range(tiles):
        lanes = slice(tile * LANES, (tile + 1) * LANES)
        rank = rank_ref[tile]

        @pl.when(rank >= 0)
        def _():
            mean_ref[core, :, lanes] = own_ref[rank]
            mean_ref[1 - core, :, lanes] = other_ref[rank]

        @pl.when(rank < 0)
        def _():
            for field in range(fields):
                mean_ref[field, :, lanes] = jnp.zeros((rows, LANES), jnp.float32)

    for member in range(members):
        for field in range(fields):
            plane = member * fields + field
            field_ref[plane] = stepped_ref[plane] - mean_ref[field]
    copy = pltpu.make_async_copy(field_ref, field_hbm, sem)
    copy.start()
    mean_seen = observe_planes([mean_ref[field] for field in range(fields)], cell_ref[...], frac_ref[...])
    halves = cell_ref.shape[1] // LANES
    stride = members * fields * halves
    sets = seen_ref.shape[0] // stride

    def tree(values):
        while len(values) > 1:
            values = [a + b for a, b in zip(values[0::2], values[1::2], strict=True)]
        return values[0]

    for field in range(fields):
        for half in range(halves):
            lanes = slice(half * LANES, (half + 1) * LANES)
            mean = mean_seen[field][:, lanes]
            observed = []
            for part in range(sets):
                for member in range(members):
                    at = part * stride + (member * fields + field) * halves + half
                    observed.append(seen_ref[at : at + 1, :] - mean)
            centre = tree(observed) / ensemble
            anomaly = [value - centre for value in observed]
            variance_ref[field : field + 1, lanes] = tree([value * value for value in anomaly]) / ensemble
            for member in range(members):
                anomaly_ref[member, field : field + 1, lanes] = anomaly[member]
    copy.wait()


def local(temp_salt, diffusivity, wet_rank, land_rows, obs_cell, obs_frac):
    members, fields, levels, rows, columns = temp_salt.shape
    tiles = wet_rank.shape[0]
    cores, level_count, member_count = (lax.axis_size(axis) for axis in ALL_AXES)
    slots = tiles * cores // 2
    chips = level_count * member_count
    bits = chips.bit_length() - 1
    assert cores == 2 and fields == 2 and members == 2 and levels == 1 and slots == 4
    assert columns == tiles * LANES and chips == 1 << bits and bits >= 3
    count = obs_cell.shape[0]
    planes = members * fields
    sizes = (members, fields, rows, tiles, slots)
    samples = members * levels * chips
    level_bit = bits - 1

    def device(core, chip):
        return core * chips + chip

    def exchange(value, masks):
        if masks is None:
            to = lambda core, chip: (1 - core, chip)
        else:
            to = lambda core, chip: (core, chip ^ masks[core])
        pairs = [(device(core, chip), device(*to(core, chip))) for core in range(2) for chip in range(chips)]
        return lax.ppermute(value, ALL_AXES, pairs)

    def struct(*shape):
        return jax.ShapeDtypeStruct(shape, jnp.float32)

    def call(kernel, out_shape, operands, scratch=(), cycles=1000, in_specs=None, out_specs=None):
        return pl.pallas_call(
            functools.partial(kernel, sizes),
            out_shape=out_shape,
            in_specs=in_specs or [SMEM if x is wet_rank else VMEM for x in operands],
            out_specs=out_specs or jax.tree.map(lambda _: VMEM, out_shape),
            scratch_shapes=list(scratch),
            compiler_params=PARAMS,
            cost_estimate=pl.CostEstimate(flops=cycles * 4096, bytes_accessed=1 << 20, transcendentals=0),
        )(*operands)

    def halo(count):
        return pltpu.VMEM((2, count, slots, rows + 2 * PAD, LANES), jnp.float32)

    temp = temp_salt.reshape(planes, rows, columns)
    land = land_rows.reshape(tiles, LANES)
    cell = obs_cell.reshape(1, count)
    masks = {1: (1, 2), 2: (2, 1), 3: (3, 3)}

    inputs = tuple(pltpu.with_memory_space_constraint(x, pltpu.HBM) for x in (wet_rank, temp, diffusivity, land))
    send, keep, temp, kappa, land = call(
        sums_kernel,
        (
            struct(slots, rows, LANES),
            struct(slots, rows, LANES),
            struct(planes, rows, columns),
            struct(*diffusivity.shape),
            jax.ShapeDtypeStruct((tiles, LANES), jnp.int32),
        ),
        inputs,
        scratch=[pltpu.SMEM((tiles,), jnp.int32), pltpu.SemaphoreType.DMA((4,))],
        in_specs=[HBM] * 4,
    )
    arrived = exchange(send, None)
    pack = call(pack_kernel, struct(fields + 4, slots, rows, LANES), (wet_rank, temp, kappa, land))
    packed = exchange(pack, None)
    total = keep + arrived
    got = [exchange(total[k], masks[k]) for k in (1, 2, 3)]
    total = (total[0] + got[0]) + (got[1] + got[2])

    weights = call(
        weights_kernel, struct(9, slots, rows, LANES), (wet_rank, kappa, land, packed),
        [pltpu.VMEM((4, slots, rows + 2 * PAD, LANES), jnp.float32)] * 2,
    )
    own = call(
        member_kernel, struct(fields, slots, rows, LANES), (wet_rank, temp, land, packed, weights),
        [halo(fields)], cycles=4000,
    )
    other = exchange(own, None)
    stepped, seen = call(
        observe_kernel, (struct(planes, rows, columns), struct(planes * count // LANES, LANES)),
        (wet_rank, own, other, cell, obs_frac), cycles=2000,
    )

    for bit in [level_bit] + list(range(2, level_bit)):
        mask = (1 << bit, 1 << bit)
        if bit == level_bit:
            total = total + exchange(total, mask)
        else:
            got = exchange(jnp.concatenate([total, seen], axis=0), mask)
            total = total + got[:rows]
            seen = jnp.concatenate([seen, got[rows:]], axis=0)
    payload = jnp.concatenate([total, seen], axis=0)
    got = [payload] + [exchange(payload, masks[k]) for k in (1, 2, 3)]
    gathered = jnp.stack([x[:rows] for x in got])
    seen = jnp.concatenate([x[rows:] for x in got], axis=0)

    def step_mean(sizes, *refs):
        mean_kernel(sizes, samples, *refs)

    own_mean = call(step_mean, struct(slots, rows, LANES), (gathered, weights), [halo(1)], cycles=2000)
    other_mean = exchange(own_mean, None)

    def last_kernel(sizes, *refs):
        final_kernel(sizes, members * member_count, *refs)

    field, anomaly, variance = call(
        last_kernel,
        (struct(planes, rows, columns), struct(members, fields, count), struct(fields, count)),
        (wet_rank, own_mean, other_mean, cell, obs_frac, seen, stepped),
        [
            pltpu.VMEM((planes, rows, columns), jnp.float32),
            pltpu.VMEM((fields, rows, columns), jnp.float32),
            pltpu.SemaphoreType.DMA,
        ],
        out_specs=(HBM, VMEM, VMEM),
    )
    return field.reshape(members, fields, levels, rows, columns), anomaly, variance


def solution(mesh):
    placed = (
        P("member", None, "level", None, "tile"),
        P(None, None, "tile"),
        P("tile"),
        P("tile"),
        P(("tile", "level")),
        P(None, ("tile", "level")),
    )

    return jax.shard_map(
        local,
        mesh=mesh,
        in_specs=placed,
        out_specs=(
            P("member", None, "level", None, "tile"),
            P("member", None, ("tile", "level")),
            P(None, ("tile", "level")),
        ),
        check_vma=False,
    )
```

```python
import functools

import jax
import jax.numpy as jnp
from jax import lax
from jax.experimental import pallas as pl
from jax.experimental.pallas import tpu as pltpu
from jax.sharding import PartitionSpec as P


STEPS = 6
LANES = 128
PAD = 8
ALL_AXES = ("tile", "level", "member")
VMEM = pl.BlockSpec(memory_space=pltpu.VMEM)
SMEM = pl.BlockSpec(memory_space=pltpu.SMEM)
HBM = pl.BlockSpec(memory_space=pltpu.HBM)
HIGHEST = lax.Precision.HIGHEST
PARAMS = pltpu.CompilerParams(vmem_limit_bytes=20 << 20)


def chunk_number():
    member = lax.axis_index("member")
    core = lax.axis_index("tile")
    low = lax.rem(member, 2)
    high = lax.rem(member // 2, 2)
    mine = jnp.where(core == 0, 2 * high + low, 2 * low + high)
    other = jnp.where(core == 0, 2 * low + high, 2 * high + low)
    return core, mine, other


def wet_mask(land_ref, rank_ref, tile, rows):
    row = lax.broadcasted_iota(jnp.int32, (rows, LANES), 0)
    land = land_ref[pl.ds(tile, 1), :]
    dry = jnp.where(rank_ref[tile] >= 0, 0, rows)
    return (row >= jnp.maximum(land, dry)).astype(jnp.float32)


def slot_owner(rank_ref, slot, tiles):
    tile, owned = jnp.int32(0), jnp.int32(0)
    for t in range(tiles):
        here = (rank_ref[t] == slot).astype(jnp.int32)
        owned, tile = owned + here, tile + t * here
    return owned > 0, tile


def tile_lanes(tile):
    return pl.ds(pl.multiple_of(tile * LANES, LANES), LANES)


def signed_number(land_ref, rank_ref, core, tile, rows, tiles):
    number = (core * tiles + tile + 1).astype(jnp.float32)
    return (2.0 * wet_mask(land_ref, rank_ref, tile, rows) - 1.0) * number


def sums_kernel(
    sizes, rank_hbm, temp_hbm, kappa_hbm, land_hbm, send_ref, keep_ref, temp_ref, kappa_ref, land_ref, rank_ref, sem
):
    members, fields, rows, tiles, _ = sizes
    core, mine, other = chunk_number()
    pairs = ((rank_hbm, rank_ref), (land_hbm, land_ref), (temp_hbm, temp_ref), (kappa_hbm, kappa_ref))
    copies = [pltpu.make_async_copy(*pair, sem.at[number]) for number, pair in enumerate(pairs)]
    for copy in copies:
        copy.start()
    send_ref[...] = jnp.zeros_like(send_ref)
    keep_ref[...] = jnp.zeros_like(keep_ref)
    for copy in copies[:3]:
        copy.wait()
    for tile in range(tiles):
        lanes = slice(tile * LANES, (tile + 1) * LANES)

        @pl.when(rank_ref[tile] >= 0)
        def _():
            rank = rank_ref[tile]
            wet = wet_mask(land_ref, rank_ref, tile, rows)
            for ref, slot, field in ((send_ref, other, 1 - core), (keep_ref, mine, core)):
                total = temp_ref[field, :, lanes] * wet
                for member in range(1, members):
                    total = total + temp_ref[member * fields + field, :, lanes] * wet
                ref[jnp.bitwise_xor(slot, rank)] = total

    copies[3].wait()


def pack_kernel(sizes, rank_ref, temp_ref, kappa_ref, land_ref, pack_ref):
    _, fields, rows, tiles, _ = sizes
    core, _, _ = chunk_number()
    for tile in range(tiles):
        lanes = slice(tile * LANES, (tile + 1) * LANES)

        @pl.when(rank_ref[tile] >= 0)
        def _():
            rank = rank_ref[tile]
            wet = wet_mask(land_ref, rank_ref, tile, rows)
            for field in range(fields):
                pack_ref[field, rank] = temp_ref[(1 - core) * fields + field, :, lanes] * wet
            for part in range(3):
                pack_ref[fields + part, rank] = kappa_ref[part, :, lanes]
            pack_ref[fields + 3, rank] = signed_number(land_ref, rank_ref, core, tile, rows, tiles)


def weights_kernel(sizes, rank_ref, kappa_ref, land_ref, pack_ref, weight_ref, pad_ref, face_ref):
    _, fields, rows, tiles, slots = sizes
    core, _, _ = chunk_number()
    band = float(2 * tiles)
    zeros = jnp.zeros((PAD, LANES), jnp.float32)
    inside = slice(PAD, PAD + rows)
    for slot in range(slots):
        owned, tile = slot_owner(rank_ref, slot, tiles)
        for part in range(4):
            pad_ref[part, slot, :PAD, :] = zeros
            pad_ref[part, slot, PAD + rows :, :] = zeros

        @pl.when(owned)
        def _():
            for part in range(3):
                pad_ref[part, slot, inside, :] = kappa_ref[part, :, tile_lanes(tile)]
            pad_ref[3, slot, inside, :] = signed_number(land_ref, rank_ref, core, tile, rows, tiles)

        @pl.when(jnp.logical_not(owned))
        def _():
            for part in range(4):
                pad_ref[part, slot, inside, :] = pack_ref[fields + part, slot]

    lane = lax.broadcasted_iota(jnp.int32, (8, LANES), 1)
    is_first, is_last = lane == 0, lane == LANES - 1
    numbers = [jnp.abs(pad_ref[3, slot, PAD : PAD + 8, :]) for slot in range(slots)]
    joined = []
    for slot in range(slots):
        here, following = numbers[slot], numbers[(slot + 1) % slots]
        expected = jnp.where(here == band, 1.0, here + 1.0)
        joined.append((following == expected).astype(jnp.float32))

    def east(values):
        rolled = [pltpu.roll(x, LANES - 1, axis=1) for x in values]
        return [jnp.where(is_last, rolled[(t + 1) % slots], rolled[t]) for t in range(slots)]

    def west(values):
        rolled = [pltpu.roll(x, 1, axis=1) for x in values]
        return [jnp.where(is_first, rolled[t - 1], rolled[t]) for t in range(slots)]

    to_east = [jnp.where(is_last, joined[t], 1.0) for t in range(slots)]
    to_west = [jnp.where(is_first, joined[t - 1], 1.0) for t in range(slots)]

    def each(f, *lists):
        return [f(*values) for values in zip(*lists, strict=True)]

    def load(ref, part, start):
        return [ref[part, slot, start : start + 8, :] for slot in range(slots)]

    def flags(start):
        return [(x > 0.0).astype(jnp.float32) for x in load(pad_ref, 3, start)]

    for part in range(4):
        for slot in range(slots):
            face_ref[part, slot, :PAD, :] = zeros
    for block in range(rows // 8):
        start = PAD + 8 * block
        kyy, kxy, wet = load(pad_ref, 1, start), load(pad_ref, 2, start), flags(start)
        kyy_n, kxy_n, wet_n = load(pad_ref, 1, start + 1), load(pad_ref, 2, start + 1), flags(start + 1)
        y_gate = each(lambda w, n: w * n, wet, wet_n)
        ay = each(lambda k, n, g: 0.5 * (k + n) * g, kyy, kyy_n, y_gate)
        cy = each(lambda k, n, g: 0.125 * (k + n) * g, kxy, kxy_n, y_gate)
        for part, values in enumerate((cy, west(cy), east(cy), ay)):
            for slot in range(slots):
                face_ref[part, slot, start : start + 8, :] = values[slot]
    for block in range(rows // 8):
        start = PAD + 8 * block
        kxx, kxy, wet = load(pad_ref, 0, start), load(pad_ref, 2, start), flags(start)
        wet_e = each(lambda w, j: w * j, east(wet), to_east)
        wet_w = each(lambda w, j: w * j, west(wet), to_west)
        x_gate = each(lambda w, e: w * e, wet, wet_e)
        ax = each(lambda k, e, g: 0.5 * (k + e) * g, kxx, east(kxx), x_gate)
        cx = each(lambda k, e, g: 0.125 * (k + e) * g, kxy, east(kxy), x_gate)
        axw, cxw = west(ax), west(cx)
        cy, cyw, cye, ay = (load(face_ref, part, start) for part in range(4))
        cysw, cyse, ays = (load(face_ref, part, start - 1) for part in (1, 2, 3))
        terms = (
            each(lambda w, a, b, c, d: 1.0 - w * (a + b + c + d), wet, ax, axw, ay, ays),
            each(lambda w, a, b, c: w * (a + b - c), wet, ay, cx, cxw),
            each(lambda w, a, b, c: w * (a - b + c), wet, ays, cx, cxw),
            each(lambda w, a, b, c: w * (a + b - c), wet_w, axw, cyw, cysw),
            each(lambda w, a, b: w * (a + b), wet_w, cxw, cyw),
            each(lambda w, a, b: w * (-a - b), wet_w, cxw, cysw),
            each(lambda w, a, b, c: w * (a - b + c), wet_e, ax, cye, cyse),
            each(lambda w, a, b: w * (-a - b), wet_e, cx, cye),
            each(lambda w, a, b: w * (a + b), wet_e, cx, cyse),
        )
        for number, values in enumerate(terms):
            for slot in range(slots):
                weight_ref[number, slot, 8 * block : 8 * block + 8, :] = values[slot]


def run_steps(planes, rows, slots, weight_ref, u_ref):
    lane = lax.broadcasted_iota(jnp.int32, (8, LANES), 1)
    is_first, is_last = lane == 0, lane == LANES - 1

    def one_step(source, target):
        for block in range(rows // 8):
            base, row0 = PAD + 8 * block, 8 * block
            parts = [[] for _ in range(planes)]
            for slot in range(slots):
                weights = [weight_ref[k, slot, row0 : row0 + 8, :] for k in range(9)]
                for plane in range(planes):
                    here = u_ref[source, plane, slot, base : base + 8, :]
                    up = u_ref[source, plane, slot, base + 1 : base + 9, :]
                    down = u_ref[source, plane, slot, base - 1 : base + 7, :]
                    centre, to_west, to_east = (
                        weights[3 * g] * here + weights[3 * g + 1] * up + weights[3 * g + 2] * down
                        for g in range(3)
                    )
                    parts[plane].append(
                        (centre, pltpu.roll(to_west, LANES - 1, axis=1), pltpu.roll(to_east, 1, axis=1))
                    )
            for plane in range(planes):
                for slot in range(slots):
                    centre, from_east, from_west = parts[plane][slot]
                    after = parts[plane][(slot + 1) % slots][1]
                    before = parts[plane][slot - 1][2]
                    u_ref[target, plane, slot, base : base + 8, :] = (
                        centre
                        + jnp.where(is_last, after, from_east)
                        + jnp.where(is_first, before, from_west)
                    )

    def two_steps(_, carry):
        one_step(0, 1)
        one_step(1, 0)
        return carry

    lax.fori_loop(0, STEPS // 2, two_steps, 0)


def clear_pads(planes, rows, slots, u_ref):
    zeros = jnp.zeros((PAD, LANES), jnp.float32)
    for half in range(2):
        for plane in range(planes):
            for slot in range(slots):
                u_ref[half, plane, slot, :PAD, :] = zeros
                u_ref[half, plane, slot, PAD + rows :, :] = zeros


def member_kernel(sizes, rank_ref, temp_ref, land_ref, pack_ref, weight_ref, stepped_ref, u_ref):
    _, fields, rows, tiles, slots = sizes
    core, _, _ = chunk_number()
    clear_pads(fields, rows, slots, u_ref)
    inside = slice(PAD, PAD + rows)
    for slot in range(slots):
        owned, tile = slot_owner(rank_ref, slot, tiles)

        @pl.when(owned)
        def _():
            wet = wet_mask(land_ref, rank_ref, tile, rows)
            for field in range(fields):
                u_ref[0, field, slot, inside, :] = temp_ref[core * fields + field, :, tile_lanes(tile)] * wet

        @pl.when(jnp.logical_not(owned))
        def _():
            for field in range(fields):
                u_ref[0, field, slot, inside, :] = pack_ref[field, slot]

    run_steps(fields, rows, slots, weight_ref, u_ref)
    for field in range(fields):
        for slot in range(slots):
            stepped_ref[field, slot] = u_ref[0, field, slot, inside, :]


def mean_kernel(sizes, samples, gathered_ref, weight_ref, stepped_ref, u_ref):
    _, _, rows, _, slots = sizes
    _, mine, _ = chunk_number()
    clear_pads(1, rows, slots, u_ref)
    inside = slice(PAD, PAD + rows)
    for slot in range(slots):
        u_ref[0, 0, slot, inside, :] = gathered_ref[jnp.bitwise_xor(mine, slot)] * (1.0 / samples)
    run_steps(1, rows, slots, weight_ref, u_ref)
    for slot in range(slots):
        stepped_ref[slot] = u_ref[0, 0, slot, inside, :]


def observe_planes(fields, cell, frac):
    rows, columns = fields[0].shape
    count = cell.shape[1]
    frac_east, frac_north = frac[0:1, :], frac[1:2, :]
    column, row = lax.rem(cell, columns), lax.rem(cell // columns, rows)
    at = lax.broadcasted_iota(jnp.int32, (columns, count), 0) - column
    pick = jnp.where(at == 0, 1.0 - frac_east, jnp.where(at == 1, frac_east, 0.0))
    values = jnp.concatenate(fields, axis=0)
    picked = jnp.dot(values, pick, precision=HIGHEST, preferred_element_type=jnp.float32)
    at = lax.broadcasted_iota(jnp.int32, (rows, count), 0) - row
    pick = jnp.where(at == 0, 1.0 - frac_north, jnp.where(at == 1, frac_north, 0.0))
    return [
        jnp.sum(picked[number * rows : (number + 1) * rows] * pick, axis=0, keepdims=True)
        for number in range(len(fields))
    ]


def observe_kernel(sizes, rank_ref, own_ref, other_ref, cell_ref, frac_ref, stepped_ref, seen_ref):
    members, fields, rows, tiles, _ = sizes
    core, _, _ = chunk_number()
    for tile in range(tiles):
        lanes = slice(tile * LANES, (tile + 1) * LANES)
        rank = rank_ref[tile]

        @pl.when(rank >= 0)
        def _():
            for field in range(fields):
                stepped_ref[core * fields + field, :, lanes] = own_ref[field, rank]
                stepped_ref[(1 - core) * fields + field, :, lanes] = other_ref[field, rank]

        @pl.when(rank < 0)
        def _():
            for plane in range(members * fields):
                stepped_ref[plane, :, lanes] = jnp.zeros((rows, LANES), jnp.float32)

    planes = [stepped_ref[plane] for plane in range(members * fields)]
    halves = cell_ref.shape[1] // LANES
    for plane, seen in enumerate(observe_planes(planes, cell_ref[...], frac_ref[...])):
        for half in range(halves):
            at = plane * halves + half
            seen_ref[at : at + 1, :] = seen[:, half * LANES : (half + 1) * LANES]


def picks_kernel(sizes, cell_ref, frac_ref, column_ref, row_ref):
    _, _, rows, tiles, _ = sizes
    columns, count = tiles * LANES, cell_ref.shape[1]
    cell, frac = cell_ref[...], frac_ref[...]
    column, row = lax.rem(cell, columns), lax.rem(cell // columns, rows)
    at = lax.broadcasted_iota(jnp.int32, (columns, count), 0) - column
    pick = jnp.where(at == 0, 1.0 - frac[0:1, :], jnp.where(at == 1, frac[0:1, :], 0.0))
    for number, part in enumerate(split_parts(pick)):
        for place in ((0, 1, 2), (3, 4), (5,))[number]:
            column_ref[place * columns : (place + 1) * columns, :] = part
    at = lax.broadcasted_iota(jnp.int32, (rows, count), 0) - row
    row_ref[...] = jnp.where(at == 0, 1.0 - frac[1:2, :], jnp.where(at == 1, frac[1:2, :], 0.0))


def split_parts(values):
    high = values.astype(jnp.bfloat16)
    rest = values - high.astype(jnp.float32)
    middle = rest.astype(jnp.bfloat16)
    low = (rest - middle.astype(jnp.float32)).astype(jnp.bfloat16)
    return high, middle, low


def split_values(values):
    high, middle, low = split_parts(values)
    return jnp.concatenate([high, middle, low, high, middle, high], axis=1)


def own_field_kernel(sizes, rank_ref, mean_ref, stepped_ref, field_hbm, field_ref, sem):
    members, _, _, _, _ = sizes
    core, _, _ = chunk_number()
    write_planes(sizes, core, rank_ref, mean_ref, stepped_ref, field_hbm, field_ref, sem)
    for member in range(members):
        plane_copy(sizes, member, core, field_hbm, field_ref, sem).wait()


def plane_copy(sizes, member, field, field_hbm, field_ref, sem):
    _, fields, _, _, _ = sizes
    return pltpu.make_async_copy(field_ref.at[member], field_hbm.at[member * fields + field], sem.at[member])


def write_planes(sizes, field, rank_ref, mean_ref, stepped_ref, field_hbm, field_ref, sem):
    members, fields, _, tiles, _ = sizes
    for member in range(members):
        for tile in range(tiles):
            lanes = slice(tile * LANES, (tile + 1) * LANES)
            rank = rank_ref[tile]

            @pl.when(rank >= 0)
            def _():
                field_ref[member, :, lanes] = stepped_ref[member * fields + field, :, lanes] - mean_ref[rank]

            @pl.when(rank < 0)
            def _():
                field_ref[member, :, lanes] = stepped_ref[member * fields + field, :, lanes]

        plane_copy(sizes, member, field, field_hbm, field_ref, sem).start()


def final_kernel(
    sizes, ensemble, rank_ref, own_ref, other_ref, column_ref, row_ref, seen_ref, stepped_ref, started_hbm,
    field_hbm, anomaly_hbm, variance_hbm, field_ref, mean_ref, anomaly_ref, variance_ref, sem,
):
    members, fields, rows, tiles, _ = sizes
    core, _, _ = chunk_number()
    write_planes(sizes, 1 - core, rank_ref, other_ref, stepped_ref, field_hbm, field_ref, sem)
    for tile in range(tiles):
        lanes = slice(tile * LANES, (tile + 1) * LANES)
        rank = rank_ref[tile]

        @pl.when(rank >= 0)
        def _():
            mean_ref[core, :, lanes] = own_ref[rank]
            mean_ref[1 - core, :, lanes] = other_ref[rank]

        @pl.when(rank < 0)
        def _():
            for field in range(fields):
                mean_ref[field, :, lanes] = jnp.zeros((rows, LANES), jnp.float32)

    values = jnp.concatenate([split_values(mean_ref[field]) for field in range(fields)], axis=0)
    picked = jnp.dot(values, column_ref[...], preferred_element_type=jnp.float32)
    halves = row_ref.shape[1] // LANES
    stride = members * fields * halves
    sets = seen_ref.shape[0] // stride

    def tree(values):
        while len(values) > 1:
            values = [a + b for a, b in zip(values[0::2], values[1::2], strict=True)]
        return values[0]

    for field in range(fields):
        mean_seen = jnp.sum(picked[field * rows : (field + 1) * rows] * row_ref[...], axis=0, keepdims=True)
        for half in range(halves):
            lanes = slice(half * LANES, (half + 1) * LANES)
            mean = mean_seen[:, lanes]
            observed = []
            for part in range(sets):
                for member in range(members):
                    at = part * stride + (member * fields + field) * halves + half
                    observed.append(seen_ref[at : at + 1, :] - mean)
            centre = tree(observed) / ensemble
            anomaly = [value - centre for value in observed]
            variance_ref[field : field + 1, lanes] = tree([value * value for value in anomaly]) / ensemble
            for member in range(members):
                anomaly_ref[member, field : field + 1, lanes] = anomaly[member]
    small = (
        pltpu.make_async_copy(anomaly_ref, anomaly_hbm, sem.at[members]),
        pltpu.make_async_copy(variance_ref, variance_hbm, sem.at[members + 1]),
    )
    for copy in small:
        copy.start()
    for member in range(members):
        plane_copy(sizes, member, 1 - core, field_hbm, field_ref, sem).wait()
    for copy in small:
        copy.wait()


def local(temp_salt, diffusivity, wet_rank, land_rows, obs_cell, obs_frac):
    members, fields, levels, rows, columns = temp_salt.shape
    tiles = wet_rank.shape[0]
    cores, level_count, member_count = (lax.axis_size(axis) for axis in ALL_AXES)
    slots = tiles * cores // 2
    chips = level_count * member_count
    bits = chips.bit_length() - 1
    assert cores == 2 and fields == 2 and members == 2 and levels == 1 and slots == 4
    assert columns == tiles * LANES and chips == 1 << bits and bits >= 3
    count = obs_cell.shape[0]
    planes = members * fields
    sizes = (members, fields, rows, tiles, slots)
    samples = members * levels * chips
    level_bit = bits - 1

    def device(core, chip):
        return core * chips + chip

    def exchange(value, masks):
        if masks is None:
            to = lambda core, chip: (1 - core, chip)
        else:
            to = lambda core, chip: (core, chip ^ masks[core])
        pairs = [(device(core, chip), device(*to(core, chip))) for core in range(2) for chip in range(chips)]
        return lax.ppermute(value, ALL_AXES, pairs)

    def struct(*shape):
        return jax.ShapeDtypeStruct(shape, jnp.float32)

    def call(kernel, out_shape, operands, scratch=(), cycles=1000, in_specs=None, out_specs=None, aliases={}):
        return pl.pallas_call(
            functools.partial(kernel, sizes),
            out_shape=out_shape,
            in_specs=in_specs or [SMEM if x is wet_rank else VMEM for x in operands],
            out_specs=out_specs or jax.tree.map(lambda _: VMEM, out_shape),
            scratch_shapes=list(scratch),
            input_output_aliases=aliases,
            compiler_params=PARAMS,
            cost_estimate=pl.CostEstimate(flops=cycles * 4096, bytes_accessed=1 << 20, transcendentals=0),
        )(*operands)

    def halo(count):
        return pltpu.VMEM((2, count, slots, rows + 2 * PAD, LANES), jnp.float32)

    temp = temp_salt.reshape(planes, rows, columns)
    land = land_rows.reshape(tiles, LANES)
    cell = obs_cell.reshape(1, count)
    masks = {1: (1, 2), 2: (2, 1), 3: (3, 3)}

    inputs = tuple(pltpu.with_memory_space_constraint(x, pltpu.HBM) for x in (wet_rank, temp, diffusivity, land))
    send, keep, temp, kappa, land = call(
        sums_kernel,
        (
            struct(slots, rows, LANES),
            struct(slots, rows, LANES),
            struct(planes, rows, columns),
            struct(*diffusivity.shape),
            jax.ShapeDtypeStruct((tiles, LANES), jnp.int32),
        ),
        inputs,
        scratch=[pltpu.SMEM((tiles,), jnp.int32), pltpu.SemaphoreType.DMA((4,))],
        in_specs=[HBM] * 4,
    )
    arrived = exchange(send, None)
    pack = call(pack_kernel, struct(fields + 4, slots, rows, LANES), (wet_rank, temp, kappa, land))
    packed = exchange(pack, None)
    total = keep + arrived
    got = [exchange(total[k], masks[k]) for k in (1, 2, 3)]
    total = (total[0] + got[0]) + (got[1] + got[2])

    weights = call(
        weights_kernel, struct(9, slots, rows, LANES), (wet_rank, kappa, land, packed),
        [pltpu.VMEM((4, slots, rows + 2 * PAD, LANES), jnp.float32)] * 2,
    )
    own = call(
        member_kernel, struct(fields, slots, rows, LANES), (wet_rank, temp, land, packed, weights),
        [halo(fields)], cycles=4000,
    )
    other = exchange(own, None)
    stepped, seen = call(
        observe_kernel, (struct(planes, rows, columns), struct(planes * count // LANES, LANES)),
        (wet_rank, own, other, cell, obs_frac), cycles=2000,
    )

    for bit in [level_bit] + list(range(2, level_bit)):
        mask = (1 << bit, 1 << bit)
        if bit == level_bit:
            total = total + exchange(total, mask)
        else:
            got = exchange(jnp.concatenate([total, seen], axis=0), mask)
            total = total + got[:rows]
            seen = jnp.concatenate([seen, got[rows:]], axis=0)
    payload = jnp.concatenate([total, seen], axis=0)
    got = [payload] + [exchange(payload, masks[k]) for k in (1, 2, 3)]
    gathered = jnp.stack([x[:rows] for x in got])
    seen = jnp.concatenate([x[rows:] for x in got], axis=0)

    def step_mean(sizes, *refs):
        mean_kernel(sizes, samples, *refs)

    own_mean = call(step_mean, struct(slots, rows, LANES), (gathered, weights), [halo(1)], cycles=2000)
    other_mean = exchange(own_mean, None)
    column_picks, row_picks = call(
        picks_kernel,
        (jax.ShapeDtypeStruct((6 * columns, count), jnp.bfloat16), struct(rows, count)), (cell, obs_frac),
    )
    plane_scratch = pltpu.VMEM((members, rows, columns), jnp.float32)
    started = call(
        own_field_kernel, struct(planes, rows, columns), (wet_rank, own_mean, stepped),
        [plane_scratch, pltpu.SemaphoreType.DMA((members,))], out_specs=HBM,
    )

    def last_kernel(sizes, *refs):
        final_kernel(sizes, members * member_count, *refs)

    operands = (wet_rank, own_mean, other_mean, column_picks, row_picks, seen, stepped, started)
    field, anomaly, variance = call(
        last_kernel,
        (struct(planes, rows, columns), struct(members, fields, count), struct(fields, count)),
        operands,
        [
            plane_scratch,
            pltpu.VMEM((fields, rows, columns), jnp.float32),
            pltpu.VMEM((members, fields, count), jnp.float32),
            pltpu.VMEM((fields, count), jnp.float32),
            pltpu.SemaphoreType.DMA((members + 2,)),
        ],
        in_specs=[SMEM] + [VMEM] * 6 + [HBM],
        out_specs=(HBM, HBM, HBM),
        aliases={len(operands) - 1: 0},
    )
    return field.reshape(members, fields, levels, rows, columns), anomaly, variance


def solution(mesh):
    placed = (
        P("member", None, "level", None, "tile"),
        P(None, None, "tile"),
        P("tile"),
        P("tile"),
        P(("tile", "level")),
        P(None, ("tile", "level")),
    )

    return jax.shard_map(
        local,
        mesh=mesh,
        in_specs=placed,
        out_specs=(
            P("member", None, "level", None, "tile"),
            P("member", None, ("tile", "level")),
            P(None, ("tile", "level")),
        ),
        check_vma=False,
    )
```

```python
import functools

import jax
import jax.numpy as jnp
from jax import lax
from jax.experimental import pallas as pl
from jax.experimental.pallas import tpu as pltpu
from jax.sharding import PartitionSpec as P


STEPS = 6
LANES = 128
PAD = 8
ALL_AXES = ("tile", "level", "member")
VMEM = pl.BlockSpec(memory_space=pltpu.VMEM)
SMEM = pl.BlockSpec(memory_space=pltpu.SMEM)
HBM = pl.BlockSpec(memory_space=pltpu.HBM)
HIGHEST = lax.Precision.HIGHEST
PARAMS = pltpu.CompilerParams(vmem_limit_bytes=20 << 20)


def chunk_number():
    member = lax.axis_index("member")
    core = lax.axis_index("tile")
    low = lax.rem(member, 2)
    high = lax.rem(member // 2, 2)
    mine = jnp.where(core == 0, 2 * high + low, 2 * low + high)
    other = jnp.where(core == 0, 2 * low + high, 2 * high + low)
    return core, mine, other


def wet_mask(land_ref, rank_ref, tile, rows):
    row = lax.broadcasted_iota(jnp.int32, (rows, LANES), 0)
    land = land_ref[pl.ds(tile, 1), :]
    dry = jnp.where(rank_ref[tile] >= 0, 0, rows)
    return (row >= jnp.maximum(land, dry)).astype(jnp.float32)


def slot_owner(rank_ref, slot, tiles):
    tile, owned = jnp.int32(0), jnp.int32(0)
    for t in range(tiles):
        here = (rank_ref[t] == slot).astype(jnp.int32)
        owned, tile = owned + here, tile + t * here
    return owned > 0, tile


def tile_lanes(tile):
    return pl.ds(pl.multiple_of(tile * LANES, LANES), LANES)


def signed_number(land_ref, rank_ref, core, tile, rows, tiles):
    number = (core * tiles + tile + 1).astype(jnp.float32)
    return (2.0 * wet_mask(land_ref, rank_ref, tile, rows) - 1.0) * number


def sums_kernel(
    sizes, rank_hbm, temp_hbm, land_hbm, send_ref, keep_ref, temp_ref, land_ref, rank_out, rank_ref, sem
):
    members, fields, rows, tiles, _ = sizes
    core, mine, other = chunk_number()
    pairs = ((rank_hbm, rank_ref), (land_hbm, land_ref), (temp_hbm, temp_ref), (rank_hbm, rank_out))
    copies = [pltpu.make_async_copy(*pair, sem.at[number]) for number, pair in enumerate(pairs)]
    for copy in copies:
        copy.start()
    send_ref[...] = jnp.zeros_like(send_ref)
    keep_ref[...] = jnp.zeros_like(keep_ref)
    for copy in copies:
        copy.wait()
    for tile in range(tiles):
        lanes = slice(tile * LANES, (tile + 1) * LANES)

        @pl.when(rank_ref[tile] >= 0)
        def _():
            rank = rank_ref[tile]
            wet = wet_mask(land_ref, rank_ref, tile, rows)
            for ref, slot, field in ((send_ref, other, 1 - core), (keep_ref, mine, core)):
                total = temp_ref[field, :, lanes] * wet
                for member in range(1, members):
                    total = total + temp_ref[member * fields + field, :, lanes] * wet
                ref[jnp.bitwise_xor(slot, rank)] = total


def pack_kernel(sizes, rank_ref, temp_ref, kappa_ref, land_ref, pack_ref):
    _, fields, rows, tiles, _ = sizes
    core, _, _ = chunk_number()
    for tile in range(tiles):
        lanes = slice(tile * LANES, (tile + 1) * LANES)

        @pl.when(rank_ref[tile] >= 0)
        def _():
            rank = rank_ref[tile]
            wet = wet_mask(land_ref, rank_ref, tile, rows)
            for field in range(fields):
                pack_ref[field, rank] = temp_ref[(1 - core) * fields + field, :, lanes] * wet
            for part in range(3):
                pack_ref[fields + part, rank] = kappa_ref[part, :, lanes]
            pack_ref[fields + 3, rank] = signed_number(land_ref, rank_ref, core, tile, rows, tiles)


def weights_kernel(sizes, rank_ref, kappa_ref, land_ref, pack_ref, weight_ref, pad_ref, face_ref):
    _, fields, rows, tiles, slots = sizes
    core, _, _ = chunk_number()
    band = float(2 * tiles)
    zeros = jnp.zeros((PAD, LANES), jnp.float32)
    inside = slice(PAD, PAD + rows)
    for slot in range(slots):
        owned, tile = slot_owner(rank_ref, slot, tiles)
        for part in range(4):
            pad_ref[part, slot, :PAD, :] = zeros
            pad_ref[part, slot, PAD + rows :, :] = zeros

        @pl.when(owned)
        def _():
            for part in range(3):
                pad_ref[part, slot, inside, :] = kappa_ref[part, :, tile_lanes(tile)]
            pad_ref[3, slot, inside, :] = signed_number(land_ref, rank_ref, core, tile, rows, tiles)

        @pl.when(jnp.logical_not(owned))
        def _():
            for part in range(4):
                pad_ref[part, slot, inside, :] = pack_ref[fields + part, slot]

    lane = lax.broadcasted_iota(jnp.int32, (8, LANES), 1)
    is_first, is_last = lane == 0, lane == LANES - 1
    numbers = [jnp.abs(pad_ref[3, slot, PAD : PAD + 8, :]) for slot in range(slots)]
    joined = []
    for slot in range(slots):
        here, following = numbers[slot], numbers[(slot + 1) % slots]
        expected = jnp.where(here == band, 1.0, here + 1.0)
        joined.append((following == expected).astype(jnp.float32))

    def east(values):
        rolled = [pltpu.roll(x, LANES - 1, axis=1) for x in values]
        return [jnp.where(is_last, rolled[(t + 1) % slots], rolled[t]) for t in range(slots)]

    def west(values):
        rolled = [pltpu.roll(x, 1, axis=1) for x in values]
        return [jnp.where(is_first, rolled[t - 1], rolled[t]) for t in range(slots)]

    to_east = [jnp.where(is_last, joined[t], 1.0) for t in range(slots)]
    to_west = [jnp.where(is_first, joined[t - 1], 1.0) for t in range(slots)]

    def each(f, *lists):
        return [f(*values) for values in zip(*lists, strict=True)]

    def load(ref, part, start):
        return [ref[part, slot, start : start + 8, :] for slot in range(slots)]

    def flags(start):
        return [(x > 0.0).astype(jnp.float32) for x in load(pad_ref, 3, start)]

    for part in range(4):
        for slot in range(slots):
            face_ref[part, slot, :PAD, :] = zeros
    for block in range(rows // 8):
        start = PAD + 8 * block
        kyy, kxy, wet = load(pad_ref, 1, start), load(pad_ref, 2, start), flags(start)
        kyy_n, kxy_n, wet_n = load(pad_ref, 1, start + 1), load(pad_ref, 2, start + 1), flags(start + 1)
        y_gate = each(lambda w, n: w * n, wet, wet_n)
        ay = each(lambda k, n, g: 0.5 * (k + n) * g, kyy, kyy_n, y_gate)
        cy = each(lambda k, n, g: 0.125 * (k + n) * g, kxy, kxy_n, y_gate)
        for part, values in enumerate((cy, west(cy), east(cy), ay)):
            for slot in range(slots):
                face_ref[part, slot, start : start + 8, :] = values[slot]
    for block in range(rows // 8):
        start = PAD + 8 * block
        kxx, kxy, wet = load(pad_ref, 0, start), load(pad_ref, 2, start), flags(start)
        wet_e = each(lambda w, j: w * j, east(wet), to_east)
        wet_w = each(lambda w, j: w * j, west(wet), to_west)
        x_gate = each(lambda w, e: w * e, wet, wet_e)
        ax = each(lambda k, e, g: 0.5 * (k + e) * g, kxx, east(kxx), x_gate)
        cx = each(lambda k, e, g: 0.125 * (k + e) * g, kxy, east(kxy), x_gate)
        axw, cxw = west(ax), west(cx)
        cy, cyw, cye, ay = (load(face_ref, part, start) for part in range(4))
        cysw, cyse, ays = (load(face_ref, part, start - 1) for part in (1, 2, 3))
        terms = (
            each(lambda w, a, b, c, d: 1.0 - w * (a + b + c + d), wet, ax, axw, ay, ays),
            each(lambda w, a, b, c: w * (a + b - c), wet, ay, cx, cxw),
            each(lambda w, a, b, c: w * (a - b + c), wet, ays, cx, cxw),
            each(lambda w, a, b, c: w * (a + b - c), wet_w, axw, cyw, cysw),
            each(lambda w, a, b: w * (a + b), wet_w, cxw, cyw),
            each(lambda w, a, b: w * (-a - b), wet_w, cxw, cysw),
            each(lambda w, a, b, c: w * (a - b + c), wet_e, ax, cye, cyse),
            each(lambda w, a, b: w * (-a - b), wet_e, cx, cye),
            each(lambda w, a, b: w * (a + b), wet_e, cx, cyse),
        )
        for number, values in enumerate(terms):
            for slot in range(slots):
                weight_ref[number, slot, 8 * block : 8 * block + 8, :] = values[slot]


def run_steps(planes, rows, slots, weight_ref, u_ref):
    lane = lax.broadcasted_iota(jnp.int32, (8, LANES), 1)
    is_first, is_last = lane == 0, lane == LANES - 1

    def one_step(source, target):
        for block in range(rows // 8):
            base, row0 = PAD + 8 * block, 8 * block
            parts = [[] for _ in range(planes)]
            for slot in range(slots):
                weights = [weight_ref[k, slot, row0 : row0 + 8, :] for k in range(9)]
                for plane in range(planes):
                    here = u_ref[source, plane, slot, base : base + 8, :]
                    up = u_ref[source, plane, slot, base + 1 : base + 9, :]
                    down = u_ref[source, plane, slot, base - 1 : base + 7, :]
                    centre, to_west, to_east = (
                        weights[3 * g] * here + weights[3 * g + 1] * up + weights[3 * g + 2] * down
                        for g in range(3)
                    )
                    parts[plane].append(
                        (centre, pltpu.roll(to_west, LANES - 1, axis=1), pltpu.roll(to_east, 1, axis=1))
                    )
            for plane in range(planes):
                for slot in range(slots):
                    centre, from_east, from_west = parts[plane][slot]
                    after = parts[plane][(slot + 1) % slots][1]
                    before = parts[plane][slot - 1][2]
                    u_ref[target, plane, slot, base : base + 8, :] = (
                        centre
                        + jnp.where(is_last, after, from_east)
                        + jnp.where(is_first, before, from_west)
                    )

    def two_steps(_, carry):
        one_step(0, 1)
        one_step(1, 0)
        return carry

    lax.fori_loop(0, STEPS // 2, two_steps, 0)


def clear_pads(planes, rows, slots, u_ref):
    zeros = jnp.zeros((PAD, LANES), jnp.float32)
    for half in range(2):
        for plane in range(planes):
            for slot in range(slots):
                u_ref[half, plane, slot, :PAD, :] = zeros
                u_ref[half, plane, slot, PAD + rows :, :] = zeros


def member_kernel(sizes, rank_ref, temp_ref, land_ref, pack_ref, weight_ref, stepped_ref, u_ref):
    _, fields, rows, tiles, slots = sizes
    core, _, _ = chunk_number()
    clear_pads(fields, rows, slots, u_ref)
    inside = slice(PAD, PAD + rows)
    for slot in range(slots):
        owned, tile = slot_owner(rank_ref, slot, tiles)

        @pl.when(owned)
        def _():
            wet = wet_mask(land_ref, rank_ref, tile, rows)
            for field in range(fields):
                u_ref[0, field, slot, inside, :] = temp_ref[core * fields + field, :, tile_lanes(tile)] * wet

        @pl.when(jnp.logical_not(owned))
        def _():
            for field in range(fields):
                u_ref[0, field, slot, inside, :] = pack_ref[field, slot]

    run_steps(fields, rows, slots, weight_ref, u_ref)
    for field in range(fields):
        for slot in range(slots):
            stepped_ref[field, slot] = u_ref[0, field, slot, inside, :]


def mean_kernel(sizes, samples, gathered_ref, weight_ref, stepped_ref, u_ref):
    _, _, rows, _, slots = sizes
    _, mine, _ = chunk_number()
    clear_pads(1, rows, slots, u_ref)
    inside = slice(PAD, PAD + rows)
    for slot in range(slots):
        u_ref[0, 0, slot, inside, :] = gathered_ref[jnp.bitwise_xor(mine, slot)] * (1.0 / samples)
    run_steps(1, rows, slots, weight_ref, u_ref)
    for slot in range(slots):
        stepped_ref[slot] = u_ref[0, 0, slot, inside, :]


def observe_planes(fields, cell, frac):
    rows, columns = fields[0].shape
    count = cell.shape[1]
    frac_east, frac_north = frac[0:1, :], frac[1:2, :]
    column, row = lax.rem(cell, columns), lax.rem(cell // columns, rows)
    at = lax.broadcasted_iota(jnp.int32, (columns, count), 0) - column
    pick = jnp.where(at == 0, 1.0 - frac_east, jnp.where(at == 1, frac_east, 0.0))
    values = jnp.concatenate(fields, axis=0)
    picked = jnp.dot(values, pick, precision=HIGHEST, preferred_element_type=jnp.float32)
    at = lax.broadcasted_iota(jnp.int32, (rows, count), 0) - row
    pick = jnp.where(at == 0, 1.0 - frac_north, jnp.where(at == 1, frac_north, 0.0))
    return [
        jnp.sum(picked[number * rows : (number + 1) * rows] * pick, axis=0, keepdims=True)
        for number in range(len(fields))
    ]


def observe_kernel(sizes, rank_ref, own_ref, other_ref, cell_ref, frac_ref, stepped_ref, seen_ref):
    members, fields, rows, tiles, _ = sizes
    core, _, _ = chunk_number()
    for tile in range(tiles):
        lanes = slice(tile * LANES, (tile + 1) * LANES)
        rank = rank_ref[tile]

        @pl.when(rank >= 0)
        def _():
            for field in range(fields):
                stepped_ref[core * fields + field, :, lanes] = own_ref[field, rank]
                stepped_ref[(1 - core) * fields + field, :, lanes] = other_ref[field, rank]

        @pl.when(rank < 0)
        def _():
            for plane in range(members * fields):
                stepped_ref[plane, :, lanes] = jnp.zeros((rows, LANES), jnp.float32)

    planes = [stepped_ref[plane] for plane in range(members * fields)]
    halves = cell_ref.shape[1] // LANES
    for plane, seen in enumerate(observe_planes(planes, cell_ref[...], frac_ref[...])):
        for half in range(halves):
            at = plane * halves + half
            seen_ref[at : at + 1, :] = seen[:, half * LANES : (half + 1) * LANES]


def picks_kernel(sizes, cell_ref, frac_ref, column_ref, row_ref):
    _, _, rows, tiles, _ = sizes
    columns, count = tiles * LANES, cell_ref.shape[1]
    cell, frac = cell_ref[...], frac_ref[...]
    column, row = lax.rem(cell, columns), lax.rem(cell // columns, rows)
    at = lax.broadcasted_iota(jnp.int32, (columns, count), 0) - column
    pick = jnp.where(at == 0, 1.0 - frac[0:1, :], jnp.where(at == 1, frac[0:1, :], 0.0))
    for number, part in enumerate(split_parts(pick)):
        for place in ((0, 1, 2), (3, 4), (5,))[number]:
            column_ref[place * columns : (place + 1) * columns, :] = part
    at = lax.broadcasted_iota(jnp.int32, (rows, count), 0) - row
    row_ref[...] = jnp.where(at == 0, 1.0 - frac[1:2, :], jnp.where(at == 1, frac[1:2, :], 0.0))


def split_parts(values):
    high = values.astype(jnp.bfloat16)
    rest = values - high.astype(jnp.float32)
    middle = rest.astype(jnp.bfloat16)
    low = (rest - middle.astype(jnp.float32)).astype(jnp.bfloat16)
    return high, middle, low


def split_values(values):
    high, middle, low = split_parts(values)
    return jnp.concatenate([high, middle, low, high, middle, high], axis=1)


def observe_mean(sizes, rank_ref, mean_ref, column_ref, row_ref, whole_ref):
    _, _, _, tiles, _ = sizes
    for tile in range(tiles):
        lanes = slice(tile * LANES, (tile + 1) * LANES)
        rank = rank_ref[tile]
        wet = jnp.where(rank >= 0, 1.0, 0.0)
        whole_ref[:, lanes] = mean_ref[jnp.maximum(rank, 0)] * wet
    picked = jnp.dot(split_values(whole_ref[...]), column_ref[...], preferred_element_type=jnp.float32)
    return jnp.sum(picked * row_ref[...], axis=0, keepdims=True)


def own_field_kernel(
    sizes, rank_ref, mean_ref, stepped_ref, column_ref, row_ref, field_hbm, mean_seen_ref, field_ref, whole_ref, sem
):
    members, _, _, _, _ = sizes
    core, _, _ = chunk_number()
    write_planes(sizes, core, rank_ref, mean_ref, stepped_ref, field_hbm, field_ref, sem)
    mean_seen_ref[...] = observe_mean(sizes, rank_ref, mean_ref, column_ref, row_ref, whole_ref)
    for member in range(members):
        plane_copy(sizes, member, core, field_hbm, field_ref, sem).wait()


def plane_copy(sizes, member, field, field_hbm, field_ref, sem):
    _, fields, _, _, _ = sizes
    return pltpu.make_async_copy(field_ref.at[member], field_hbm.at[member * fields + field], sem.at[member])


def write_planes(sizes, field, rank_ref, mean_ref, stepped_ref, field_hbm, field_ref, sem):
    members, fields, _, tiles, _ = sizes
    for member in range(members):
        for tile in range(tiles):
            lanes = slice(tile * LANES, (tile + 1) * LANES)
            rank = rank_ref[tile]

            @pl.when(rank >= 0)
            def _():
                field_ref[member, :, lanes] = stepped_ref[member * fields + field, :, lanes] - mean_ref[rank]

            @pl.when(rank < 0)
            def _():
                field_ref[member, :, lanes] = stepped_ref[member * fields + field, :, lanes]

        plane_copy(sizes, member, field, field_hbm, field_ref, sem).start()


def final_kernel(
    sizes, ensemble, rank_ref, other_ref, column_ref, row_ref, own_seen_ref, seen_ref, stepped_ref, started_hbm,
    field_hbm, anomaly_hbm, variance_hbm, field_ref, whole_ref, anomaly_ref, variance_ref, sem,
):
    members, fields, _, _, _ = sizes
    core, _, _ = chunk_number()
    write_planes(sizes, 1 - core, rank_ref, other_ref, stepped_ref, field_hbm, field_ref, sem)
    own_seen = own_seen_ref[...]
    other_seen = observe_mean(sizes, rank_ref, other_ref, column_ref, row_ref, whole_ref)
    halves = row_ref.shape[1] // LANES
    stride = members * fields * halves
    sets = seen_ref.shape[0] // stride

    def tree(values):
        while len(values) > 1:
            values = [a + b for a, b in zip(values[0::2], values[1::2], strict=True)]
        return values[0]

    for field in range(fields):
        mean_seen = jnp.where(core == field, own_seen, other_seen)
        for half in range(halves):
            lanes = slice(half * LANES, (half + 1) * LANES)
            mean = mean_seen[:, lanes]
            observed = []
            for part in range(sets):
                for member in range(members):
                    at = part * stride + (member * fields + field) * halves + half
                    observed.append(seen_ref[at : at + 1, :] - mean)
            centre = tree(observed) / ensemble
            anomaly = [value - centre for value in observed]
            variance_ref[field : field + 1, lanes] = tree([value * value for value in anomaly]) / ensemble
            for member in range(members):
                anomaly_ref[member, field : field + 1, lanes] = anomaly[member]
    small = (
        pltpu.make_async_copy(anomaly_ref, anomaly_hbm, sem.at[members]),
        pltpu.make_async_copy(variance_ref, variance_hbm, sem.at[members + 1]),
    )
    for copy in small:
        copy.start()
    for member in range(members):
        plane_copy(sizes, member, 1 - core, field_hbm, field_ref, sem).wait()
    for copy in small:
        copy.wait()


def local(temp_salt, diffusivity, wet_rank, land_rows, obs_cell, obs_frac):
    members, fields, levels, rows, columns = temp_salt.shape
    tiles = wet_rank.shape[0]
    cores, level_count, member_count = (lax.axis_size(axis) for axis in ALL_AXES)
    slots = tiles * cores // 2
    chips = level_count * member_count
    bits = chips.bit_length() - 1
    assert cores == 2 and fields == 2 and members == 2 and levels == 1 and slots == 4
    assert columns == tiles * LANES and chips == 1 << bits and bits >= 3
    count = obs_cell.shape[0]
    planes = members * fields
    sizes = (members, fields, rows, tiles, slots)
    samples = members * levels * chips
    level_bit = bits - 1

    def device(core, chip):
        return core * chips + chip

    def exchange(value, masks):
        if masks is None:
            to = lambda core, chip: (1 - core, chip)
        else:
            to = lambda core, chip: (core, chip ^ masks[core])
        pairs = [(device(core, chip), device(*to(core, chip))) for core in range(2) for chip in range(chips)]
        return lax.ppermute(value, ALL_AXES, pairs)

    def struct(*shape):
        return jax.ShapeDtypeStruct(shape, jnp.float32)

    def call(kernel, out_shape, operands, scratch=(), cycles=1000, in_specs=None, out_specs=None, aliases={}):
        return pl.pallas_call(
            functools.partial(kernel, sizes),
            out_shape=out_shape,
            in_specs=in_specs or [SMEM if x.shape == wet_rank.shape else VMEM for x in operands],
            out_specs=out_specs or jax.tree.map(lambda _: VMEM, out_shape),
            scratch_shapes=list(scratch),
            input_output_aliases=aliases,
            compiler_params=PARAMS,
            cost_estimate=pl.CostEstimate(flops=cycles * 4096, bytes_accessed=1 << 20, transcendentals=0),
        )(*operands)

    def halo(count):
        return pltpu.VMEM((2, count, slots, rows + 2 * PAD, LANES), jnp.float32)

    temp = temp_salt.reshape(planes, rows, columns)
    land = land_rows.reshape(tiles, LANES)
    cell = obs_cell.reshape(1, count)
    masks = {1: (1, 2), 2: (2, 1), 3: (3, 3)}

    inputs = tuple(pltpu.with_memory_space_constraint(x, pltpu.HBM) for x in (wet_rank, temp, land))
    send, keep, temp, land, rank = call(
        sums_kernel,
        (
            struct(slots, rows, LANES),
            struct(slots, rows, LANES),
            struct(planes, rows, columns),
            jax.ShapeDtypeStruct((tiles, LANES), jnp.int32),
            jax.ShapeDtypeStruct((tiles,), jnp.int32),
        ),
        inputs,
        scratch=[pltpu.SMEM((tiles,), jnp.int32), pltpu.SemaphoreType.DMA((4,))],
        in_specs=[HBM] * 3,
    )
    arrived = exchange(send, None)
    pack = call(pack_kernel, struct(fields + 4, slots, rows, LANES), (rank, temp, diffusivity, land))
    packed = exchange(pack, None)
    total = keep + arrived
    got = [exchange(total[k], masks[k]) for k in (1, 2, 3)]
    total = (total[0] + got[0]) + (got[1] + got[2])

    weights = call(
        weights_kernel, struct(9, slots, rows, LANES), (rank, diffusivity, land, packed),
        [pltpu.VMEM((4, slots, rows + 2 * PAD, LANES), jnp.float32)] * 2,
    )
    own = call(
        member_kernel, struct(fields, slots, rows, LANES), (rank, temp, land, packed, weights),
        [halo(fields)], cycles=4000,
    )
    other = exchange(own, None)
    stepped, seen = call(
        observe_kernel, (struct(planes, rows, columns), struct(planes * count // LANES, LANES)),
        (rank, own, other, cell, obs_frac), cycles=2000,
    )

    for bit in [level_bit] + list(range(2, level_bit)):
        mask = (1 << bit, 1 << bit)
        if bit == level_bit:
            total = total + exchange(total, mask)
        else:
            got = exchange(jnp.concatenate([total, seen], axis=0), mask)
            total = total + got[:rows]
            seen = jnp.concatenate([seen, got[rows:]], axis=0)
    payload = jnp.concatenate([total, seen], axis=0)
    got = [payload] + [exchange(payload, masks[k]) for k in (1, 2, 3)]
    gathered = jnp.stack([x[:rows] for x in got])
    seen = jnp.concatenate([x[rows:] for x in got], axis=0)

    def step_mean(sizes, *refs):
        mean_kernel(sizes, samples, *refs)

    own_mean = call(step_mean, struct(slots, rows, LANES), (gathered, weights), [halo(1)], cycles=2000)
    other_mean = exchange(own_mean, None)
    column_picks, row_picks = call(
        picks_kernel,
        (jax.ShapeDtypeStruct((6 * columns, count), jnp.bfloat16), struct(rows, count)), (cell, obs_frac),
    )
    plane_scratch = pltpu.VMEM((members, rows, columns), jnp.float32)
    whole_scratch = pltpu.VMEM((rows, columns), jnp.float32)
    started, own_seen = call(
        own_field_kernel, (struct(planes, rows, columns), struct(1, count)),
        (rank, own_mean, stepped, column_picks, row_picks),
        [plane_scratch, whole_scratch, pltpu.SemaphoreType.DMA((members,))], out_specs=(HBM, VMEM),
    )

    def last_kernel(sizes, *refs):
        final_kernel(sizes, members * member_count, *refs)

    operands = (rank, other_mean, column_picks, row_picks, own_seen, seen, stepped, started)
    field, anomaly, variance = call(
        last_kernel,
        (struct(planes, rows, columns), struct(members, fields, count), struct(fields, count)),
        operands,
        [
            plane_scratch,
            whole_scratch,
            pltpu.VMEM((members, fields, count), jnp.float32),
            pltpu.VMEM((fields, count), jnp.float32),
            pltpu.SemaphoreType.DMA((members + 2,)),
        ],
        in_specs=[SMEM] + [VMEM] * 6 + [HBM],
        out_specs=(HBM, HBM, HBM),
        aliases={len(operands) - 1: 0},
    )
    return field.reshape(members, fields, levels, rows, columns), anomaly, variance


def solution(mesh):
    placed = (
        P("member", None, "level", None, "tile"),
        P(None, None, "tile"),
        P("tile"),
        P("tile"),
        P(("tile", "level")),
        P(None, ("tile", "level")),
    )

    return jax.shard_map(
        local,
        mesh=mesh,
        in_specs=placed,
        out_specs=(
            P("member", None, "level", None, "tile"),
            P("member", None, ("tile", "level")),
            P(None, ("tile", "level")),
        ),
        check_vma=False,
    )
```

```python
import functools

import jax
import jax.numpy as jnp
from jax import lax
from jax.experimental import pallas as pl
from jax.experimental.pallas import tpu as pltpu
from jax.sharding import PartitionSpec as P


STEPS = 6
LANES = 128
PAD = 8
ALL_AXES = ("tile", "level", "member")
VMEM = pl.BlockSpec(memory_space=pltpu.VMEM)
SMEM = pl.BlockSpec(memory_space=pltpu.SMEM)
HBM = pl.BlockSpec(memory_space=pltpu.HBM)
HIGHEST = lax.Precision.HIGHEST
PARAMS = pltpu.CompilerParams(vmem_limit_bytes=20 << 20)


def chunk_number():
    member = lax.axis_index("member")
    core = lax.axis_index("tile")
    low = lax.rem(member, 2)
    high = lax.rem(member // 2, 2)
    mine = jnp.where(core == 0, 2 * high + low, 2 * low + high)
    other = jnp.where(core == 0, 2 * low + high, 2 * high + low)
    return core, mine, other


def wet_mask(land_ref, rank_ref, tile, rows):
    row = lax.broadcasted_iota(jnp.int32, (rows, LANES), 0)
    land = land_ref[pl.ds(tile, 1), :]
    dry = jnp.where(rank_ref[tile] >= 0, 0, rows)
    return (row >= jnp.maximum(land, dry)).astype(jnp.float32)


def slot_owner(rank_ref, slot, tiles):
    tile, owned = jnp.int32(0), jnp.int32(0)
    for t in range(tiles):
        here = (rank_ref[t] == slot).astype(jnp.int32)
        owned, tile = owned + here, tile + t * here
    return owned > 0, tile


def tile_lanes(tile):
    return pl.ds(pl.multiple_of(tile * LANES, LANES), LANES)


def signed_number(land_ref, rank_ref, core, tile, rows, tiles):
    number = (core * tiles + tile + 1).astype(jnp.float32)
    return (2.0 * wet_mask(land_ref, rank_ref, tile, rows) - 1.0) * number


def sums_kernel(
    sizes, rank_hbm, temp_hbm, land_hbm, send_ref, keep_ref, temp_ref, land_ref, rank_out, rank_ref, sem
):
    members, fields, rows, tiles, _ = sizes
    core, mine, other = chunk_number()
    pairs = ((rank_hbm, rank_ref), (land_hbm, land_ref), (temp_hbm, temp_ref), (rank_hbm, rank_out))
    copies = [pltpu.make_async_copy(*pair, sem.at[number]) for number, pair in enumerate(pairs)]
    for copy in copies:
        copy.start()
    send_ref[...] = jnp.zeros_like(send_ref)
    keep_ref[...] = jnp.zeros_like(keep_ref)
    for copy in copies:
        copy.wait()
    for tile in range(tiles):
        lanes = slice(tile * LANES, (tile + 1) * LANES)

        @pl.when(rank_ref[tile] >= 0)
        def _():
            rank = rank_ref[tile]
            wet = wet_mask(land_ref, rank_ref, tile, rows)
            for ref, slot, field in ((send_ref, other, 1 - core), (keep_ref, mine, core)):
                total = temp_ref[field, :, lanes] * wet
                for member in range(1, members):
                    total = total + temp_ref[member * fields + field, :, lanes] * wet
                ref[jnp.bitwise_xor(slot, rank)] = total


def pack_kernel(sizes, rank_ref, temp_ref, kappa_ref, land_ref, pack_ref):
    _, fields, rows, tiles, _ = sizes
    core, _, _ = chunk_number()
    for tile in range(tiles):
        lanes = slice(tile * LANES, (tile + 1) * LANES)

        @pl.when(rank_ref[tile] >= 0)
        def _():
            rank = rank_ref[tile]
            wet = wet_mask(land_ref, rank_ref, tile, rows)
            for field in range(fields):
                pack_ref[field, rank] = temp_ref[(1 - core) * fields + field, :, lanes] * wet
            for part in range(3):
                pack_ref[fields + part, rank] = kappa_ref[part, :, lanes]
            pack_ref[fields + 3, rank] = signed_number(land_ref, rank_ref, core, tile, rows, tiles)


def weights_kernel(sizes, rank_ref, kappa_ref, land_ref, pack_ref, weight_ref, pad_ref, face_ref):
    _, fields, rows, tiles, slots = sizes
    core, _, _ = chunk_number()
    band = float(2 * tiles)
    zeros = jnp.zeros((PAD, LANES), jnp.float32)
    inside = slice(PAD, PAD + rows)
    for slot in range(slots):
        owned, tile = slot_owner(rank_ref, slot, tiles)
        for part in range(4):
            pad_ref[part, slot, :PAD, :] = zeros
            pad_ref[part, slot, PAD + rows :, :] = zeros

        @pl.when(owned)
        def _():
            for part in range(3):
                pad_ref[part, slot, inside, :] = kappa_ref[part, :, tile_lanes(tile)]
            pad_ref[3, slot, inside, :] = signed_number(land_ref, rank_ref, core, tile, rows, tiles)

        @pl.when(jnp.logical_not(owned))
        def _():
            for part in range(4):
                pad_ref[part, slot, inside, :] = pack_ref[fields + part, slot]

    lane = lax.broadcasted_iota(jnp.int32, (8, LANES), 1)
    is_first, is_last = lane == 0, lane == LANES - 1
    numbers = [jnp.abs(pad_ref[3, slot, PAD : PAD + 8, :]) for slot in range(slots)]
    joined = []
    for slot in range(slots):
        here, following = numbers[slot], numbers[(slot + 1) % slots]
        expected = jnp.where(here == band, 1.0, here + 1.0)
        joined.append((following == expected).astype(jnp.float32))

    def east(values):
        rolled = [pltpu.roll(x, LANES - 1, axis=1) for x in values]
        return [jnp.where(is_last, rolled[(t + 1) % slots], rolled[t]) for t in range(slots)]

    def west(values):
        rolled = [pltpu.roll(x, 1, axis=1) for x in values]
        return [jnp.where(is_first, rolled[t - 1], rolled[t]) for t in range(slots)]

    to_east = [jnp.where(is_last, joined[t], 1.0) for t in range(slots)]
    to_west = [jnp.where(is_first, joined[t - 1], 1.0) for t in range(slots)]

    def each(f, *lists):
        return [f(*values) for values in zip(*lists, strict=True)]

    def load(ref, part, start):
        return [ref[part, slot, start : start + 8, :] for slot in range(slots)]

    def flags(start):
        return [(x > 0.0).astype(jnp.float32) for x in load(pad_ref, 3, start)]

    for part in range(4):
        for slot in range(slots):
            face_ref[part, slot, :PAD, :] = zeros
    for block in range(rows // 8):
        start = PAD + 8 * block
        kyy, kxy, wet = load(pad_ref, 1, start), load(pad_ref, 2, start), flags(start)
        kyy_n, kxy_n, wet_n = load(pad_ref, 1, start + 1), load(pad_ref, 2, start + 1), flags(start + 1)
        y_gate = each(lambda w, n: w * n, wet, wet_n)
        ay = each(lambda k, n, g: 0.5 * (k + n) * g, kyy, kyy_n, y_gate)
        cy = each(lambda k, n, g: 0.125 * (k + n) * g, kxy, kxy_n, y_gate)
        for part, values in enumerate((cy, west(cy), east(cy), ay)):
            for slot in range(slots):
                face_ref[part, slot, start : start + 8, :] = values[slot]
    for block in range(rows // 8):
        start = PAD + 8 * block
        kxx, kxy, wet = load(pad_ref, 0, start), load(pad_ref, 2, start), flags(start)
        wet_e = each(lambda w, j: w * j, east(wet), to_east)
        wet_w = each(lambda w, j: w * j, west(wet), to_west)
        x_gate = each(lambda w, e: w * e, wet, wet_e)
        ax = each(lambda k, e, g: 0.5 * (k + e) * g, kxx, east(kxx), x_gate)
        cx = each(lambda k, e, g: 0.125 * (k + e) * g, kxy, east(kxy), x_gate)
        axw, cxw = west(ax), west(cx)
        cy, cyw, cye, ay = (load(face_ref, part, start) for part in range(4))
        cysw, cyse, ays = (load(face_ref, part, start - 1) for part in (1, 2, 3))
        terms = (
            each(lambda w, a, b, c, d: 1.0 - w * (a + b + c + d), wet, ax, axw, ay, ays),
            each(lambda w, a, b, c: w * (a + b - c), wet, ay, cx, cxw),
            each(lambda w, a, b, c: w * (a - b + c), wet, ays, cx, cxw),
            each(lambda w, a, b, c: w * (a + b - c), wet_w, axw, cyw, cysw),
            each(lambda w, a, b: w * (a + b), wet_w, cxw, cyw),
            each(lambda w, a, b: w * (-a - b), wet_w, cxw, cysw),
            each(lambda w, a, b, c: w * (a - b + c), wet_e, ax, cye, cyse),
            each(lambda w, a, b: w * (-a - b), wet_e, cx, cye),
            each(lambda w, a, b: w * (a + b), wet_e, cx, cyse),
        )
        for number, values in enumerate(terms):
            for slot in range(slots):
                weight_ref[number, slot, 8 * block : 8 * block + 8, :] = values[slot]


def run_steps(planes, rows, slots, weight_ref, u_ref):
    lane = lax.broadcasted_iota(jnp.int32, (8, LANES), 1)
    is_first, is_last = lane == 0, lane == LANES - 1

    def one_step(source, target):
        for block in range(rows // 8):
            base, row0 = PAD + 8 * block, 8 * block
            parts = [[] for _ in range(planes)]
            for slot in range(slots):
                weights = [weight_ref[k, slot, row0 : row0 + 8, :] for k in range(9)]
                for plane in range(planes):
                    here = u_ref[source, plane, slot, base : base + 8, :]
                    up = u_ref[source, plane, slot, base + 1 : base + 9, :]
                    down = u_ref[source, plane, slot, base - 1 : base + 7, :]
                    centre, to_west, to_east = (
                        weights[3 * g] * here + weights[3 * g + 1] * up + weights[3 * g + 2] * down
                        for g in range(3)
                    )
                    parts[plane].append(
                        (centre, pltpu.roll(to_west, LANES - 1, axis=1), pltpu.roll(to_east, 1, axis=1))
                    )
            for plane in range(planes):
                for slot in range(slots):
                    centre, from_east, from_west = parts[plane][slot]
                    after = parts[plane][(slot + 1) % slots][1]
                    before = parts[plane][slot - 1][2]
                    u_ref[target, plane, slot, base : base + 8, :] = (
                        centre
                        + jnp.where(is_last, after, from_east)
                        + jnp.where(is_first, before, from_west)
                    )

    def two_steps(_, carry):
        one_step(0, 1)
        one_step(1, 0)
        return carry

    lax.fori_loop(0, STEPS // 2, two_steps, 0)


def clear_pads(planes, rows, slots, u_ref):
    zeros = jnp.zeros((PAD, LANES), jnp.float32)
    for half in range(2):
        for plane in range(planes):
            for slot in range(slots):
                u_ref[half, plane, slot, :PAD, :] = zeros
                u_ref[half, plane, slot, PAD + rows :, :] = zeros


def member_kernel(sizes, rank_ref, temp_ref, land_ref, pack_ref, weight_ref, stepped_ref, u_ref):
    _, fields, rows, tiles, slots = sizes
    core, _, _ = chunk_number()
    clear_pads(fields, rows, slots, u_ref)
    inside = slice(PAD, PAD + rows)
    for slot in range(slots):
        owned, tile = slot_owner(rank_ref, slot, tiles)

        @pl.when(owned)
        def _():
            wet = wet_mask(land_ref, rank_ref, tile, rows)
            for field in range(fields):
                u_ref[0, field, slot, inside, :] = temp_ref[core * fields + field, :, tile_lanes(tile)] * wet

        @pl.when(jnp.logical_not(owned))
        def _():
            for field in range(fields):
                u_ref[0, field, slot, inside, :] = pack_ref[field, slot]

    run_steps(fields, rows, slots, weight_ref, u_ref)
    for field in range(fields):
        for slot in range(slots):
            stepped_ref[field, slot] = u_ref[0, field, slot, inside, :]


def mean_kernel(sizes, samples, gathered_ref, weight_ref, stepped_ref, u_ref):
    _, _, rows, _, slots = sizes
    _, mine, _ = chunk_number()
    clear_pads(1, rows, slots, u_ref)
    inside = slice(PAD, PAD + rows)
    for slot in range(slots):
        u_ref[0, 0, slot, inside, :] = gathered_ref[jnp.bitwise_xor(mine, slot)] * (1.0 / samples)
    run_steps(1, rows, slots, weight_ref, u_ref)
    for slot in range(slots):
        stepped_ref[slot] = u_ref[0, 0, slot, inside, :]


def observe_planes(fields, cell, frac):
    rows, columns = fields[0].shape
    count = cell.shape[1]
    frac_east, frac_north = frac[0:1, :], frac[1:2, :]
    column, row = lax.rem(cell, columns), lax.rem(cell // columns, rows)
    at = lax.broadcasted_iota(jnp.int32, (columns, count), 0) - column
    pick = jnp.where(at == 0, 1.0 - frac_east, jnp.where(at == 1, frac_east, 0.0))
    values = jnp.concatenate(fields, axis=0)
    picked = jnp.dot(values, pick, precision=HIGHEST, preferred_element_type=jnp.float32)
    at = lax.broadcasted_iota(jnp.int32, (rows, count), 0) - row
    pick = jnp.where(at == 0, 1.0 - frac_north, jnp.where(at == 1, frac_north, 0.0))
    return [
        jnp.sum(picked[number * rows : (number + 1) * rows] * pick, axis=0, keepdims=True)
        for number in range(len(fields))
    ]


def observe_kernel(sizes, rank_ref, own_ref, other_ref, cell_ref, frac_ref, stepped_ref, seen_ref):
    members, fields, rows, tiles, _ = sizes
    core, _, _ = chunk_number()
    for tile in range(tiles):
        lanes = slice(tile * LANES, (tile + 1) * LANES)
        rank = rank_ref[tile]

        @pl.when(rank >= 0)
        def _():
            for field in range(fields):
                stepped_ref[core * fields + field, :, lanes] = own_ref[field, rank]
                stepped_ref[(1 - core) * fields + field, :, lanes] = other_ref[field, rank]

        @pl.when(rank < 0)
        def _():
            for plane in range(members * fields):
                stepped_ref[plane, :, lanes] = jnp.zeros((rows, LANES), jnp.float32)

    planes = [stepped_ref[plane] for plane in range(members * fields)]
    halves = cell_ref.shape[1] // LANES
    for plane, seen in enumerate(observe_planes(planes, cell_ref[...], frac_ref[...])):
        for half in range(halves):
            at = plane * halves + half
            seen_ref[at : at + 1, :] = seen[:, half * LANES : (half + 1) * LANES]


def picks_kernel(sizes, cell_ref, frac_ref, column_ref, row_ref):
    _, _, rows, tiles, _ = sizes
    columns, count = tiles * LANES, cell_ref.shape[1]
    cell, frac = cell_ref[...], frac_ref[...]
    column, row = lax.rem(cell, columns), lax.rem(cell // columns, rows)
    at = lax.broadcasted_iota(jnp.int32, (columns, count), 0) - column
    pick = jnp.where(at == 0, 1.0 - frac[0:1, :], jnp.where(at == 1, frac[0:1, :], 0.0))
    for number, part in enumerate(split_parts(pick)):
        for place in ((0, 1, 2), (3, 4), (5,))[number]:
            column_ref[place * columns : (place + 1) * columns, :] = part
    at = lax.broadcasted_iota(jnp.int32, (rows, count), 0) - row
    row_ref[...] = jnp.where(at == 0, 1.0 - frac[1:2, :], jnp.where(at == 1, frac[1:2, :], 0.0))


def split_parts(values):
    high = values.astype(jnp.bfloat16)
    rest = values - high.astype(jnp.float32)
    middle = rest.astype(jnp.bfloat16)
    low = (rest - middle.astype(jnp.float32)).astype(jnp.bfloat16)
    return high, middle, low


def split_values(values):
    high, middle, low = split_parts(values)
    return jnp.concatenate([high, middle, low, high, middle, high], axis=1)


def observe_mean(sizes, rank_ref, mean_ref, column_ref, row_ref, whole_ref):
    _, _, _, tiles, _ = sizes
    for tile in range(tiles):
        lanes = slice(tile * LANES, (tile + 1) * LANES)
        rank = rank_ref[tile]
        wet = jnp.where(rank >= 0, 1.0, 0.0)
        whole_ref[:, lanes] = mean_ref[jnp.maximum(rank, 0)] * wet
    picked = jnp.dot(split_values(whole_ref[...]), column_ref[...], preferred_element_type=jnp.float32)
    return jnp.sum(picked * row_ref[...], axis=0, keepdims=True)


def own_field_kernel(
    sizes, rank_ref, mean_ref, stepped_ref, column_ref, row_ref, field_hbm, mean_seen_ref, field_ref, whole_ref, sem
):
    members, _, _, _, _ = sizes
    core, _, _ = chunk_number()
    write_planes(sizes, core, rank_ref, mean_ref, stepped_ref, field_hbm, field_ref, sem)
    mean_seen_ref[...] = observe_mean(sizes, rank_ref, mean_ref, column_ref, row_ref, whole_ref)
    for member in range(members):
        plane_copy(sizes, member, core, field_hbm, field_ref, sem).wait()


def plane_copy(sizes, member, field, field_hbm, field_ref, sem):
    _, fields, _, _, _ = sizes
    return pltpu.make_async_copy(field_ref.at[member], field_hbm.at[member * fields + field], sem.at[member])


def write_planes(sizes, field, rank_ref, mean_ref, stepped_ref, field_hbm, field_ref, sem):
    members, fields, _, tiles, _ = sizes
    for member in range(members):
        for tile in range(tiles):
            lanes = slice(tile * LANES, (tile + 1) * LANES)
            rank = rank_ref[tile]

            @pl.when(rank >= 0)
            def _():
                field_ref[member, :, lanes] = stepped_ref[member * fields + field, :, lanes] - mean_ref[rank]

            @pl.when(rank < 0)
            def _():
                field_ref[member, :, lanes] = stepped_ref[member * fields + field, :, lanes]

        plane_copy(sizes, member, field, field_hbm, field_ref, sem).start()


def final_kernel(
    sizes, ensemble, rank_ref, other_ref, column_ref, row_ref, own_seen_ref, seen_ref, stepped_ref, started_hbm,
    field_hbm, anomaly_hbm, variance_hbm, field_ref, whole_ref, anomaly_ref, variance_ref, sem,
):
    members, fields, _, _, _ = sizes
    core, _, _ = chunk_number()
    write_planes(sizes, 1 - core, rank_ref, other_ref, stepped_ref, field_hbm, field_ref, sem)
    own_seen = own_seen_ref[...]
    other_seen = observe_mean(sizes, rank_ref, other_ref, column_ref, row_ref, whole_ref)
    halves = row_ref.shape[1] // LANES
    stride = members * fields * halves
    sets = seen_ref.shape[0] // stride

    def tree(values):
        while len(values) > 1:
            values = [a + b for a, b in zip(values[0::2], values[1::2], strict=True)]
        return values[0]

    for field in range(fields):
        mean_seen = jnp.where(core == field, own_seen, other_seen)
        for half in range(halves):
            lanes = slice(half * LANES, (half + 1) * LANES)
            mean = mean_seen[:, lanes]
            observed = []
            for part in range(sets):
                for member in range(members):
                    at = part * stride + (member * fields + field) * halves + half
                    observed.append(seen_ref[at : at + 1, :] - mean)
            centre = tree(observed) / ensemble
            anomaly = [value - centre for value in observed]
            variance_ref[field : field + 1, lanes] = tree([value * value for value in anomaly]) / ensemble
            for member in range(members):
                anomaly_ref[member, field : field + 1, lanes] = anomaly[member]
    small = (
        pltpu.make_async_copy(anomaly_ref, anomaly_hbm, sem.at[members]),
        pltpu.make_async_copy(variance_ref, variance_hbm, sem.at[members + 1]),
    )
    for copy in small:
        copy.start()
    for member in range(members):
        plane_copy(sizes, member, 1 - core, field_hbm, field_ref, sem).wait()
    for copy in small:
        copy.wait()


def local(temp_salt, diffusivity, wet_rank, land_rows, obs_cell, obs_frac):
    members, fields, levels, rows, columns = temp_salt.shape
    tiles = wet_rank.shape[0]
    cores, level_count, member_count = (lax.axis_size(axis) for axis in ALL_AXES)
    slots = tiles * cores // 2
    chips = level_count * member_count
    bits = chips.bit_length() - 1
    assert cores == 2 and fields == 2 and members == 2 and levels == 1 and slots == 4
    assert columns == tiles * LANES and chips == 1 << bits and bits >= 3
    count = obs_cell.shape[0]
    planes = members * fields
    sizes = (members, fields, rows, tiles, slots)
    samples = members * levels * chips
    level_bit = bits - 1

    def device(core, chip):
        return core * chips + chip

    def exchange(value, masks):
        if masks is None:
            to = lambda core, chip: (1 - core, chip)
        else:
            to = lambda core, chip: (core, chip ^ masks[core])
        pairs = [(device(core, chip), device(*to(core, chip))) for core in range(2) for chip in range(chips)]
        return lax.ppermute(value, ALL_AXES, pairs)

    def struct(*shape):
        return jax.ShapeDtypeStruct(shape, jnp.float32)

    def call(kernel, out_shape, operands, scratch=(), cycles=1000, in_specs=None, out_specs=None, aliases={}):
        return pl.pallas_call(
            functools.partial(kernel, sizes),
            out_shape=out_shape,
            in_specs=in_specs or [SMEM if x.shape == wet_rank.shape else VMEM for x in operands],
            out_specs=out_specs or jax.tree.map(lambda _: VMEM, out_shape),
            scratch_shapes=list(scratch),
            input_output_aliases=aliases,
            compiler_params=PARAMS,
            cost_estimate=pl.CostEstimate(flops=cycles * 4096, bytes_accessed=1 << 20, transcendentals=0),
        )(*operands)

    def halo(count):
        return pltpu.VMEM((2, count, slots, rows + 2 * PAD, LANES), jnp.float32)

    temp = temp_salt.reshape(planes, rows, columns)
    land = land_rows.reshape(tiles, LANES)
    cell = obs_cell.reshape(1, count)
    masks = {1: (1, 2), 2: (2, 1), 3: (3, 3)}

    inputs = tuple(pltpu.with_memory_space_constraint(x, pltpu.HBM) for x in (wet_rank, temp, land))
    send, keep, temp, land, rank = call(
        sums_kernel,
        (
            struct(slots, rows, LANES),
            struct(slots, rows, LANES),
            struct(planes, rows, columns),
            jax.ShapeDtypeStruct((tiles, LANES), jnp.int32),
            jax.ShapeDtypeStruct((tiles,), jnp.int32),
        ),
        inputs,
        scratch=[pltpu.SMEM((tiles,), jnp.int32), pltpu.SemaphoreType.DMA((4,))],
        in_specs=[HBM] * 3,
    )
    arrived = exchange(send, None)
    pack = call(pack_kernel, struct(fields + 4, slots, rows, LANES), (rank, temp, diffusivity, land))
    packed = exchange(pack, None)
    total = keep + arrived
    got = [exchange(total[k], masks[k]) for k in (1, 2, 3)]
    total = (total[0] + got[0]) + (got[1] + got[2])

    weights = call(
        weights_kernel, struct(9, slots, rows, LANES), (rank, diffusivity, land, packed),
        [pltpu.VMEM((4, slots, rows + 2 * PAD, LANES), jnp.float32)] * 2,
    )
    own = call(
        member_kernel, struct(fields, slots, rows, LANES), (rank, temp, land, packed, weights),
        [halo(fields)], cycles=4000,
    )
    other = exchange(own, None)
    stepped, seen = call(
        observe_kernel, (struct(planes, rows, columns), struct(planes * count // LANES, LANES)),
        (rank, own, other, cell, obs_frac), cycles=2000,
    )

    level, member = 1 << level_bit, 1 << 2
    total = total + exchange(total, (member, level))
    total = total + exchange(total, (level, member))
    seen = jnp.concatenate([seen, exchange(seen, (member, member))], axis=0)
    for bit in range(3, level_bit):
        got = exchange(jnp.concatenate([total, seen], axis=0), (1 << bit, 1 << bit))
        total = total + got[:rows]
        seen = jnp.concatenate([seen, got[rows:]], axis=0)
    payload = jnp.concatenate([total, seen], axis=0)
    got = [payload] + [exchange(payload, masks[k]) for k in (1, 2, 3)]
    gathered = jnp.stack([x[:rows] for x in got])
    seen = jnp.concatenate([x[rows:] for x in got], axis=0)

    def step_mean(sizes, *refs):
        mean_kernel(sizes, samples, *refs)

    own_mean = call(step_mean, struct(slots, rows, LANES), (gathered, weights), [halo(1)], cycles=2000)
    other_mean = exchange(own_mean, None)
    column_picks, row_picks = call(
        picks_kernel,
        (jax.ShapeDtypeStruct((6 * columns, count), jnp.bfloat16), struct(rows, count)), (cell, obs_frac),
    )
    plane_scratch = pltpu.VMEM((members, rows, columns), jnp.float32)
    whole_scratch = pltpu.VMEM((rows, columns), jnp.float32)
    started, own_seen = call(
        own_field_kernel, (struct(planes, rows, columns), struct(1, count)),
        (rank, own_mean, stepped, column_picks, row_picks),
        [plane_scratch, whole_scratch, pltpu.SemaphoreType.DMA((members,))], out_specs=(HBM, VMEM),
    )

    def last_kernel(sizes, *refs):
        final_kernel(sizes, members * member_count, *refs)

    operands = (rank, other_mean, column_picks, row_picks, own_seen, seen, stepped, started)
    field, anomaly, variance = call(
        last_kernel,
        (struct(planes, rows, columns), struct(members, fields, count), struct(fields, count)),
        operands,
        [
            plane_scratch,
            whole_scratch,
            pltpu.VMEM((members, fields, count), jnp.float32),
            pltpu.VMEM((fields, count), jnp.float32),
            pltpu.SemaphoreType.DMA((members + 2,)),
        ],
        in_specs=[SMEM] + [VMEM] * 6 + [HBM],
        out_specs=(HBM, HBM, HBM),
        aliases={len(operands) - 1: 0},
    )
    return field.reshape(members, fields, levels, rows, columns), anomaly, variance


def solution(mesh):
    placed = (
        P("member", None, "level", None, "tile"),
        P(None, None, "tile"),
        P("tile"),
        P("tile"),
        P(("tile", "level")),
        P(None, ("tile", "level")),
    )

    return jax.shard_map(
        local,
        mesh=mesh,
        in_specs=placed,
        out_specs=(
            P("member", None, "level", None, "tile"),
            P("member", None, ("tile", "level")),
            P(None, ("tile", "level")),
        ),
        check_vma=False,
    )
```

```python
import functools

import jax
import jax.numpy as jnp
from jax import lax
from jax.experimental import pallas as pl
from jax.experimental.pallas import tpu as pltpu
from jax.sharding import PartitionSpec as P


STEPS = 6
LANES = 128
PAD = 8
COPIES = 2
ALL_AXES = ("tile", "level", "member")
VMEM = pl.BlockSpec(memory_space=pltpu.VMEM)
SMEM = pl.BlockSpec(memory_space=pltpu.SMEM)
HBM = pl.BlockSpec(memory_space=pltpu.HBM)
HIGHEST = lax.Precision.HIGHEST
PARAMS = pltpu.CompilerParams(vmem_limit_bytes=20 << 20)


def chunk_number():
    member = lax.axis_index("member")
    core = lax.axis_index("tile")
    low = lax.rem(member, 2)
    high = lax.rem(member // 2, 2)
    mine = jnp.where(core == 0, 2 * high + low, 2 * low + high)
    other = jnp.where(core == 0, 2 * low + high, 2 * high + low)
    return core, mine, other


def wet_mask(land_ref, rank_ref, tile, rows):
    row = lax.broadcasted_iota(jnp.int32, (rows, LANES), 0)
    land = land_ref[pl.ds(tile, 1), :]
    dry = jnp.where(rank_ref[tile] >= 0, 0, rows)
    return (row >= jnp.maximum(land, dry)).astype(jnp.float32)


def slot_owner(rank_ref, slot, tiles):
    tile, owned = jnp.int32(0), jnp.int32(0)
    for t in range(tiles):
        here = (rank_ref[t] == slot).astype(jnp.int32)
        owned, tile = owned + here, tile + t * here
    return owned > 0, tile


def tile_lanes(tile):
    return pl.ds(pl.multiple_of(tile * LANES, LANES), LANES)


def signed_number(land_ref, rank_ref, core, tile, rows, tiles):
    number = (core * tiles + tile + 1).astype(jnp.float32)
    return (2.0 * wet_mask(land_ref, rank_ref, tile, rows) - 1.0) * number


def sums_kernel(
    sizes, rank_hbm, temp_hbm, land_hbm, send_ref, keep_ref, temp_ref, land_ref, rank_out, rank_ref, sem
):
    members, fields, rows, tiles, _ = sizes
    core, mine, other = chunk_number()
    pairs = [(rank_hbm, rank_ref), (land_hbm, land_ref), (rank_hbm, rank_out)]
    for plane in range(members * fields):
        for part in range(COPIES):
            at = pl.ds(part * rows // COPIES, rows // COPIES)
            pairs.append((temp_hbm.at[plane, at], temp_ref.at[plane, at]))
    copies = [pltpu.make_async_copy(*pair, sem.at[number]) for number, pair in enumerate(pairs)]
    for copy in copies:
        copy.start()
    send_ref[...] = jnp.zeros_like(send_ref)
    keep_ref[...] = jnp.zeros_like(keep_ref)
    for copy in copies:
        copy.wait()
    for tile in range(tiles):
        lanes = slice(tile * LANES, (tile + 1) * LANES)

        @pl.when(rank_ref[tile] >= 0)
        def _():
            rank = rank_ref[tile]
            wet = wet_mask(land_ref, rank_ref, tile, rows)
            for ref, slot, field in ((send_ref, other, 1 - core), (keep_ref, mine, core)):
                total = temp_ref[field, :, lanes] * wet
                for member in range(1, members):
                    total = total + temp_ref[member * fields + field, :, lanes] * wet
                ref[jnp.bitwise_xor(slot, rank)] = total


def pack_kernel(sizes, rank_ref, temp_ref, kappa_ref, land_ref, pack_ref):
    _, fields, rows, tiles, _ = sizes
    core, _, _ = chunk_number()
    for tile in range(tiles):
        lanes = slice(tile * LANES, (tile + 1) * LANES)

        @pl.when(rank_ref[tile] >= 0)
        def _():
            rank = rank_ref[tile]
            wet = wet_mask(land_ref, rank_ref, tile, rows)
            for field in range(fields):
                pack_ref[field, rank] = temp_ref[(1 - core) * fields + field, :, lanes] * wet
            for part in range(3):
                pack_ref[fields + part, rank] = kappa_ref[part, :, lanes]
            pack_ref[fields + 3, rank] = signed_number(land_ref, rank_ref, core, tile, rows, tiles)


def make_weights(sizes, rank_ref, kappa_ref, land_ref, pack_ref, weight_ref, pad_ref, face_ref):
    _, fields, rows, tiles, slots = sizes
    core, _, _ = chunk_number()
    band = float(2 * tiles)
    zeros = jnp.zeros((PAD, LANES), jnp.float32)
    inside = slice(PAD, PAD + rows)
    for slot in range(slots):
        owned, tile = slot_owner(rank_ref, slot, tiles)
        for part in range(4):
            pad_ref[part, slot, :PAD, :] = zeros
            pad_ref[part, slot, PAD + rows :, :] = zeros

        @pl.when(owned)
        def _():
            for part in range(3):
                pad_ref[part, slot, inside, :] = kappa_ref[part, :, tile_lanes(tile)]
            pad_ref[3, slot, inside, :] = signed_number(land_ref, rank_ref, core, tile, rows, tiles)

        @pl.when(jnp.logical_not(owned))
        def _():
            for part in range(4):
                pad_ref[part, slot, inside, :] = pack_ref[fields + part, slot]

    lane = lax.broadcasted_iota(jnp.int32, (8, LANES), 1)
    is_first, is_last = lane == 0, lane == LANES - 1
    numbers = [jnp.abs(pad_ref[3, slot, PAD : PAD + 8, :]) for slot in range(slots)]
    joined = []
    for slot in range(slots):
        here, following = numbers[slot], numbers[(slot + 1) % slots]
        expected = jnp.where(here == band, 1.0, here + 1.0)
        joined.append((following == expected).astype(jnp.float32))

    def east(values):
        rolled = [pltpu.roll(x, LANES - 1, axis=1) for x in values]
        return [jnp.where(is_last, rolled[(t + 1) % slots], rolled[t]) for t in range(slots)]

    def west(values):
        rolled = [pltpu.roll(x, 1, axis=1) for x in values]
        return [jnp.where(is_first, rolled[t - 1], rolled[t]) for t in range(slots)]

    to_east = [jnp.where(is_last, joined[t], 1.0) for t in range(slots)]
    to_west = [jnp.where(is_first, joined[t - 1], 1.0) for t in range(slots)]

    def each(f, *lists):
        return [f(*values) for values in zip(*lists, strict=True)]

    def load(ref, part, start):
        return [ref[part, slot, start : start + 8, :] for slot in range(slots)]

    def flags(start):
        return [(x > 0.0).astype(jnp.float32) for x in load(pad_ref, 3, start)]

    for part in range(4):
        for slot in range(slots):
            face_ref[part, slot, :PAD, :] = zeros
    for block in range(rows // 8):
        start = PAD + 8 * block
        kyy, kxy, wet = load(pad_ref, 1, start), load(pad_ref, 2, start), flags(start)
        kyy_n, kxy_n, wet_n = load(pad_ref, 1, start + 1), load(pad_ref, 2, start + 1), flags(start + 1)
        y_gate = each(lambda w, n: w * n, wet, wet_n)
        ay = each(lambda k, n, g: 0.5 * (k + n) * g, kyy, kyy_n, y_gate)
        cy = each(lambda k, n, g: 0.125 * (k + n) * g, kxy, kxy_n, y_gate)
        for part, values in enumerate((cy, west(cy), east(cy), ay)):
            for slot in range(slots):
                face_ref[part, slot, start : start + 8, :] = values[slot]
    for block in range(rows // 8):
        start = PAD + 8 * block
        kxx, kxy, wet = load(pad_ref, 0, start), load(pad_ref, 2, start), flags(start)
        wet_e = each(lambda w, j: w * j, east(wet), to_east)
        wet_w = each(lambda w, j: w * j, west(wet), to_west)
        x_gate = each(lambda w, e: w * e, wet, wet_e)
        ax = each(lambda k, e, g: 0.5 * (k + e) * g, kxx, east(kxx), x_gate)
        cx = each(lambda k, e, g: 0.125 * (k + e) * g, kxy, east(kxy), x_gate)
        axw, cxw = west(ax), west(cx)
        cy, cyw, cye, ay = (load(face_ref, part, start) for part in range(4))
        cysw, cyse, ays = (load(face_ref, part, start - 1) for part in (1, 2, 3))
        terms = (
            each(lambda w, a, b, c, d: 1.0 - w * (a + b + c + d), wet, ax, axw, ay, ays),
            each(lambda w, a, b, c: w * (a + b - c), wet, ay, cx, cxw),
            each(lambda w, a, b, c: w * (a - b + c), wet, ays, cx, cxw),
            each(lambda w, a, b, c: w * (a + b - c), wet_w, axw, cyw, cysw),
            each(lambda w, a, b: w * (a + b), wet_w, cxw, cyw),
            each(lambda w, a, b: w * (-a - b), wet_w, cxw, cysw),
            each(lambda w, a, b, c: w * (a - b + c), wet_e, ax, cye, cyse),
            each(lambda w, a, b: w * (-a - b), wet_e, cx, cye),
            each(lambda w, a, b: w * (a + b), wet_e, cx, cyse),
        )
        for number, values in enumerate(terms):
            for slot in range(slots):
                weight_ref[number, slot, 8 * block : 8 * block + 8, :] = values[slot]


def run_steps(planes, rows, slots, weight_ref, u_ref):
    lane = lax.broadcasted_iota(jnp.int32, (8, LANES), 1)
    is_first, is_last = lane == 0, lane == LANES - 1

    def one_step(source, target):
        for block in range(rows // 8):
            base, row0 = PAD + 8 * block, 8 * block
            parts = [[] for _ in range(planes)]
            for slot in range(slots):
                weights = [weight_ref[k, slot, row0 : row0 + 8, :] for k in range(9)]
                for plane in range(planes):
                    here = u_ref[source, plane, slot, base : base + 8, :]
                    up = u_ref[source, plane, slot, base + 1 : base + 9, :]
                    down = u_ref[source, plane, slot, base - 1 : base + 7, :]
                    centre, to_west, to_east = (
                        weights[3 * g] * here + weights[3 * g + 1] * up + weights[3 * g + 2] * down
                        for g in range(3)
                    )
                    parts[plane].append(
                        (centre, pltpu.roll(to_west, LANES - 1, axis=1), pltpu.roll(to_east, 1, axis=1))
                    )
            for plane in range(planes):
                for slot in range(slots):
                    centre, from_east, from_west = parts[plane][slot]
                    after = parts[plane][(slot + 1) % slots][1]
                    before = parts[plane][slot - 1][2]
                    u_ref[target, plane, slot, base : base + 8, :] = (
                        centre
                        + jnp.where(is_last, after, from_east)
                        + jnp.where(is_first, before, from_west)
                    )

    def two_steps(_, carry):
        one_step(0, 1)
        one_step(1, 0)
        return carry

    lax.fori_loop(0, STEPS // 2, two_steps, 0)


def clear_pads(planes, rows, slots, u_ref):
    zeros = jnp.zeros((PAD, LANES), jnp.float32)
    for half in range(2):
        for plane in range(planes):
            for slot in range(slots):
                u_ref[half, plane, slot, :PAD, :] = zeros
                u_ref[half, plane, slot, PAD + rows :, :] = zeros


def member_kernel(sizes, rank_ref, kappa_ref, temp_ref, land_ref, pack_ref, weight_ref, stepped_ref, u_ref, pad_ref, face_ref):
    _, fields, rows, tiles, slots = sizes
    core, _, _ = chunk_number()
    make_weights(sizes, rank_ref, kappa_ref, land_ref, pack_ref, weight_ref, pad_ref, face_ref)
    clear_pads(fields, rows, slots, u_ref)
    inside = slice(PAD, PAD + rows)
    for slot in range(slots):
        owned, tile = slot_owner(rank_ref, slot, tiles)

        @pl.when(owned)
        def _():
            wet = wet_mask(land_ref, rank_ref, tile, rows)
            for field in range(fields):
                u_ref[0, field, slot, inside, :] = temp_ref[core * fields + field, :, tile_lanes(tile)] * wet

        @pl.when(jnp.logical_not(owned))
        def _():
            for field in range(fields):
                u_ref[0, field, slot, inside, :] = pack_ref[field, slot]

    run_steps(fields, rows, slots, weight_ref, u_ref)
    for field in range(fields):
        for slot in range(slots):
            stepped_ref[field, slot] = u_ref[0, field, slot, inside, :]


def mean_kernel(sizes, samples, gathered_ref, weight_ref, stepped_ref, u_ref):
    _, _, rows, _, slots = sizes
    _, mine, _ = chunk_number()
    clear_pads(1, rows, slots, u_ref)
    inside = slice(PAD, PAD + rows)
    for slot in range(slots):
        u_ref[0, 0, slot, inside, :] = gathered_ref[jnp.bitwise_xor(mine, slot)] * (1.0 / samples)
    run_steps(1, rows, slots, weight_ref, u_ref)
    for slot in range(slots):
        stepped_ref[slot] = u_ref[0, 0, slot, inside, :]


def observe_planes(fields, cell, frac):
    rows, columns = fields[0].shape
    count = cell.shape[1]
    frac_east, frac_north = frac[0:1, :], frac[1:2, :]
    column, row = lax.rem(cell, columns), lax.rem(cell // columns, rows)
    at = lax.broadcasted_iota(jnp.int32, (columns, count), 0) - column
    pick = jnp.where(at == 0, 1.0 - frac_east, jnp.where(at == 1, frac_east, 0.0))
    values = jnp.concatenate(fields, axis=0)
    picked = jnp.dot(values, pick, precision=HIGHEST, preferred_element_type=jnp.float32)
    at = lax.broadcasted_iota(jnp.int32, (rows, count), 0) - row
    pick = jnp.where(at == 0, 1.0 - frac_north, jnp.where(at == 1, frac_north, 0.0))
    return [
        jnp.sum(picked[number * rows : (number + 1) * rows] * pick, axis=0, keepdims=True)
        for number in range(len(fields))
    ]


def observe_kernel(sizes, rank_ref, own_ref, other_ref, cell_ref, frac_ref, stepped_ref, seen_ref):
    members, fields, rows, tiles, _ = sizes
    core, _, _ = chunk_number()
    for tile in range(tiles):
        lanes = slice(tile * LANES, (tile + 1) * LANES)
        rank = rank_ref[tile]

        @pl.when(rank >= 0)
        def _():
            for field in range(fields):
                stepped_ref[core * fields + field, :, lanes] = own_ref[field, rank]
                stepped_ref[(1 - core) * fields + field, :, lanes] = other_ref[field, rank]

        @pl.when(rank < 0)
        def _():
            for plane in range(members * fields):
                stepped_ref[plane, :, lanes] = jnp.zeros((rows, LANES), jnp.float32)

    planes = [stepped_ref[plane] for plane in range(members * fields)]
    halves = cell_ref.shape[1] // LANES
    for plane, seen in enumerate(observe_planes(planes, cell_ref[...], frac_ref[...])):
        for half in range(halves):
            at = plane * halves + half
            seen_ref[at : at + 1, :] = seen[:, half * LANES : (half + 1) * LANES]


def picks_kernel(sizes, cell_ref, frac_ref, column_ref, row_ref):
    _, _, rows, tiles, _ = sizes
    columns, count = tiles * LANES, cell_ref.shape[1]
    cell, frac = cell_ref[...], frac_ref[...]
    column, row = lax.rem(cell, columns), lax.rem(cell // columns, rows)
    at = lax.broadcasted_iota(jnp.int32, (columns, count), 0) - column
    pick = jnp.where(at == 0, 1.0 - frac[0:1, :], jnp.where(at == 1, frac[0:1, :], 0.0))
    for number, part in enumerate(split_parts(pick)):
        for place in ((0, 1, 2), (3, 4), (5,))[number]:
            column_ref[place * columns : (place + 1) * columns, :] = part
    at = lax.broadcasted_iota(jnp.int32, (rows, count), 0) - row
    row_ref[...] = jnp.where(at == 0, 1.0 - frac[1:2, :], jnp.where(at == 1, frac[1:2, :], 0.0))


def split_parts(values):
    high = values.astype(jnp.bfloat16)
    rest = values - high.astype(jnp.float32)
    middle = rest.astype(jnp.bfloat16)
    low = (rest - middle.astype(jnp.float32)).astype(jnp.bfloat16)
    return high, middle, low


def split_values(values):
    high, middle, low = split_parts(values)
    return jnp.concatenate([high, middle, low, high, middle, high], axis=1)


def observe_mean(sizes, rank_ref, mean_ref, column_ref, row_ref, whole_ref):
    _, _, _, tiles, _ = sizes
    for tile in range(tiles):
        lanes = slice(tile * LANES, (tile + 1) * LANES)
        rank = rank_ref[tile]
        wet = jnp.where(rank >= 0, 1.0, 0.0)
        whole_ref[:, lanes] = mean_ref[jnp.maximum(rank, 0)] * wet
    picked = jnp.dot(split_values(whole_ref[...]), column_ref[...], preferred_element_type=jnp.float32)
    return jnp.sum(picked * row_ref[...], axis=0, keepdims=True)


def own_field_kernel(
    sizes, rank_ref, mean_ref, stepped_ref, column_ref, row_ref, field_hbm, mean_seen_ref, field_ref, whole_ref, sem
):
    members, _, _, _, _ = sizes
    core, _, _ = chunk_number()
    write_planes(sizes, core, rank_ref, mean_ref, stepped_ref, field_hbm, field_ref, sem)
    mean_seen_ref[...] = observe_mean(sizes, rank_ref, mean_ref, column_ref, row_ref, whole_ref)
    for copy in plane_copies(sizes, range(members), core, field_hbm, field_ref, sem):
        copy.wait()


def plane_copies(sizes, of_members, field, field_hbm, field_ref, sem):
    _, fields, rows, _, _ = sizes
    copies = []
    for member in of_members:
        for part in range(COPIES):
            at = pl.ds(part * rows // COPIES, rows // COPIES)
            target = field_hbm.at[member * fields + field, at]
            copies.append(pltpu.make_async_copy(field_ref.at[member, at], target, sem.at[member * COPIES + part]))
    return copies


def write_planes(sizes, field, rank_ref, mean_ref, stepped_ref, field_hbm, field_ref, sem):
    members, fields, _, tiles, _ = sizes
    for member in range(members):
        for tile in range(tiles):
            lanes = slice(tile * LANES, (tile + 1) * LANES)
            rank = rank_ref[tile]

            @pl.when(rank >= 0)
            def _():
                field_ref[member, :, lanes] = stepped_ref[member * fields + field, :, lanes] - mean_ref[rank]

            @pl.when(rank < 0)
            def _():
                field_ref[member, :, lanes] = stepped_ref[member * fields + field, :, lanes]

        for copy in plane_copies(sizes, [member], field, field_hbm, field_ref, sem):
            copy.start()


def final_kernel(
    sizes, ensemble, rank_ref, other_ref, column_ref, row_ref, own_seen_ref, seen_ref, stepped_ref, started_hbm,
    field_hbm, anomaly_hbm, variance_hbm, field_ref, whole_ref, anomaly_ref, variance_ref, sem,
):
    members, fields, _, _, _ = sizes
    core, _, _ = chunk_number()
    write_planes(sizes, 1 - core, rank_ref, other_ref, stepped_ref, field_hbm, field_ref, sem)
    own_seen = own_seen_ref[...]
    other_seen = observe_mean(sizes, rank_ref, other_ref, column_ref, row_ref, whole_ref)
    halves = row_ref.shape[1] // LANES
    stride = members * fields * halves
    sets = seen_ref.shape[0] // stride

    def tree(values):
        while len(values) > 1:
            values = [a + b for a, b in zip(values[0::2], values[1::2], strict=True)]
        return values[0]

    for field in range(fields):
        mean_seen = jnp.where(core == field, own_seen, other_seen)
        for half in range(halves):
            lanes = slice(half * LANES, (half + 1) * LANES)
            mean = mean_seen[:, lanes]
            observed = []
            for part in range(sets):
                for member in range(members):
                    at = part * stride + (member * fields + field) * halves + half
                    observed.append(seen_ref[at : at + 1, :] - mean)
            centre = tree(observed) / ensemble
            anomaly = [value - centre for value in observed]
            variance_ref[field : field + 1, lanes] = tree([value * value for value in anomaly]) / ensemble
            for member in range(members):
                anomaly_ref[member, field : field + 1, lanes] = anomaly[member]
    small = (
        pltpu.make_async_copy(anomaly_ref, anomaly_hbm, sem.at[members * COPIES]),
        pltpu.make_async_copy(variance_ref, variance_hbm, sem.at[members * COPIES + 1]),
    )
    for copy in small:
        copy.start()
    for copy in plane_copies(sizes, range(members), 1 - core, field_hbm, field_ref, sem):
        copy.wait()
    for copy in small:
        copy.wait()


def local(temp_salt, diffusivity, wet_rank, land_rows, obs_cell, obs_frac):
    members, fields, levels, rows, columns = temp_salt.shape
    tiles = wet_rank.shape[0]
    cores, level_count, member_count = (lax.axis_size(axis) for axis in ALL_AXES)
    slots = tiles * cores // 2
    chips = level_count * member_count
    bits = chips.bit_length() - 1
    assert cores == 2 and fields == 2 and members == 2 and levels == 1 and slots == 4
    assert columns == tiles * LANES and chips == 1 << bits and bits >= 3
    count = obs_cell.shape[0]
    planes = members * fields
    sizes = (members, fields, rows, tiles, slots)
    samples = members * levels * chips
    level_bit = bits - 1

    def device(core, chip):
        return core * chips + chip

    def exchange(value, masks):
        if masks is None:
            to = lambda core, chip: (1 - core, chip)
        else:
            to = lambda core, chip: (core, chip ^ masks[core])
        pairs = [(device(core, chip), device(*to(core, chip))) for core in range(2) for chip in range(chips)]
        return lax.ppermute(value, ALL_AXES, pairs)

    def struct(*shape):
        return jax.ShapeDtypeStruct(shape, jnp.float32)

    def call(kernel, out_shape, operands, scratch=(), cycles=1000, in_specs=None, out_specs=None, aliases={}):
        return pl.pallas_call(
            functools.partial(kernel, sizes),
            out_shape=out_shape,
            in_specs=in_specs or [SMEM if x.shape == wet_rank.shape else VMEM for x in operands],
            out_specs=out_specs or jax.tree.map(lambda _: VMEM, out_shape),
            scratch_shapes=list(scratch),
            input_output_aliases=aliases,
            compiler_params=PARAMS,
            cost_estimate=pl.CostEstimate(flops=cycles * 4096, bytes_accessed=1 << 20, transcendentals=0),
        )(*operands)

    def halo(count):
        return pltpu.VMEM((2, count, slots, rows + 2 * PAD, LANES), jnp.float32)

    temp = temp_salt.reshape(planes, rows, columns)
    land = land_rows.reshape(tiles, LANES)
    cell = obs_cell.reshape(1, count)
    masks = {1: (1, 2), 2: (2, 1), 3: (3, 3)}

    inputs = tuple(pltpu.with_memory_space_constraint(x, pltpu.HBM) for x in (wet_rank, temp, land))
    send, keep, temp, land, rank = call(
        sums_kernel,
        (
            struct(slots, rows, LANES),
            struct(slots, rows, LANES),
            struct(planes, rows, columns),
            jax.ShapeDtypeStruct((tiles, LANES), jnp.int32),
            jax.ShapeDtypeStruct((tiles,), jnp.int32),
        ),
        inputs,
        scratch=[pltpu.SMEM((tiles,), jnp.int32), pltpu.SemaphoreType.DMA((3 + planes * COPIES,))],
        in_specs=[HBM] * 3,
    )
    arrived = exchange(send, None)
    pack = call(pack_kernel, struct(fields + 4, slots, rows, LANES), (rank, temp, diffusivity, land))
    packed = exchange(pack, None)
    total = keep + arrived
    got = [exchange(total[k], masks[k]) for k in (1, 2, 3)]
    total = (total[0] + got[0]) + (got[1] + got[2])

    face = pltpu.VMEM((4, slots, rows + 2 * PAD, LANES), jnp.float32)
    weights, own = call(
        member_kernel, (struct(9, slots, rows, LANES), struct(fields, slots, rows, LANES)),
        (rank, diffusivity, temp, land, packed), [halo(fields), face, face], cycles=6000,
    )
    other = exchange(own, None)
    stepped, seen = call(
        observe_kernel, (struct(planes, rows, columns), struct(planes * count // LANES, LANES)),
        (rank, own, other, cell, obs_frac), cycles=2000,
    )

    for bit in [level_bit] + list(range(2, level_bit)):
        mask = (1 << bit, 1 << bit)
        if bit == level_bit:
            total = total + exchange(total, mask)
        else:
            got = exchange(jnp.concatenate([total, seen], axis=0), mask)
            total = total + got[:rows]
            seen = jnp.concatenate([seen, got[rows:]], axis=0)
    payload = jnp.concatenate([total, seen], axis=0)
    got = [payload] + [exchange(payload, masks[k]) for k in (1, 2, 3)]
    gathered = jnp.stack([x[:rows] for x in got])
    seen = jnp.concatenate([x[rows:] for x in got], axis=0)

    def step_mean(sizes, *refs):
        mean_kernel(sizes, samples, *refs)

    own_mean = call(step_mean, struct(slots, rows, LANES), (gathered, weights), [halo(1)], cycles=2000)
    other_mean = exchange(own_mean, None)
    column_picks, row_picks = call(
        picks_kernel,
        (jax.ShapeDtypeStruct((6 * columns, count), jnp.bfloat16), struct(rows, count)), (cell, obs_frac),
    )
    plane_scratch = pltpu.VMEM((members, rows, columns), jnp.float32)
    whole_scratch = pltpu.VMEM((rows, columns), jnp.float32)
    started, own_seen = call(
        own_field_kernel, (struct(planes, rows, columns), struct(1, count)),
        (rank, own_mean, stepped, column_picks, row_picks),
        [plane_scratch, whole_scratch, pltpu.SemaphoreType.DMA((members * COPIES,))], out_specs=(HBM, VMEM),
    )

    def last_kernel(sizes, *refs):
        final_kernel(sizes, members * member_count, *refs)

    operands = (rank, other_mean, column_picks, row_picks, own_seen, seen, stepped, started)
    field, anomaly, variance = call(
        last_kernel,
        (struct(planes, rows, columns), struct(members, fields, count), struct(fields, count)),
        operands,
        [
            plane_scratch,
            whole_scratch,
            pltpu.VMEM((members, fields, count), jnp.float32),
            pltpu.VMEM((fields, count), jnp.float32),
            pltpu.SemaphoreType.DMA((members * COPIES + 2,)),
        ],
        in_specs=[SMEM] + [VMEM] * 6 + [HBM],
        out_specs=(HBM, HBM, HBM),
        aliases={len(operands) - 1: 0},
    )
    return field.reshape(members, fields, levels, rows, columns), anomaly, variance


def solution(mesh):
    placed = (
        P("member", None, "level", None, "tile"),
        P(None, None, "tile"),
        P("tile"),
        P("tile"),
        P(("tile", "level")),
        P(None, ("tile", "level")),
    )

    return jax.shard_map(
        local,
        mesh=mesh,
        in_specs=placed,
        out_specs=(
            P("member", None, "level", None, "tile"),
            P("member", None, ("tile", "level")),
            P(None, ("tile", "level")),
        ),
        check_vma=False,
    )
```

```python
import functools

import jax
import jax.numpy as jnp
from jax import lax
from jax.experimental import pallas as pl
from jax.experimental.pallas import tpu as pltpu
from jax.sharding import PartitionSpec as P


STEPS = 6
LANES = 128
PAD = 8
COPIES = 1
ALL_AXES = ("tile", "level", "member")
VMEM = pl.BlockSpec(memory_space=pltpu.VMEM)
SMEM = pl.BlockSpec(memory_space=pltpu.SMEM)
HBM = pl.BlockSpec(memory_space=pltpu.HBM)
HIGHEST = lax.Precision.HIGHEST
PARAMS = pltpu.CompilerParams(vmem_limit_bytes=20 << 20)


def chunk_number():
    member = lax.axis_index("member")
    core = lax.axis_index("tile")
    low = lax.rem(member, 2)
    high = lax.rem(member // 2, 2)
    mine = jnp.where(core == 0, 2 * high + low, 2 * low + high)
    other = jnp.where(core == 0, 2 * low + high, 2 * high + low)
    return core, mine, other


def wet_mask(land_ref, rank_ref, tile, rows):
    row = lax.broadcasted_iota(jnp.int32, (rows, LANES), 0)
    land = land_ref[pl.ds(tile, 1), :]
    dry = jnp.where(rank_ref[tile] >= 0, 0, rows)
    return (row >= jnp.maximum(land, dry)).astype(jnp.float32)


def slot_owner(rank_ref, slot, tiles):
    tile, owned = jnp.int32(0), jnp.int32(0)
    for t in range(tiles):
        here = (rank_ref[t] == slot).astype(jnp.int32)
        owned, tile = owned + here, tile + t * here
    return owned > 0, tile


def tile_lanes(tile):
    return pl.ds(pl.multiple_of(tile * LANES, LANES), LANES)


def signed_number(land_ref, rank_ref, core, tile, rows, tiles):
    number = (core * tiles + tile + 1).astype(jnp.float32)
    return (2.0 * wet_mask(land_ref, rank_ref, tile, rows) - 1.0) * number


def slot_sums(sizes, rank_ref, land_ref, load, slot, total_ref):
    members, _, rows, tiles, _ = sizes
    for tile in range(tiles):
        lanes = slice(tile * LANES, (tile + 1) * LANES)

        @pl.when(rank_ref[tile] >= 0)
        def _():
            rank = rank_ref[tile]
            wet = wet_mask(land_ref, rank_ref, tile, rows)
            total = load(0, lanes) * wet
            for member in range(1, members):
                total = total + load(member, lanes) * wet
            total_ref[jnp.bitwise_xor(slot, rank)] = total


def sums_kernel(sizes, rank_hbm, temp_hbm, land_hbm, send_ref, land_ref, rank_out, rank_ref, temp_ref, sem):
    members, fields, _, _, _ = sizes
    core, _, other = chunk_number()
    pairs = [(rank_hbm, rank_ref), (land_hbm, land_ref), (rank_hbm, rank_out)]
    pairs += [(temp_hbm.at[member * fields + 1 - core], temp_ref.at[member]) for member in range(members)]
    copies = [pltpu.make_async_copy(*pair, sem.at[number]) for number, pair in enumerate(pairs)]
    for copy in copies:
        copy.start()
    send_ref[...] = jnp.zeros_like(send_ref)
    for copy in copies:
        copy.wait()
    slot_sums(sizes, rank_ref, land_ref, lambda member, lanes: temp_ref[member, :, lanes], other, send_ref)


def pack_kernel(sizes, rank_ref, temp_ref, kappa_hbm, land_ref, pack_ref, keep_ref, kappa_ref, sem):
    _, fields, rows, tiles, _ = sizes
    core, mine, _ = chunk_number()
    copy = pltpu.make_async_copy(kappa_hbm, kappa_ref, sem)
    copy.start()
    keep_ref[...] = jnp.zeros_like(keep_ref)
    slot_sums(
        sizes, rank_ref, land_ref, lambda member, lanes: temp_ref[member * fields + core, :, lanes], mine, keep_ref
    )
    for tile in range(tiles):
        lanes = slice(tile * LANES, (tile + 1) * LANES)

        @pl.when(rank_ref[tile] >= 0)
        def _():
            rank = rank_ref[tile]
            wet = wet_mask(land_ref, rank_ref, tile, rows)
            for field in range(fields):
                pack_ref[field, rank] = temp_ref[(1 - core) * fields + field, :, lanes] * wet
            pack_ref[fields + 3, rank] = signed_number(land_ref, rank_ref, core, tile, rows, tiles)

    copy.wait()
    for tile in range(tiles):
        lanes = slice(tile * LANES, (tile + 1) * LANES)

        @pl.when(rank_ref[tile] >= 0)
        def _():
            for part in range(3):
                pack_ref[fields + part, rank_ref[tile]] = kappa_ref[part, :, lanes]


def make_weights(sizes, rank_ref, kappa_ref, land_ref, pack_ref, weight_ref, pad_ref, face_ref):
    _, fields, rows, tiles, slots = sizes
    core, _, _ = chunk_number()
    band = float(2 * tiles)
    zeros = jnp.zeros((PAD, LANES), jnp.float32)
    inside = slice(PAD, PAD + rows)
    for slot in range(slots):
        owned, tile = slot_owner(rank_ref, slot, tiles)
        for part in range(4):
            pad_ref[part, slot, :PAD, :] = zeros
            pad_ref[part, slot, PAD + rows :, :] = zeros

        @pl.when(owned)
        def _():
            for part in range(3):
                pad_ref[part, slot, inside, :] = kappa_ref[part, :, tile_lanes(tile)]
            pad_ref[3, slot, inside, :] = signed_number(land_ref, rank_ref, core, tile, rows, tiles)

        @pl.when(jnp.logical_not(owned))
        def _():
            for part in range(4):
                pad_ref[part, slot, inside, :] = pack_ref[fields + part, slot]

    lane = lax.broadcasted_iota(jnp.int32, (8, LANES), 1)
    is_first, is_last = lane == 0, lane == LANES - 1
    numbers = [jnp.abs(pad_ref[3, slot, PAD : PAD + 8, :]) for slot in range(slots)]
    joined = []
    for slot in range(slots):
        here, following = numbers[slot], numbers[(slot + 1) % slots]
        expected = jnp.where(here == band, 1.0, here + 1.0)
        joined.append((following == expected).astype(jnp.float32))

    def east(values):
        rolled = [pltpu.roll(x, LANES - 1, axis=1) for x in values]
        return [jnp.where(is_last, rolled[(t + 1) % slots], rolled[t]) for t in range(slots)]

    def west(values):
        rolled = [pltpu.roll(x, 1, axis=1) for x in values]
        return [jnp.where(is_first, rolled[t - 1], rolled[t]) for t in range(slots)]

    to_east = [jnp.where(is_last, joined[t], 1.0) for t in range(slots)]
    to_west = [jnp.where(is_first, joined[t - 1], 1.0) for t in range(slots)]

    def each(f, *lists):
        return [f(*values) for values in zip(*lists, strict=True)]

    def load(ref, part, start):
        return [ref[part, slot, start : start + 8, :] for slot in range(slots)]

    def flags(start):
        return [(x > 0.0).astype(jnp.float32) for x in load(pad_ref, 3, start)]

    for part in range(4):
        for slot in range(slots):
            face_ref[part, slot, :PAD, :] = zeros
    for block in range(rows // 8):
        start = PAD + 8 * block
        kyy, kxy, wet = load(pad_ref, 1, start), load(pad_ref, 2, start), flags(start)
        kyy_n, kxy_n, wet_n = load(pad_ref, 1, start + 1), load(pad_ref, 2, start + 1), flags(start + 1)
        y_gate = each(lambda w, n: w * n, wet, wet_n)
        ay = each(lambda k, n, g: 0.5 * (k + n) * g, kyy, kyy_n, y_gate)
        cy = each(lambda k, n, g: 0.125 * (k + n) * g, kxy, kxy_n, y_gate)
        for part, values in enumerate((cy, west(cy), east(cy), ay)):
            for slot in range(slots):
                face_ref[part, slot, start : start + 8, :] = values[slot]
    for block in range(rows // 8):
        start = PAD + 8 * block
        kxx, kxy, wet = load(pad_ref, 0, start), load(pad_ref, 2, start), flags(start)
        wet_e = each(lambda w, j: w * j, east(wet), to_east)
        wet_w = each(lambda w, j: w * j, west(wet), to_west)
        x_gate = each(lambda w, e: w * e, wet, wet_e)
        ax = each(lambda k, e, g: 0.5 * (k + e) * g, kxx, east(kxx), x_gate)
        cx = each(lambda k, e, g: 0.125 * (k + e) * g, kxy, east(kxy), x_gate)
        axw, cxw = west(ax), west(cx)
        cy, cyw, cye, ay = (load(face_ref, part, start) for part in range(4))
        cysw, cyse, ays = (load(face_ref, part, start - 1) for part in (1, 2, 3))
        terms = (
            each(lambda w, a, b, c, d: 1.0 - w * (a + b + c + d), wet, ax, axw, ay, ays),
            each(lambda w, a, b, c: w * (a + b - c), wet, ay, cx, cxw),
            each(lambda w, a, b, c: w * (a - b + c), wet, ays, cx, cxw),
            each(lambda w, a, b, c: w * (a + b - c), wet_w, axw, cyw, cysw),
            each(lambda w, a, b: w * (a + b), wet_w, cxw, cyw),
            each(lambda w, a, b: w * (-a - b), wet_w, cxw, cysw),
            each(lambda w, a, b, c: w * (a - b + c), wet_e, ax, cye, cyse),
            each(lambda w, a, b: w * (-a - b), wet_e, cx, cye),
            each(lambda w, a, b: w * (a + b), wet_e, cx, cyse),
        )
        for number, values in enumerate(terms):
            for slot in range(slots):
                weight_ref[number, slot, 8 * block : 8 * block + 8, :] = values[slot]


def run_steps(planes, rows, slots, weight_ref, u_ref):
    lane = lax.broadcasted_iota(jnp.int32, (8, LANES), 1)
    is_first, is_last = lane == 0, lane == LANES - 1

    def one_step(source, target):
        for block in range(rows // 8):
            base, row0 = PAD + 8 * block, 8 * block
            parts = [[] for _ in range(planes)]
            for slot in range(slots):
                weights = [weight_ref[k, slot, row0 : row0 + 8, :] for k in range(9)]
                for plane in range(planes):
                    here = u_ref[source, plane, slot, base : base + 8, :]
                    up = u_ref[source, plane, slot, base + 1 : base + 9, :]
                    down = u_ref[source, plane, slot, base - 1 : base + 7, :]
                    centre, to_west, to_east = (
                        weights[3 * g] * here + weights[3 * g + 1] * up + weights[3 * g + 2] * down
                        for g in range(3)
                    )
                    parts[plane].append(
                        (centre, pltpu.roll(to_west, LANES - 1, axis=1), pltpu.roll(to_east, 1, axis=1))
                    )
            for plane in range(planes):
                for slot in range(slots):
                    centre, from_east, from_west = parts[plane][slot]
                    after = parts[plane][(slot + 1) % slots][1]
                    before = parts[plane][slot - 1][2]
                    u_ref[target, plane, slot, base : base + 8, :] = (
                        centre
                        + jnp.where(is_last, after, from_east)
                        + jnp.where(is_first, before, from_west)
                    )

    def two_steps(_, carry):
        one_step(0, 1)
        one_step(1, 0)
        return carry

    lax.fori_loop(0, STEPS // 2, two_steps, 0)


def clear_pads(planes, rows, slots, u_ref):
    zeros = jnp.zeros((PAD, LANES), jnp.float32)
    for half in range(2):
        for plane in range(planes):
            for slot in range(slots):
                u_ref[half, plane, slot, :PAD, :] = zeros
                u_ref[half, plane, slot, PAD + rows :, :] = zeros


def member_kernel(sizes, rank_ref, kappa_ref, temp_ref, land_ref, pack_ref, weight_ref, stepped_ref, u_ref, pad_ref, face_ref):
    _, fields, rows, tiles, slots = sizes
    core, _, _ = chunk_number()
    make_weights(sizes, rank_ref, kappa_ref, land_ref, pack_ref, weight_ref, pad_ref, face_ref)
    clear_pads(fields, rows, slots, u_ref)
    inside = slice(PAD, PAD + rows)
    for slot in range(slots):
        owned, tile = slot_owner(rank_ref, slot, tiles)

        @pl.when(owned)
        def _():
            wet = wet_mask(land_ref, rank_ref, tile, rows)
            for field in range(fields):
                u_ref[0, field, slot, inside, :] = temp_ref[core * fields + field, :, tile_lanes(tile)] * wet

        @pl.when(jnp.logical_not(owned))
        def _():
            for field in range(fields):
                u_ref[0, field, slot, inside, :] = pack_ref[field, slot]

    run_steps(fields, rows, slots, weight_ref, u_ref)
    for field in range(fields):
        for slot in range(slots):
            stepped_ref[field, slot] = u_ref[0, field, slot, inside, :]


def mean_kernel(sizes, samples, gathered_ref, weight_ref, stepped_ref, u_ref):
    _, _, rows, _, slots = sizes
    _, mine, _ = chunk_number()
    clear_pads(1, rows, slots, u_ref)
    inside = slice(PAD, PAD + rows)
    for slot in range(slots):
        u_ref[0, 0, slot, inside, :] = gathered_ref[jnp.bitwise_xor(mine, slot)] * (1.0 / samples)
    run_steps(1, rows, slots, weight_ref, u_ref)
    for slot in range(slots):
        stepped_ref[slot] = u_ref[0, 0, slot, inside, :]


def observe_planes(fields, cell, frac):
    rows, columns = fields[0].shape
    count = cell.shape[1]
    frac_east, frac_north = frac[0:1, :], frac[1:2, :]
    column, row = lax.rem(cell, columns), lax.rem(cell // columns, rows)
    at = lax.broadcasted_iota(jnp.int32, (columns, count), 0) - column
    pick = jnp.where(at == 0, 1.0 - frac_east, jnp.where(at == 1, frac_east, 0.0))
    values = jnp.concatenate(fields, axis=0)
    picked = jnp.dot(values, pick, precision=HIGHEST, preferred_element_type=jnp.float32)
    at = lax.broadcasted_iota(jnp.int32, (rows, count), 0) - row
    pick = jnp.where(at == 0, 1.0 - frac_north, jnp.where(at == 1, frac_north, 0.0))
    return [
        jnp.sum(picked[number * rows : (number + 1) * rows] * pick, axis=0, keepdims=True)
        for number in range(len(fields))
    ]


def observe_kernel(sizes, rank_ref, own_ref, other_ref, cell_ref, frac_ref, stepped_ref, seen_ref):
    members, fields, rows, tiles, _ = sizes
    core, _, _ = chunk_number()
    for tile in range(tiles):
        lanes = slice(tile * LANES, (tile + 1) * LANES)
        rank = rank_ref[tile]

        @pl.when(rank >= 0)
        def _():
            for field in range(fields):
                stepped_ref[core * fields + field, :, lanes] = own_ref[field, rank]
                stepped_ref[(1 - core) * fields + field, :, lanes] = other_ref[field, rank]

        @pl.when(rank < 0)
        def _():
            for plane in range(members * fields):
                stepped_ref[plane, :, lanes] = jnp.zeros((rows, LANES), jnp.float32)

    planes = [stepped_ref[plane] for plane in range(members * fields)]
    halves = cell_ref.shape[1] // LANES
    for plane, seen in enumerate(observe_planes(planes, cell_ref[...], frac_ref[...])):
        for half in range(halves):
            at = plane * halves + half
            seen_ref[at : at + 1, :] = seen[:, half * LANES : (half + 1) * LANES]


def picks_kernel(sizes, cell_ref, frac_ref, column_ref, row_ref):
    _, _, rows, tiles, _ = sizes
    columns, count = tiles * LANES, cell_ref.shape[1]
    cell, frac = cell_ref[...], frac_ref[...]
    column, row = lax.rem(cell, columns), lax.rem(cell // columns, rows)
    at = lax.broadcasted_iota(jnp.int32, (columns, count), 0) - column
    pick = jnp.where(at == 0, 1.0 - frac[0:1, :], jnp.where(at == 1, frac[0:1, :], 0.0))
    for number, part in enumerate(split_parts(pick)):
        for place in ((0, 1, 2), (3, 4), (5,))[number]:
            column_ref[place * columns : (place + 1) * columns, :] = part
    at = lax.broadcasted_iota(jnp.int32, (rows, count), 0) - row
    row_ref[...] = jnp.where(at == 0, 1.0 - frac[1:2, :], jnp.where(at == 1, frac[1:2, :], 0.0))


def split_parts(values):
    high = values.astype(jnp.bfloat16)
    rest = values - high.astype(jnp.float32)
    middle = rest.astype(jnp.bfloat16)
    low = (rest - middle.astype(jnp.float32)).astype(jnp.bfloat16)
    return high, middle, low


def split_values(values):
    high, middle, low = split_parts(values)
    return jnp.concatenate([high, middle, low, high, middle, high], axis=1)


def observe_mean(sizes, rank_ref, mean_ref, column_ref, row_ref, whole_ref):
    _, _, _, tiles, _ = sizes
    for tile in range(tiles):
        lanes = slice(tile * LANES, (tile + 1) * LANES)
        rank = rank_ref[tile]
        wet = jnp.where(rank >= 0, 1.0, 0.0)
        whole_ref[:, lanes] = mean_ref[jnp.maximum(rank, 0)] * wet
    picked = jnp.dot(split_values(whole_ref[...]), column_ref[...], preferred_element_type=jnp.float32)
    return jnp.sum(picked * row_ref[...], axis=0, keepdims=True)


def own_field_kernel(
    sizes, rank_ref, mean_ref, stepped_ref, column_ref, row_ref, field_hbm, mean_seen_ref, field_ref, whole_ref, sem
):
    members, _, _, _, _ = sizes
    core, _, _ = chunk_number()
    write_planes(sizes, core, rank_ref, mean_ref, stepped_ref, field_hbm, field_ref, sem)
    mean_seen_ref[...] = observe_mean(sizes, rank_ref, mean_ref, column_ref, row_ref, whole_ref)
    for copy in plane_copies(sizes, range(members), core, field_hbm, field_ref, sem):
        copy.wait()


def plane_copies(sizes, of_members, field, field_hbm, field_ref, sem):
    _, fields, rows, _, _ = sizes
    copies = []
    for member in of_members:
        for part in range(COPIES):
            at = pl.ds(part * rows // COPIES, rows // COPIES)
            target = field_hbm.at[member * fields + field, at]
            copies.append(pltpu.make_async_copy(field_ref.at[member, at], target, sem.at[member * COPIES + part]))
    return copies


def write_planes(sizes, field, rank_ref, mean_ref, stepped_ref, field_hbm, field_ref, sem):
    members, fields, _, tiles, _ = sizes
    for member in range(members):
        for tile in range(tiles):
            lanes = slice(tile * LANES, (tile + 1) * LANES)
            rank = rank_ref[tile]

            @pl.when(rank >= 0)
            def _():
                field_ref[member, :, lanes] = stepped_ref[member * fields + field, :, lanes] - mean_ref[rank]

            @pl.when(rank < 0)
            def _():
                field_ref[member, :, lanes] = stepped_ref[member * fields + field, :, lanes]

        for copy in plane_copies(sizes, [member], field, field_hbm, field_ref, sem):
            copy.start()


def final_kernel(
    sizes, ensemble, rank_ref, other_ref, column_ref, row_ref, own_seen_ref, seen_ref, stepped_ref, started_hbm,
    field_hbm, anomaly_hbm, variance_hbm, field_ref, whole_ref, anomaly_ref, variance_ref, sem,
):
    members, fields, _, _, _ = sizes
    core, _, _ = chunk_number()
    write_planes(sizes, 1 - core, rank_ref, other_ref, stepped_ref, field_hbm, field_ref, sem)
    own_seen = own_seen_ref[...]
    other_seen = observe_mean(sizes, rank_ref, other_ref, column_ref, row_ref, whole_ref)
    halves = row_ref.shape[1] // LANES
    stride = members * fields * halves
    sets = seen_ref.shape[0] // stride

    def tree(values):
        while len(values) > 1:
            values = [a + b for a, b in zip(values[0::2], values[1::2], strict=True)]
        return values[0]

    for field in range(fields):
        mean_seen = jnp.where(core == field, own_seen, other_seen)
        for half in range(halves):
            lanes = slice(half * LANES, (half + 1) * LANES)
            mean = mean_seen[:, lanes]
            observed = []
            for part in range(sets):
                for member in range(members):
                    at = part * stride + (member * fields + field) * halves + half
                    observed.append(seen_ref[at : at + 1, :] - mean)
            centre = tree(observed) / ensemble
            anomaly = [value - centre for value in observed]
            variance_ref[field : field + 1, lanes] = tree([value * value for value in anomaly]) / ensemble
            for member in range(members):
                anomaly_ref[member, field : field + 1, lanes] = anomaly[member]
    small = (
        pltpu.make_async_copy(anomaly_ref, anomaly_hbm, sem.at[members * COPIES]),
        pltpu.make_async_copy(variance_ref, variance_hbm, sem.at[members * COPIES + 1]),
    )
    for copy in small:
        copy.start()
    for copy in plane_copies(sizes, range(members), 1 - core, field_hbm, field_ref, sem):
        copy.wait()
    for copy in small:
        copy.wait()


def local(temp_salt, diffusivity, wet_rank, land_rows, obs_cell, obs_frac):
    members, fields, levels, rows, columns = temp_salt.shape
    tiles = wet_rank.shape[0]
    cores, level_count, member_count = (lax.axis_size(axis) for axis in ALL_AXES)
    slots = tiles * cores // 2
    chips = level_count * member_count
    bits = chips.bit_length() - 1
    assert cores == 2 and fields == 2 and members == 2 and levels == 1 and slots == 4
    assert columns == tiles * LANES and chips == 1 << bits and bits >= 3
    count = obs_cell.shape[0]
    planes = members * fields
    sizes = (members, fields, rows, tiles, slots)
    samples = members * levels * chips
    level_bit = bits - 1

    def device(core, chip):
        return core * chips + chip

    def exchange(value, masks):
        if masks is None:
            to = lambda core, chip: (1 - core, chip)
        else:
            to = lambda core, chip: (core, chip ^ masks[core])
        pairs = [(device(core, chip), device(*to(core, chip))) for core in range(2) for chip in range(chips)]
        return lax.ppermute(value, ALL_AXES, pairs)

    def struct(*shape):
        return jax.ShapeDtypeStruct(shape, jnp.float32)

    def call(kernel, out_shape, operands, scratch=(), cycles=1000, in_specs=None, out_specs=None, aliases={}):
        return pl.pallas_call(
            functools.partial(kernel, sizes),
            out_shape=out_shape,
            in_specs=in_specs or [SMEM if x.shape == wet_rank.shape else VMEM for x in operands],
            out_specs=out_specs or jax.tree.map(lambda _: VMEM, out_shape),
            scratch_shapes=list(scratch),
            input_output_aliases=aliases,
            compiler_params=PARAMS,
            cost_estimate=pl.CostEstimate(flops=cycles * 4096, bytes_accessed=1 << 20, transcendentals=0),
        )(*operands)

    def halo(count):
        return pltpu.VMEM((2, count, slots, rows + 2 * PAD, LANES), jnp.float32)

    temp = temp_salt.reshape(planes, rows, columns)
    land = land_rows.reshape(tiles, LANES)
    cell = obs_cell.reshape(1, count)
    masks = {1: (1, 2), 2: (2, 1), 3: (3, 3)}

    inputs = tuple(pltpu.with_memory_space_constraint(x, pltpu.HBM) for x in (wet_rank, temp, land))
    send, land, rank = call(
        sums_kernel,
        (
            struct(slots, rows, LANES),
            jax.ShapeDtypeStruct((tiles, LANES), jnp.int32),
            jax.ShapeDtypeStruct((tiles,), jnp.int32),
        ),
        inputs,
        scratch=[
            pltpu.SMEM((tiles,), jnp.int32),
            pltpu.VMEM((members, rows, columns), jnp.float32),
            pltpu.SemaphoreType.DMA((3 + members,)),
        ],
        in_specs=[HBM] * 3,
    )
    arrived = exchange(send, None)
    pack, keep, kappa = call(
        pack_kernel,
        (struct(fields + 4, slots, rows, LANES), struct(slots, rows, LANES), struct(*diffusivity.shape)),
        (rank, temp, pltpu.with_memory_space_constraint(diffusivity, pltpu.HBM), land),
        scratch=[pltpu.SemaphoreType.DMA],
        in_specs=[SMEM, VMEM, HBM, VMEM],
    )
    packed = exchange(pack, None)
    total = keep + arrived
    got = [exchange(total[k], masks[k]) for k in (1, 2, 3)]
    total = (total[0] + got[0]) + (got[1] + got[2])

    face = pltpu.VMEM((4, slots, rows + 2 * PAD, LANES), jnp.float32)
    weights, own = call(
        member_kernel, (struct(9, slots, rows, LANES), struct(fields, slots, rows, LANES)),
        (rank, kappa, temp, land, packed), [halo(fields), face, face], cycles=6000,
    )
    other = exchange(own, None)
    stepped, seen = call(
        observe_kernel, (struct(planes, rows, columns), struct(planes * count // LANES, LANES)),
        (rank, own, other, cell, obs_frac), cycles=2000,
    )

    for bit in [level_bit] + list(range(2, level_bit)):
        mask = (1 << bit, 1 << bit)
        if bit == level_bit:
            total = total + exchange(total, mask)
        else:
            got = exchange(jnp.concatenate([total, seen], axis=0), mask)
            total = total + got[:rows]
            seen = jnp.concatenate([seen, got[rows:]], axis=0)
    payload = jnp.concatenate([total, seen], axis=0)
    got = [payload] + [exchange(payload, masks[k]) for k in (1, 2, 3)]
    gathered = jnp.stack([x[:rows] for x in got])
    seen = jnp.concatenate([x[rows:] for x in got], axis=0)

    def step_mean(sizes, *refs):
        mean_kernel(sizes, samples, *refs)

    own_mean = call(step_mean, struct(slots, rows, LANES), (gathered, weights), [halo(1)], cycles=2000)
    other_mean = exchange(own_mean, None)
    column_picks, row_picks = call(
        picks_kernel,
        (jax.ShapeDtypeStruct((6 * columns, count), jnp.bfloat16), struct(rows, count)), (cell, obs_frac),
    )
    plane_scratch = pltpu.VMEM((members, rows, columns), jnp.float32)
    whole_scratch = pltpu.VMEM((rows, columns), jnp.float32)
    started, own_seen = call(
        own_field_kernel, (struct(planes, rows, columns), struct(1, count)),
        (rank, own_mean, stepped, column_picks, row_picks),
        [plane_scratch, whole_scratch, pltpu.SemaphoreType.DMA((members * COPIES,))], out_specs=(HBM, VMEM),
    )

    def last_kernel(sizes, *refs):
        final_kernel(sizes, members * member_count, *refs)

    operands = (rank, other_mean, column_picks, row_picks, own_seen, seen, stepped, started)
    field, anomaly, variance = call(
        last_kernel,
        (struct(planes, rows, columns), struct(members, fields, count), struct(fields, count)),
        operands,
        [
            plane_scratch,
            whole_scratch,
            pltpu.VMEM((members, fields, count), jnp.float32),
            pltpu.VMEM((fields, count), jnp.float32),
            pltpu.SemaphoreType.DMA((members * COPIES + 2,)),
        ],
        in_specs=[SMEM] + [VMEM] * 6 + [HBM],
        out_specs=(HBM, HBM, HBM),
        aliases={len(operands) - 1: 0},
    )
    return field.reshape(members, fields, levels, rows, columns), anomaly, variance


def solution(mesh):
    placed = (
        P("member", None, "level", None, "tile"),
        P(None, None, "tile"),
        P("tile"),
        P("tile"),
        P(("tile", "level")),
        P(None, ("tile", "level")),
    )

    return jax.shard_map(
        local,
        mesh=mesh,
        in_specs=placed,
        out_specs=(
            P("member", None, "level", None, "tile"),
            P("member", None, ("tile", "level")),
            P(None, ("tile", "level")),
        ),
        check_vma=False,
    )
```

```python
import functools

import jax
import jax.numpy as jnp
from jax import lax
from jax.experimental import pallas as pl
from jax.experimental.pallas import tpu as pltpu
from jax.sharding import PartitionSpec as P


STEPS = 6
LANES = 128
PAD = 8
COPIES = 1
ALL_AXES = ("tile", "level", "member")
VMEM = pl.BlockSpec(memory_space=pltpu.VMEM)
SMEM = pl.BlockSpec(memory_space=pltpu.SMEM)
HBM = pl.BlockSpec(memory_space=pltpu.HBM)
HIGHEST = lax.Precision.HIGHEST
PARAMS = pltpu.CompilerParams(vmem_limit_bytes=20 << 20)


def chunk_number():
    member = lax.axis_index("member")
    core = lax.axis_index("tile")
    low = lax.rem(member, 2)
    high = lax.rem(member // 2, 2)
    mine = jnp.where(core == 0, 2 * high + low, 2 * low + high)
    other = jnp.where(core == 0, 2 * low + high, 2 * high + low)
    return core, mine, other


def wet_mask(land_ref, rank_ref, tile, rows):
    row = lax.broadcasted_iota(jnp.int32, (rows, LANES), 0)
    land = land_ref[pl.ds(tile, 1), :]
    dry = jnp.where(rank_ref[tile] >= 0, 0, rows)
    return (row >= jnp.maximum(land, dry)).astype(jnp.float32)


def slot_owner(rank_ref, slot, tiles):
    tile, owned = jnp.int32(0), jnp.int32(0)
    for t in range(tiles):
        here = (rank_ref[t] == slot).astype(jnp.int32)
        owned, tile = owned + here, tile + t * here
    return owned > 0, tile


def tile_lanes(tile):
    return pl.ds(pl.multiple_of(tile * LANES, LANES), LANES)


def signed_number(land_ref, rank_ref, core, tile, rows, tiles):
    number = (core * tiles + tile + 1).astype(jnp.float32)
    return (2.0 * wet_mask(land_ref, rank_ref, tile, rows) - 1.0) * number


def sums_kernel(
    sizes, rank_hbm, temp_hbm, land_hbm, send_ref, keep_ref, temp_ref, land_ref, rank_out, rank_ref, sem
):
    members, fields, rows, tiles, _ = sizes
    core, mine, other = chunk_number()
    pairs = [(rank_hbm, rank_ref), (land_hbm, land_ref), (rank_hbm, rank_out)]
    pairs.append((temp_hbm, temp_ref))
    copies = [pltpu.make_async_copy(*pair, sem.at[number]) for number, pair in enumerate(pairs)]
    for copy in copies:
        copy.start()
    send_ref[...] = jnp.zeros_like(send_ref)
    keep_ref[...] = jnp.zeros_like(keep_ref)
    for copy in copies:
        copy.wait()
    for tile in range(tiles):
        lanes = slice(tile * LANES, (tile + 1) * LANES)

        @pl.when(rank_ref[tile] >= 0)
        def _():
            rank = rank_ref[tile]
            wet = wet_mask(land_ref, rank_ref, tile, rows)
            for ref, slot, field in ((send_ref, other, 1 - core), (keep_ref, mine, core)):
                total = temp_ref[field, :, lanes] * wet
                for member in range(1, members):
                    total = total + temp_ref[member * fields + field, :, lanes] * wet
                ref[jnp.bitwise_xor(slot, rank)] = total


def pack_kernel(sizes, rank_ref, temp_ref, kappa_ref, land_ref, pack_ref):
    _, fields, rows, tiles, _ = sizes
    core, _, _ = chunk_number()
    for tile in range(tiles):
        lanes = slice(tile * LANES, (tile + 1) * LANES)

        @pl.when(rank_ref[tile] >= 0)
        def _():
            rank = rank_ref[tile]
            wet = wet_mask(land_ref, rank_ref, tile, rows)
            for field in range(fields):
                pack_ref[field, rank] = temp_ref[(1 - core) * fields + field, :, lanes] * wet
            for part in range(3):
                pack_ref[fields + part, rank] = kappa_ref[part, :, lanes]
            pack_ref[fields + 3, rank] = signed_number(land_ref, rank_ref, core, tile, rows, tiles)


def make_weights(sizes, rank_ref, kappa_ref, land_ref, pack_ref, weight_ref, pad_ref, face_ref):
    _, fields, rows, tiles, slots = sizes
    core, _, _ = chunk_number()
    band = float(2 * tiles)
    zeros = jnp.zeros((PAD, LANES), jnp.float32)
    inside = slice(PAD, PAD + rows)
    for slot in range(slots):
        owned, tile = slot_owner(rank_ref, slot, tiles)
        for part in range(4):
            pad_ref[part, slot, :PAD, :] = zeros
            pad_ref[part, slot, PAD + rows :, :] = zeros

        @pl.when(owned)
        def _():
            for part in range(3):
                pad_ref[part, slot, inside, :] = kappa_ref[part, :, tile_lanes(tile)]
            pad_ref[3, slot, inside, :] = signed_number(land_ref, rank_ref, core, tile, rows, tiles)

        @pl.when(jnp.logical_not(owned))
        def _():
            for part in range(4):
                pad_ref[part, slot, inside, :] = pack_ref[fields + part, slot]

    lane = lax.broadcasted_iota(jnp.int32, (8, LANES), 1)
    is_first, is_last = lane == 0, lane == LANES - 1
    numbers = [jnp.abs(pad_ref[3, slot, PAD : PAD + 8, :]) for slot in range(slots)]
    joined = []
    for slot in range(slots):
        here, following = numbers[slot], numbers[(slot + 1) % slots]
        expected = jnp.where(here == band, 1.0, here + 1.0)
        joined.append((following == expected).astype(jnp.float32))

    def east(values):
        rolled = [pltpu.roll(x, LANES - 1, axis=1) for x in values]
        return [jnp.where(is_last, rolled[(t + 1) % slots], rolled[t]) for t in range(slots)]

    def west(values):
        rolled = [pltpu.roll(x, 1, axis=1) for x in values]
        return [jnp.where(is_first, rolled[t - 1], rolled[t]) for t in range(slots)]

    to_east = [jnp.where(is_last, joined[t], 1.0) for t in range(slots)]
    to_west = [jnp.where(is_first, joined[t - 1], 1.0) for t in range(slots)]

    def each(f, *lists):
        return [f(*values) for values in zip(*lists, strict=True)]

    def load(ref, part, start):
        return [ref[part, slot, start : start + 8, :] for slot in range(slots)]

    def flags(start):
        return [(x > 0.0).astype(jnp.float32) for x in load(pad_ref, 3, start)]

    for part in range(4):
        for slot in range(slots):
            face_ref[part, slot, :PAD, :] = zeros
    for block in range(rows // 8):
        start = PAD + 8 * block
        kyy, kxy, wet = load(pad_ref, 1, start), load(pad_ref, 2, start), flags(start)
        kyy_n, kxy_n, wet_n = load(pad_ref, 1, start + 1), load(pad_ref, 2, start + 1), flags(start + 1)
        y_gate = each(lambda w, n: w * n, wet, wet_n)
        ay = each(lambda k, n, g: 0.5 * (k + n) * g, kyy, kyy_n, y_gate)
        cy = each(lambda k, n, g: 0.125 * (k + n) * g, kxy, kxy_n, y_gate)
        for part, values in enumerate((cy, west(cy), east(cy), ay)):
            for slot in range(slots):
                face_ref[part, slot, start : start + 8, :] = values[slot]
    for block in range(rows // 8):
        start = PAD + 8 * block
        kxx, kxy, wet = load(pad_ref, 0, start), load(pad_ref, 2, start), flags(start)
        wet_e = each(lambda w, j: w * j, east(wet), to_east)
        wet_w = each(lambda w, j: w * j, west(wet), to_west)
        x_gate = each(lambda w, e: w * e, wet, wet_e)
        ax = each(lambda k, e, g: 0.5 * (k + e) * g, kxx, east(kxx), x_gate)
        cx = each(lambda k, e, g: 0.125 * (k + e) * g, kxy, east(kxy), x_gate)
        axw, cxw = west(ax), west(cx)
        cy, cyw, cye, ay = (load(face_ref, part, start) for part in range(4))
        cysw, cyse, ays = (load(face_ref, part, start - 1) for part in (1, 2, 3))
        terms = (
            each(lambda w, a, b, c, d: 1.0 - w * (a + b + c + d), wet, ax, axw, ay, ays),
            each(lambda w, a, b, c: w * (a + b - c), wet, ay, cx, cxw),
            each(lambda w, a, b, c: w * (a - b + c), wet, ays, cx, cxw),
            each(lambda w, a, b, c: w * (a + b - c), wet_w, axw, cyw, cysw),
            each(lambda w, a, b: w * (a + b), wet_w, cxw, cyw),
            each(lambda w, a, b: w * (-a - b), wet_w, cxw, cysw),
            each(lambda w, a, b, c: w * (a - b + c), wet_e, ax, cye, cyse),
            each(lambda w, a, b: w * (-a - b), wet_e, cx, cye),
            each(lambda w, a, b: w * (a + b), wet_e, cx, cyse),
        )
        for number, values in enumerate(terms):
            for slot in range(slots):
                weight_ref[number, slot, 8 * block : 8 * block + 8, :] = values[slot]


def run_steps(planes, rows, slots, weight_ref, u_ref):
    lane = lax.broadcasted_iota(jnp.int32, (8, LANES), 1)
    is_first, is_last = lane == 0, lane == LANES - 1

    def one_step(source, target):
        for block in range(rows // 8):
            base, row0 = PAD + 8 * block, 8 * block
            parts = [[] for _ in range(planes)]
            for slot in range(slots):
                weights = [weight_ref[k, slot, row0 : row0 + 8, :] for k in range(9)]
                for plane in range(planes):
                    here = u_ref[source, plane, slot, base : base + 8, :]
                    up = u_ref[source, plane, slot, base + 1 : base + 9, :]
                    down = u_ref[source, plane, slot, base - 1 : base + 7, :]
                    centre, to_west, to_east = (
                        weights[3 * g] * here + weights[3 * g + 1] * up + weights[3 * g + 2] * down
                        for g in range(3)
                    )
                    parts[plane].append(
                        (centre, pltpu.roll(to_west, LANES - 1, axis=1), pltpu.roll(to_east, 1, axis=1))
                    )
            for plane in range(planes):
                for slot in range(slots):
                    centre, from_east, from_west = parts[plane][slot]
                    after = parts[plane][(slot + 1) % slots][1]
                    before = parts[plane][slot - 1][2]
                    u_ref[target, plane, slot, base : base + 8, :] = (
                        centre
                        + jnp.where(is_last, after, from_east)
                        + jnp.where(is_first, before, from_west)
                    )

    def two_steps(_, carry):
        one_step(0, 1)
        one_step(1, 0)
        return carry

    lax.fori_loop(0, STEPS // 2, two_steps, 0)


def clear_pads(planes, rows, slots, u_ref):
    zeros = jnp.zeros((PAD, LANES), jnp.float32)
    for half in range(2):
        for plane in range(planes):
            for slot in range(slots):
                u_ref[half, plane, slot, :PAD, :] = zeros
                u_ref[half, plane, slot, PAD + rows :, :] = zeros


def member_kernel(sizes, rank_ref, kappa_ref, temp_ref, land_ref, pack_ref, weight_ref, stepped_ref, u_ref, pad_ref, face_ref):
    _, fields, rows, tiles, slots = sizes
    core, _, _ = chunk_number()
    make_weights(sizes, rank_ref, kappa_ref, land_ref, pack_ref, weight_ref, pad_ref, face_ref)
    clear_pads(fields, rows, slots, u_ref)
    inside = slice(PAD, PAD + rows)
    for slot in range(slots):
        owned, tile = slot_owner(rank_ref, slot, tiles)

        @pl.when(owned)
        def _():
            wet = wet_mask(land_ref, rank_ref, tile, rows)
            for field in range(fields):
                u_ref[0, field, slot, inside, :] = temp_ref[core * fields + field, :, tile_lanes(tile)] * wet

        @pl.when(jnp.logical_not(owned))
        def _():
            for field in range(fields):
                u_ref[0, field, slot, inside, :] = pack_ref[field, slot]

    run_steps(fields, rows, slots, weight_ref, u_ref)
    for field in range(fields):
        for slot in range(slots):
            stepped_ref[field, slot] = u_ref[0, field, slot, inside, :]


def mean_kernel(sizes, samples, gathered_ref, weight_ref, stepped_ref, u_ref):
    _, _, rows, _, slots = sizes
    _, mine, _ = chunk_number()
    clear_pads(1, rows, slots, u_ref)
    inside = slice(PAD, PAD + rows)
    for slot in range(slots):
        u_ref[0, 0, slot, inside, :] = gathered_ref[jnp.bitwise_xor(mine, slot)] * (1.0 / samples)
    run_steps(1, rows, slots, weight_ref, u_ref)
    for slot in range(slots):
        stepped_ref[slot] = u_ref[0, 0, slot, inside, :]


def observe_planes(fields, cell, frac):
    rows, columns = fields[0].shape
    count = cell.shape[1]
    frac_east, frac_north = frac[0:1, :], frac[1:2, :]
    column, row = lax.rem(cell, columns), lax.rem(cell // columns, rows)
    at = lax.broadcasted_iota(jnp.int32, (columns, count), 0) - column
    pick = jnp.where(at == 0, 1.0 - frac_east, jnp.where(at == 1, frac_east, 0.0))
    values = jnp.concatenate(fields, axis=0)
    picked = jnp.dot(values, pick, precision=HIGHEST, preferred_element_type=jnp.float32)
    at = lax.broadcasted_iota(jnp.int32, (rows, count), 0) - row
    pick = jnp.where(at == 0, 1.0 - frac_north, jnp.where(at == 1, frac_north, 0.0))
    return [
        jnp.sum(picked[number * rows : (number + 1) * rows] * pick, axis=0, keepdims=True)
        for number in range(len(fields))
    ]


def observe_kernel(sizes, rank_ref, own_ref, other_ref, cell_ref, frac_ref, stepped_ref, seen_ref):
    members, fields, rows, tiles, _ = sizes
    core, _, _ = chunk_number()
    for tile in range(tiles):
        lanes = slice(tile * LANES, (tile + 1) * LANES)
        rank = rank_ref[tile]

        @pl.when(rank >= 0)
        def _():
            for field in range(fields):
                stepped_ref[core * fields + field, :, lanes] = own_ref[field, rank]
                stepped_ref[(1 - core) * fields + field, :, lanes] = other_ref[field, rank]

        @pl.when(rank < 0)
        def _():
            for plane in range(members * fields):
                stepped_ref[plane, :, lanes] = jnp.zeros((rows, LANES), jnp.float32)

    planes = [stepped_ref[plane] for plane in range(members * fields)]
    halves = cell_ref.shape[1] // LANES
    for plane, seen in enumerate(observe_planes(planes, cell_ref[...], frac_ref[...])):
        for half in range(halves):
            at = plane * halves + half
            seen_ref[at : at + 1, :] = seen[:, half * LANES : (half + 1) * LANES]


def picks_kernel(sizes, cell_ref, frac_ref, column_ref, row_ref):
    _, _, rows, tiles, _ = sizes
    columns, count = tiles * LANES, cell_ref.shape[1]
    cell, frac = cell_ref[...], frac_ref[...]
    column, row = lax.rem(cell, columns), lax.rem(cell // columns, rows)
    at = lax.broadcasted_iota(jnp.int32, (columns, count), 0) - column
    pick = jnp.where(at == 0, 1.0 - frac[0:1, :], jnp.where(at == 1, frac[0:1, :], 0.0))
    for number, part in enumerate(split_parts(pick)):
        for place in ((0, 1, 2), (3, 4), (5,))[number]:
            column_ref[place * columns : (place + 1) * columns, :] = part
    at = lax.broadcasted_iota(jnp.int32, (rows, count), 0) - row
    row_ref[...] = jnp.where(at == 0, 1.0 - frac[1:2, :], jnp.where(at == 1, frac[1:2, :], 0.0))


def split_parts(values):
    high = values.astype(jnp.bfloat16)
    rest = values - high.astype(jnp.float32)
    middle = rest.astype(jnp.bfloat16)
    low = (rest - middle.astype(jnp.float32)).astype(jnp.bfloat16)
    return high, middle, low


def split_values(values):
    high, middle, low = split_parts(values)
    return jnp.concatenate([high, middle, low, high, middle, high], axis=1)


def observe_mean(sizes, rank_ref, mean_ref, column_ref, row_ref, whole_ref):
    _, _, _, tiles, _ = sizes
    for tile in range(tiles):
        lanes = slice(tile * LANES, (tile + 1) * LANES)
        rank = rank_ref[tile]
        wet = jnp.where(rank >= 0, 1.0, 0.0)
        whole_ref[:, lanes] = mean_ref[jnp.maximum(rank, 0)] * wet
    picked = jnp.dot(split_values(whole_ref[...]), column_ref[...], preferred_element_type=jnp.float32)
    return jnp.sum(picked * row_ref[...], axis=0, keepdims=True)


def own_field_kernel(
    sizes, rank_ref, mean_ref, stepped_ref, column_ref, row_ref, field_hbm, mean_seen_ref, field_ref, whole_ref, sem
):
    members, _, _, _, _ = sizes
    core, _, _ = chunk_number()
    write_planes(sizes, core, rank_ref, mean_ref, stepped_ref, field_hbm, field_ref, sem)
    mean_seen_ref[...] = observe_mean(sizes, rank_ref, mean_ref, column_ref, row_ref, whole_ref)
    for copy in plane_copies(sizes, range(members), core, field_hbm, field_ref, sem):
        copy.wait()


def plane_copies(sizes, of_members, field, field_hbm, field_ref, sem):
    _, fields, rows, _, _ = sizes
    copies = []
    for member in of_members:
        for part in range(COPIES):
            at = pl.ds(part * rows // COPIES, rows // COPIES)
            target = field_hbm.at[member * fields + field, at]
            copies.append(pltpu.make_async_copy(field_ref.at[member, at], target, sem.at[member * COPIES + part]))
    return copies


def write_planes(sizes, field, rank_ref, mean_ref, stepped_ref, field_hbm, field_ref, sem):
    members, fields, _, tiles, _ = sizes
    for member in range(members):
        for tile in range(tiles):
            lanes = slice(tile * LANES, (tile + 1) * LANES)
            rank = rank_ref[tile]

            @pl.when(rank >= 0)
            def _():
                field_ref[member, :, lanes] = stepped_ref[member * fields + field, :, lanes] - mean_ref[rank]

            @pl.when(rank < 0)
            def _():
                field_ref[member, :, lanes] = stepped_ref[member * fields + field, :, lanes]

        for copy in plane_copies(sizes, [member], field, field_hbm, field_ref, sem):
            copy.start()


def final_kernel(
    sizes, ensemble, rank_ref, other_ref, column_ref, row_ref, own_seen_ref, seen_ref, stepped_ref, started_hbm,
    field_hbm, anomaly_hbm, variance_hbm, field_ref, whole_ref, anomaly_ref, variance_ref, sem,
):
    members, fields, _, _, _ = sizes
    core, _, _ = chunk_number()
    write_planes(sizes, 1 - core, rank_ref, other_ref, stepped_ref, field_hbm, field_ref, sem)
    own_seen = own_seen_ref[...]
    other_seen = observe_mean(sizes, rank_ref, other_ref, column_ref, row_ref, whole_ref)
    halves = row_ref.shape[1] // LANES
    stride = members * fields * halves
    sets = seen_ref.shape[0] // stride

    def tree(values):
        while len(values) > 1:
            values = [a + b for a, b in zip(values[0::2], values[1::2], strict=True)]
        return values[0]

    for field in range(fields):
        mean_seen = jnp.where(core == field, own_seen, other_seen)
        for half in range(halves):
            lanes = slice(half * LANES, (half + 1) * LANES)
            mean = mean_seen[:, lanes]
            observed = []
            for part in range(sets):
                for member in range(members):
                    at = part * stride + (member * fields + field) * halves + half
                    observed.append(seen_ref[at : at + 1, :] - mean)
            centre = tree(observed) / ensemble
            anomaly = [value - centre for value in observed]
            variance_ref[field : field + 1, lanes] = tree([value * value for value in anomaly]) / ensemble
            for member in range(members):
                anomaly_ref[member, field : field + 1, lanes] = anomaly[member]
    small = (
        pltpu.make_async_copy(anomaly_ref, anomaly_hbm, sem.at[members * COPIES]),
        pltpu.make_async_copy(variance_ref, variance_hbm, sem.at[members * COPIES + 1]),
    )
    for copy in small:
        copy.start()
    for copy in plane_copies(sizes, range(members), 1 - core, field_hbm, field_ref, sem):
        copy.wait()
    for copy in small:
        copy.wait()


def local(temp_salt, diffusivity, wet_rank, land_rows, obs_cell, obs_frac):
    members, fields, levels, rows, columns = temp_salt.shape
    tiles = wet_rank.shape[0]
    cores, level_count, member_count = (lax.axis_size(axis) for axis in ALL_AXES)
    slots = tiles * cores // 2
    chips = level_count * member_count
    bits = chips.bit_length() - 1
    assert cores == 2 and fields == 2 and members == 2 and levels == 1 and slots == 4
    assert columns == tiles * LANES and chips == 1 << bits and bits >= 3
    count = obs_cell.shape[0]
    planes = members * fields
    sizes = (members, fields, rows, tiles, slots)
    samples = members * levels * chips
    level_bit = bits - 1

    def device(core, chip):
        return core * chips + chip

    def exchange(value, masks):
        if masks is None:
            to = lambda core, chip: (1 - core, chip)
        else:
            to = lambda core, chip: (core, chip ^ masks[core])
        pairs = [(device(core, chip), device(*to(core, chip))) for core in range(2) for chip in range(chips)]
        return lax.ppermute(value, ALL_AXES, pairs)

    def struct(*shape):
        return jax.ShapeDtypeStruct(shape, jnp.float32)

    def call(kernel, out_shape, operands, scratch=(), cycles=1000, in_specs=None, out_specs=None, aliases={}):
        return pl.pallas_call(
            functools.partial(kernel, sizes),
            out_shape=out_shape,
            in_specs=in_specs or [SMEM if x.shape == wet_rank.shape else VMEM for x in operands],
            out_specs=out_specs or jax.tree.map(lambda _: VMEM, out_shape),
            scratch_shapes=list(scratch),
            input_output_aliases=aliases,
            compiler_params=PARAMS,
            cost_estimate=pl.CostEstimate(flops=cycles * 4096, bytes_accessed=1 << 20, transcendentals=0),
        )(*operands)

    def halo(count):
        return pltpu.VMEM((2, count, slots, rows + 2 * PAD, LANES), jnp.float32)

    temp = temp_salt.reshape(planes, rows, columns)
    land = land_rows.reshape(tiles, LANES)
    cell = obs_cell.reshape(1, count)
    masks = {1: (1, 2), 2: (2, 1), 3: (3, 3)}

    inputs = tuple(pltpu.with_memory_space_constraint(x, pltpu.HBM) for x in (wet_rank, temp, land))
    send, keep, temp, land, rank = call(
        sums_kernel,
        (
            struct(slots, rows, LANES),
            struct(slots, rows, LANES),
            struct(planes, rows, columns),
            jax.ShapeDtypeStruct((tiles, LANES), jnp.int32),
            jax.ShapeDtypeStruct((tiles,), jnp.int32),
        ),
        inputs,
        scratch=[pltpu.SMEM((tiles,), jnp.int32), pltpu.SemaphoreType.DMA((4,))],
        in_specs=[HBM] * 3,
    )
    arrived = exchange(send, None)
    pack = call(pack_kernel, struct(fields + 4, slots, rows, LANES), (rank, temp, diffusivity, land))
    packed = exchange(pack, None)
    total = keep + arrived
    got = [exchange(total[k], masks[k]) for k in (1, 2, 3)]
    total = (total[0] + got[0]) + (got[1] + got[2])

    face = pltpu.VMEM((4, slots, rows + 2 * PAD, LANES), jnp.float32)
    weights, own = call(
        member_kernel, (struct(9, slots, rows, LANES), struct(fields, slots, rows, LANES)),
        (rank, diffusivity, temp, land, packed), [halo(fields), face, face], cycles=6000,
    )
    other = exchange(own, None)
    stepped, seen = call(
        observe_kernel, (struct(planes, rows, columns), struct(planes * count // LANES, LANES)),
        (rank, own, other, cell, obs_frac), cycles=2000,
    )

    for bit in [level_bit] + list(range(2, level_bit)):
        mask = (1 << bit, 1 << bit)
        if bit == level_bit:
            total = total + exchange(total, mask)
        else:
            got = exchange(jnp.concatenate([total, seen], axis=0), mask)
            total = total + got[:rows]
            seen = jnp.concatenate([seen, got[rows:]], axis=0)
    payload = jnp.concatenate([total, seen], axis=0)
    got = [payload] + [exchange(payload, masks[k]) for k in (1, 2, 3)]
    gathered = jnp.stack([x[:rows] for x in got])
    seen = jnp.concatenate([x[rows:] for x in got], axis=0)

    def step_mean(sizes, *refs):
        mean_kernel(sizes, samples, *refs)

    own_mean = call(step_mean, struct(slots, rows, LANES), (gathered, weights), [halo(1)], cycles=2000)
    other_mean = exchange(own_mean, None)
    column_picks, row_picks = call(
        picks_kernel,
        (jax.ShapeDtypeStruct((6 * columns, count), jnp.bfloat16), struct(rows, count)), (cell, obs_frac),
    )
    plane_scratch = pltpu.VMEM((members, rows, columns), jnp.float32)
    whole_scratch = pltpu.VMEM((rows, columns), jnp.float32)
    started, own_seen = call(
        own_field_kernel, (struct(planes, rows, columns), struct(1, count)),
        (rank, own_mean, stepped, column_picks, row_picks),
        [plane_scratch, whole_scratch, pltpu.SemaphoreType.DMA((members * COPIES,))], out_specs=(HBM, VMEM),
    )

    def last_kernel(sizes, *refs):
        final_kernel(sizes, members * member_count, *refs)

    operands = (rank, other_mean, column_picks, row_picks, own_seen, seen, stepped, started)
    field, anomaly, variance = call(
        last_kernel,
        (struct(planes, rows, columns), struct(members, fields, count), struct(fields, count)),
        operands,
        [
            plane_scratch,
            whole_scratch,
            pltpu.VMEM((members, fields, count), jnp.float32),
            pltpu.VMEM((fields, count), jnp.float32),
            pltpu.SemaphoreType.DMA((members * COPIES + 2,)),
        ],
        in_specs=[SMEM] + [VMEM] * 6 + [HBM],
        out_specs=(HBM, HBM, HBM),
        aliases={len(operands) - 1: 0},
    )
    return field.reshape(members, fields, levels, rows, columns), anomaly, variance


def solution(mesh):
    placed = (
        P("member", None, "level", None, "tile"),
        P(None, None, "tile"),
        P("tile"),
        P("tile"),
        P(("tile", "level")),
        P(None, ("tile", "level")),
    )

    return jax.shard_map(
        local,
        mesh=mesh,
        in_specs=placed,
        out_specs=(
            P("member", None, "level", None, "tile"),
            P("member", None, ("tile", "level")),
            P(None, ("tile", "level")),
        ),
        check_vma=False,
    )
```

```python
import functools

import jax
import jax.numpy as jnp
from jax import lax
from jax.experimental import pallas as pl
from jax.experimental.pallas import tpu as pltpu
from jax.sharding import PartitionSpec as P


STEPS = 6
LANES = 128
PAD = 8
COPIES = 1
ALL_AXES = ("tile", "level", "member")
VMEM = pl.BlockSpec(memory_space=pltpu.VMEM)
SMEM = pl.BlockSpec(memory_space=pltpu.SMEM)
HBM = pl.BlockSpec(memory_space=pltpu.HBM)
HIGHEST = lax.Precision.HIGHEST
PARAMS = pltpu.CompilerParams(vmem_limit_bytes=20 << 20)
STEP_PARAMS = pltpu.CompilerParams(vmem_limit_bytes=20 << 20)


def chunk_number():
    member = lax.axis_index("member")
    core = lax.axis_index("tile")
    low = lax.rem(member, 2)
    high = lax.rem(member // 2, 2)
    mine = jnp.where(core == 0, 2 * high + low, 2 * low + high)
    other = jnp.where(core == 0, 2 * low + high, 2 * high + low)
    return core, mine, other


def wet_mask(land_ref, rank_ref, tile, rows):
    row = lax.broadcasted_iota(jnp.int32, (rows, LANES), 0)
    land = land_ref[pl.ds(tile, 1), :]
    dry = jnp.where(rank_ref[tile] >= 0, 0, rows)
    return (row >= jnp.maximum(land, dry)).astype(jnp.float32)


def slot_owner(rank_ref, slot, tiles):
    tile, owned = jnp.int32(0), jnp.int32(0)
    for t in range(tiles):
        here = (rank_ref[t] == slot).astype(jnp.int32)
        owned, tile = owned + here, tile + t * here
    return owned > 0, tile


def tile_lanes(tile):
    return pl.ds(pl.multiple_of(tile * LANES, LANES), LANES)


def signed_number(land_ref, rank_ref, core, tile, rows, tiles):
    number = (core * tiles + tile + 1).astype(jnp.float32)
    return (2.0 * wet_mask(land_ref, rank_ref, tile, rows) - 1.0) * number


def sums_kernel(
    sizes, rank_hbm, temp_hbm, land_hbm, send_ref, keep_ref, temp_ref, land_ref, rank_out, rank_ref, sem
):
    members, fields, rows, tiles, _ = sizes
    core, mine, other = chunk_number()
    pairs = [(rank_hbm, rank_ref), (land_hbm, land_ref), (rank_hbm, rank_out)]
    pairs.append((temp_hbm, temp_ref))
    copies = [pltpu.make_async_copy(*pair, sem.at[number]) for number, pair in enumerate(pairs)]
    for copy in copies:
        copy.start()
    send_ref[...] = jnp.zeros_like(send_ref)
    keep_ref[...] = jnp.zeros_like(keep_ref)
    for copy in copies:
        copy.wait()
    for tile in range(tiles):
        lanes = slice(tile * LANES, (tile + 1) * LANES)

        @pl.when(rank_ref[tile] >= 0)
        def _():
            rank = rank_ref[tile]
            wet = wet_mask(land_ref, rank_ref, tile, rows)
            for ref, slot, field in ((send_ref, other, 1 - core), (keep_ref, mine, core)):
                total = temp_ref[field, :, lanes] * wet
                for member in range(1, members):
                    total = total + temp_ref[member * fields + field, :, lanes] * wet
                ref[jnp.bitwise_xor(slot, rank)] = total


def pack_kernel(sizes, rank_ref, temp_ref, kappa_ref, land_ref, pack_ref):
    _, fields, rows, tiles, _ = sizes
    core, _, _ = chunk_number()
    for tile in range(tiles):
        lanes = slice(tile * LANES, (tile + 1) * LANES)

        @pl.when(rank_ref[tile] >= 0)
        def _():
            rank = rank_ref[tile]
            wet = wet_mask(land_ref, rank_ref, tile, rows)
            for field in range(fields):
                pack_ref[field, rank] = temp_ref[(1 - core) * fields + field, :, lanes] * wet
            for part in range(3):
                pack_ref[fields + part, rank] = kappa_ref[part, :, lanes]
            pack_ref[fields + 3, rank] = signed_number(land_ref, rank_ref, core, tile, rows, tiles)


def make_weights(sizes, rank_ref, kappa_ref, land_ref, pack_ref, weight_ref, pad_ref, face_ref):
    _, fields, rows, tiles, slots = sizes
    core, _, _ = chunk_number()
    band = float(2 * tiles)
    zeros = jnp.zeros((PAD, LANES), jnp.float32)
    inside = slice(PAD, PAD + rows)
    for slot in range(slots):
        owned, tile = slot_owner(rank_ref, slot, tiles)
        for part in range(4):
            pad_ref[part, slot, :PAD, :] = zeros
            pad_ref[part, slot, PAD + rows :, :] = zeros

        @pl.when(owned)
        def _():
            for part in range(3):
                pad_ref[part, slot, inside, :] = kappa_ref[part, :, tile_lanes(tile)]
            pad_ref[3, slot, inside, :] = signed_number(land_ref, rank_ref, core, tile, rows, tiles)

        @pl.when(jnp.logical_not(owned))
        def _():
            for part in range(4):
                pad_ref[part, slot, inside, :] = pack_ref[fields + part, slot]

    lane = lax.broadcasted_iota(jnp.int32, (8, LANES), 1)
    is_first, is_last = lane == 0, lane == LANES - 1
    numbers = [jnp.abs(pad_ref[3, slot, PAD : PAD + 8, :]) for slot in range(slots)]
    joined = []
    for slot in range(slots):
        here, following = numbers[slot], numbers[(slot + 1) % slots]
        expected = jnp.where(here == band, 1.0, here + 1.0)
        joined.append((following == expected).astype(jnp.float32))

    def east(values):
        rolled = [pltpu.roll(x, LANES - 1, axis=1) for x in values]
        return [jnp.where(is_last, rolled[(t + 1) % slots], rolled[t]) for t in range(slots)]

    def west(values):
        rolled = [pltpu.roll(x, 1, axis=1) for x in values]
        return [jnp.where(is_first, rolled[t - 1], rolled[t]) for t in range(slots)]

    to_east = [jnp.where(is_last, joined[t], 1.0) for t in range(slots)]
    to_west = [jnp.where(is_first, joined[t - 1], 1.0) for t in range(slots)]

    def each(f, *lists):
        return [f(*values) for values in zip(*lists, strict=True)]

    def load(ref, part, start):
        return [ref[part, slot, start : start + 8, :] for slot in range(slots)]

    def flags(start):
        return [(x > 0.0).astype(jnp.float32) for x in load(pad_ref, 3, start)]

    for part in range(4):
        for slot in range(slots):
            face_ref[part, slot, :PAD, :] = zeros
    for block in range(rows // 8):
        start = PAD + 8 * block
        kyy, kxy, wet = load(pad_ref, 1, start), load(pad_ref, 2, start), flags(start)
        kyy_n, kxy_n, wet_n = load(pad_ref, 1, start + 1), load(pad_ref, 2, start + 1), flags(start + 1)
        y_gate = each(lambda w, n: w * n, wet, wet_n)
        ay = each(lambda k, n, g: 0.5 * (k + n) * g, kyy, kyy_n, y_gate)
        cy = each(lambda k, n, g: 0.125 * (k + n) * g, kxy, kxy_n, y_gate)
        for part, values in enumerate((cy, west(cy), east(cy), ay)):
            for slot in range(slots):
                face_ref[part, slot, start : start + 8, :] = values[slot]
    for block in range(rows // 8):
        start = PAD + 8 * block
        kxx, kxy, wet = load(pad_ref, 0, start), load(pad_ref, 2, start), flags(start)
        wet_e = each(lambda w, j: w * j, east(wet), to_east)
        wet_w = each(lambda w, j: w * j, west(wet), to_west)
        x_gate = each(lambda w, e: w * e, wet, wet_e)
        ax = each(lambda k, e, g: 0.5 * (k + e) * g, kxx, east(kxx), x_gate)
        cx = each(lambda k, e, g: 0.125 * (k + e) * g, kxy, east(kxy), x_gate)
        axw, cxw = west(ax), west(cx)
        cy, cyw, cye, ay = (load(face_ref, part, start) for part in range(4))
        cysw, cyse, ays = (load(face_ref, part, start - 1) for part in (1, 2, 3))
        terms = (
            each(lambda w, a, b, c, d: 1.0 - w * (a + b + c + d), wet, ax, axw, ay, ays),
            each(lambda w, a, b, c: w * (a + b - c), wet, ay, cx, cxw),
            each(lambda w, a, b, c: w * (a - b + c), wet, ays, cx, cxw),
            each(lambda w, a, b, c: w * (a + b - c), wet_w, axw, cyw, cysw),
            each(lambda w, a, b: w * (a + b), wet_w, cxw, cyw),
            each(lambda w, a, b: w * (-a - b), wet_w, cxw, cysw),
            each(lambda w, a, b, c: w * (a - b + c), wet_e, ax, cye, cyse),
            each(lambda w, a, b: w * (-a - b), wet_e, cx, cye),
            each(lambda w, a, b: w * (a + b), wet_e, cx, cyse),
        )
        for number, values in enumerate(terms):
            for slot in range(slots):
                weight_ref[number, slot, 8 * block : 8 * block + 8, :] = values[slot]


def run_steps(planes, rows, slots, weight_ref, u_ref):
    lane = lax.broadcasted_iota(jnp.int32, (8, LANES), 1)
    is_first, is_last = lane == 0, lane == LANES - 1

    def one_step(source, target):
        for block in range(rows // 8):
            base, row0 = PAD + 8 * block, 8 * block
            parts = [[] for _ in range(planes)]
            for slot in range(slots):
                weights = [weight_ref[k, slot, row0 : row0 + 8, :] for k in range(9)]
                for plane in range(planes):
                    here = u_ref[source, plane, slot, base : base + 8, :]
                    up = u_ref[source, plane, slot, base + 1 : base + 9, :]
                    down = u_ref[source, plane, slot, base - 1 : base + 7, :]
                    centre, to_west, to_east = (
                        weights[3 * g] * here + weights[3 * g + 1] * up + weights[3 * g + 2] * down
                        for g in range(3)
                    )
                    parts[plane].append(
                        (centre, pltpu.roll(to_west, LANES - 1, axis=1), pltpu.roll(to_east, 1, axis=1))
                    )
            for plane in range(planes):
                for slot in range(slots):
                    centre, from_east, from_west = parts[plane][slot]
                    after = parts[plane][(slot + 1) % slots][1]
                    before = parts[plane][slot - 1][2]
                    u_ref[target, plane, slot, base : base + 8, :] = (
                        centre
                        + jnp.where(is_last, after, from_east)
                        + jnp.where(is_first, before, from_west)
                    )

    def two_steps(_, carry):
        one_step(0, 1)
        one_step(1, 0)
        return carry

    lax.fori_loop(0, STEPS // 2, two_steps, 0)


def clear_pads(planes, rows, slots, u_ref):
    zeros = jnp.zeros((PAD, LANES), jnp.float32)
    for half in range(2):
        for plane in range(planes):
            for slot in range(slots):
                u_ref[half, plane, slot, :PAD, :] = zeros
                u_ref[half, plane, slot, PAD + rows :, :] = zeros


def member_kernel(sizes, rank_ref, kappa_ref, temp_ref, land_ref, pack_ref, weight_ref, stepped_ref, u_ref, pad_ref, face_ref):
    _, fields, rows, tiles, slots = sizes
    core, _, _ = chunk_number()
    make_weights(sizes, rank_ref, kappa_ref, land_ref, pack_ref, weight_ref, pad_ref, face_ref)
    clear_pads(fields, rows, slots, u_ref)
    inside = slice(PAD, PAD + rows)
    for slot in range(slots):
        owned, tile = slot_owner(rank_ref, slot, tiles)

        @pl.when(owned)
        def _():
            wet = wet_mask(land_ref, rank_ref, tile, rows)
            for field in range(fields):
                u_ref[0, field, slot, inside, :] = temp_ref[core * fields + field, :, tile_lanes(tile)] * wet

        @pl.when(jnp.logical_not(owned))
        def _():
            for field in range(fields):
                u_ref[0, field, slot, inside, :] = pack_ref[field, slot]

    run_steps(fields, rows, slots, weight_ref, u_ref)
    for field in range(fields):
        for slot in range(slots):
            stepped_ref[field, slot] = u_ref[0, field, slot, inside, :]


def mean_kernel(sizes, samples, gathered_ref, weight_ref, stepped_ref, u_ref):
    _, _, rows, _, slots = sizes
    _, mine, _ = chunk_number()
    clear_pads(1, rows, slots, u_ref)
    inside = slice(PAD, PAD + rows)
    for slot in range(slots):
        u_ref[0, 0, slot, inside, :] = gathered_ref[jnp.bitwise_xor(mine, slot)] * (1.0 / samples)
    run_steps(1, rows, slots, weight_ref, u_ref)
    for slot in range(slots):
        stepped_ref[slot] = u_ref[0, 0, slot, inside, :]


def observe_planes(fields, cell, frac):
    rows, columns = fields[0].shape
    count = cell.shape[1]
    frac_east, frac_north = frac[0:1, :], frac[1:2, :]
    column, row = lax.rem(cell, columns), lax.rem(cell // columns, rows)
    at = lax.broadcasted_iota(jnp.int32, (columns, count), 0) - column
    pick = jnp.where(at == 0, 1.0 - frac_east, jnp.where(at == 1, frac_east, 0.0))
    values = jnp.concatenate(fields, axis=0)
    picked = jnp.dot(values, pick, precision=HIGHEST, preferred_element_type=jnp.float32)
    at = lax.broadcasted_iota(jnp.int32, (rows, count), 0) - row
    pick = jnp.where(at == 0, 1.0 - frac_north, jnp.where(at == 1, frac_north, 0.0))
    return [
        jnp.sum(picked[number * rows : (number + 1) * rows] * pick, axis=0, keepdims=True)
        for number in range(len(fields))
    ]


def observe_kernel(sizes, rank_ref, own_ref, other_ref, cell_ref, frac_ref, stepped_ref, seen_ref):
    members, fields, rows, tiles, _ = sizes
    core, _, _ = chunk_number()
    for tile in range(tiles):
        lanes = slice(tile * LANES, (tile + 1) * LANES)
        rank = rank_ref[tile]

        @pl.when(rank >= 0)
        def _():
            for field in range(fields):
                stepped_ref[core * fields + field, :, lanes] = own_ref[field, rank]
                stepped_ref[(1 - core) * fields + field, :, lanes] = other_ref[field, rank]

        @pl.when(rank < 0)
        def _():
            for plane in range(members * fields):
                stepped_ref[plane, :, lanes] = jnp.zeros((rows, LANES), jnp.float32)

    planes = [stepped_ref[plane] for plane in range(members * fields)]
    halves = cell_ref.shape[1] // LANES
    for plane, seen in enumerate(observe_planes(planes, cell_ref[...], frac_ref[...])):
        for half in range(halves):
            at = plane * halves + half
            seen_ref[at : at + 1, :] = seen[:, half * LANES : (half + 1) * LANES]


def picks_kernel(sizes, cell_ref, frac_ref, column_ref, row_ref):
    _, _, rows, tiles, _ = sizes
    columns, count = tiles * LANES, cell_ref.shape[1]
    cell, frac = cell_ref[...], frac_ref[...]
    column, row = lax.rem(cell, columns), lax.rem(cell // columns, rows)
    at = lax.broadcasted_iota(jnp.int32, (columns, count), 0) - column
    pick = jnp.where(at == 0, 1.0 - frac[0:1, :], jnp.where(at == 1, frac[0:1, :], 0.0))
    for number, part in enumerate(split_parts(pick)):
        for place in ((0, 1, 2), (3, 4), (5,))[number]:
            column_ref[place * columns : (place + 1) * columns, :] = part
    at = lax.broadcasted_iota(jnp.int32, (rows, count), 0) - row
    row_ref[...] = jnp.where(at == 0, 1.0 - frac[1:2, :], jnp.where(at == 1, frac[1:2, :], 0.0))


def split_parts(values):
    high = values.astype(jnp.bfloat16)
    rest = values - high.astype(jnp.float32)
    middle = rest.astype(jnp.bfloat16)
    low = (rest - middle.astype(jnp.float32)).astype(jnp.bfloat16)
    return high, middle, low


def split_values(values):
    high, middle, low = split_parts(values)
    return jnp.concatenate([high, middle, low, high, middle, high], axis=1)


def observe_mean(sizes, rank_ref, mean_ref, column_ref, row_ref, whole_ref):
    _, _, _, tiles, _ = sizes
    for tile in range(tiles):
        lanes = slice(tile * LANES, (tile + 1) * LANES)
        rank = rank_ref[tile]
        wet = jnp.where(rank >= 0, 1.0, 0.0)
        whole_ref[:, lanes] = mean_ref[jnp.maximum(rank, 0)] * wet
    picked = jnp.dot(split_values(whole_ref[...]), column_ref[...], preferred_element_type=jnp.float32)
    return jnp.sum(picked * row_ref[...], axis=0, keepdims=True)


def own_field_kernel(
    sizes, rank_ref, mean_ref, stepped_ref, column_ref, row_ref, field_hbm, mean_seen_ref, field_ref, whole_ref, sem
):
    members, _, _, _, _ = sizes
    core, _, _ = chunk_number()
    write_planes(sizes, core, rank_ref, mean_ref, stepped_ref, field_hbm, field_ref, sem)
    mean_seen_ref[...] = observe_mean(sizes, rank_ref, mean_ref, column_ref, row_ref, whole_ref)
    for copy in plane_copies(sizes, range(members), core, field_hbm, field_ref, sem):
        copy.wait()


def plane_copies(sizes, of_members, field, field_hbm, field_ref, sem):
    _, fields, rows, _, _ = sizes
    copies = []
    for member in of_members:
        for part in range(COPIES):
            at = pl.ds(part * rows // COPIES, rows // COPIES)
            target = field_hbm.at[member * fields + field, at]
            copies.append(pltpu.make_async_copy(field_ref.at[member, at], target, sem.at[member * COPIES + part]))
    return copies


def write_planes(sizes, field, rank_ref, mean_ref, stepped_ref, field_hbm, field_ref, sem):
    members, fields, _, tiles, _ = sizes
    for member in range(members):
        for tile in range(tiles):
            lanes = slice(tile * LANES, (tile + 1) * LANES)
            rank = rank_ref[tile]

            @pl.when(rank >= 0)
            def _():
                field_ref[member, :, lanes] = stepped_ref[member * fields + field, :, lanes] - mean_ref[rank]

            @pl.when(rank < 0)
            def _():
                field_ref[member, :, lanes] = stepped_ref[member * fields + field, :, lanes]

        for copy in plane_copies(sizes, [member], field, field_hbm, field_ref, sem):
            copy.start()


def final_kernel(
    sizes, ensemble, rank_ref, other_ref, column_ref, row_ref, own_seen_ref, seen_ref, stepped_ref, started_hbm,
    field_hbm, anomaly_hbm, variance_hbm, field_ref, whole_ref, anomaly_ref, variance_ref, sem,
):
    members, fields, _, _, _ = sizes
    core, _, _ = chunk_number()
    write_planes(sizes, 1 - core, rank_ref, other_ref, stepped_ref, field_hbm, field_ref, sem)
    own_seen = own_seen_ref[...]
    other_seen = observe_mean(sizes, rank_ref, other_ref, column_ref, row_ref, whole_ref)
    halves = row_ref.shape[1] // LANES
    stride = members * fields * halves
    sets = seen_ref.shape[0] // stride

    def tree(values):
        while len(values) > 1:
            values = [a + b for a, b in zip(values[0::2], values[1::2], strict=True)]
        return values[0]

    for field in range(fields):
        mean_seen = jnp.where(core == field, own_seen, other_seen)
        for half in range(halves):
            lanes = slice(half * LANES, (half + 1) * LANES)
            mean = mean_seen[:, lanes]
            observed = []
            for part in range(sets):
                for member in range(members):
                    at = part * stride + (member * fields + field) * halves + half
                    observed.append(seen_ref[at : at + 1, :] - mean)
            centre = tree(observed) / ensemble
            anomaly = [value - centre for value in observed]
            variance_ref[field : field + 1, lanes] = tree([value * value for value in anomaly]) / ensemble
            for member in range(members):
                anomaly_ref[member, field : field + 1, lanes] = anomaly[member]
    small = (
        pltpu.make_async_copy(anomaly_ref, anomaly_hbm, sem.at[members * COPIES]),
        pltpu.make_async_copy(variance_ref, variance_hbm, sem.at[members * COPIES + 1]),
    )
    for copy in small:
        copy.start()
    for copy in plane_copies(sizes, range(members), 1 - core, field_hbm, field_ref, sem):
        copy.wait()
    for copy in small:
        copy.wait()


def local(temp_salt, diffusivity, wet_rank, land_rows, obs_cell, obs_frac):
    members, fields, levels, rows, columns = temp_salt.shape
    tiles = wet_rank.shape[0]
    cores, level_count, member_count = (lax.axis_size(axis) for axis in ALL_AXES)
    slots = tiles * cores // 2
    chips = level_count * member_count
    bits = chips.bit_length() - 1
    assert cores == 2 and fields == 2 and members == 2 and levels == 1 and slots == 4
    assert columns == tiles * LANES and chips == 1 << bits and bits >= 3
    count = obs_cell.shape[0]
    planes = members * fields
    sizes = (members, fields, rows, tiles, slots)
    samples = members * levels * chips
    level_bit = bits - 1

    def device(core, chip):
        return core * chips + chip

    def exchange(value, masks):
        if masks is None:
            to = lambda core, chip: (1 - core, chip)
        else:
            to = lambda core, chip: (core, chip ^ masks[core])
        pairs = [(device(core, chip), device(*to(core, chip))) for core in range(2) for chip in range(chips)]
        return lax.ppermute(value, ALL_AXES, pairs)

    def struct(*shape):
        return jax.ShapeDtypeStruct(shape, jnp.float32)

    def call(name, kernel, out_shape, operands, scratch=(), cycles=1000, in_specs=None, out_specs=None, aliases={}):
        return pl.pallas_call(
            functools.partial(kernel, sizes),
            out_shape=out_shape,
            in_specs=in_specs or [SMEM if x.shape == wet_rank.shape else VMEM for x in operands],
            out_specs=out_specs or jax.tree.map(lambda _: VMEM, out_shape),
            scratch_shapes=list(scratch),
            input_output_aliases=aliases,
            compiler_params=STEP_PARAMS if name == "steps" else PARAMS,
            cost_estimate=pl.CostEstimate(flops=cycles * 4096, bytes_accessed=1 << 20, transcendentals=0),
        )(*operands)

    def halo(count):
        return pltpu.VMEM((2, count, slots, rows + 2 * PAD, LANES), jnp.float32)

    temp = temp_salt.reshape(planes, rows, columns)
    land = land_rows.reshape(tiles, LANES)
    cell = obs_cell.reshape(1, count)
    masks = {1: (1, 2), 2: (2, 1), 3: (3, 3)}

    inputs = tuple(pltpu.with_memory_space_constraint(x, pltpu.HBM) for x in (wet_rank, temp, land))
    send, keep, temp, land, rank = call(
        "sums", sums_kernel,
        (
            struct(slots, rows, LANES),
            struct(slots, rows, LANES),
            struct(planes, rows, columns),
            jax.ShapeDtypeStruct((tiles, LANES), jnp.int32),
            jax.ShapeDtypeStruct((tiles,), jnp.int32),
        ),
        inputs,
        scratch=[pltpu.SMEM((tiles,), jnp.int32), pltpu.SemaphoreType.DMA((4,))],
        in_specs=[HBM] * 3,
    )
    arrived = exchange(send, None)
    pack = call("pack", pack_kernel, struct(fields + 4, slots, rows, LANES), (rank, temp, diffusivity, land))
    packed = exchange(pack, None)
    total = keep + arrived
    got = [exchange(total[k], masks[k]) for k in (1, 2, 3)]
    total = (total[0] + got[0]) + (got[1] + got[2])

    face = pltpu.VMEM((4, slots, rows + 2 * PAD, LANES), jnp.float32)
    weights, own = call(
        "steps", member_kernel, (struct(9, slots, rows, LANES), struct(fields, slots, rows, LANES)),
        (rank, diffusivity, temp, land, packed), [halo(fields), face, face], cycles=6000,
    )
    other = exchange(own, None)
    stepped, seen = call(
        "observe", observe_kernel, (struct(planes, rows, columns), struct(planes * count // LANES, LANES)),
        (rank, own, other, cell, obs_frac), cycles=2000,
    )

    for bit in [level_bit] + list(range(2, level_bit)):
        mask = (1 << bit, 1 << bit)
        if bit == level_bit:
            total = total + exchange(total, mask)
        else:
            got = exchange(jnp.concatenate([total, seen], axis=0), mask)
            total = total + got[:rows]
            seen = jnp.concatenate([seen, got[rows:]], axis=0)
    payload = jnp.concatenate([total, seen], axis=0)
    got = [payload] + [exchange(payload, masks[k]) for k in (1, 2, 3)]
    gathered = jnp.stack([x[:rows] for x in got])
    seen = jnp.concatenate([x[rows:] for x in got], axis=0)

    def step_mean(sizes, *refs):
        mean_kernel(sizes, samples, *refs)

    own_mean = call("mean", step_mean, struct(slots, rows, LANES), (gathered, weights), [halo(1)], cycles=2000)
    other_mean = exchange(own_mean, None)
    column_picks, row_picks = call(
        "picks", picks_kernel,
        (jax.ShapeDtypeStruct((6 * columns, count), jnp.bfloat16), struct(rows, count)), (cell, obs_frac),
    )
    plane_scratch = pltpu.VMEM((members, rows, columns), jnp.float32)
    whole_scratch = pltpu.VMEM((rows, columns), jnp.float32)
    started, own_seen = call(
        "own_field", own_field_kernel, (struct(planes, rows, columns), struct(1, count)),
        (rank, own_mean, stepped, column_picks, row_picks),
        [plane_scratch, whole_scratch, pltpu.SemaphoreType.DMA((members * COPIES,))], out_specs=(HBM, VMEM),
    )

    def last_kernel(sizes, *refs):
        final_kernel(sizes, members * member_count, *refs)

    operands = (rank, other_mean, column_picks, row_picks, own_seen, seen, stepped, started)
    field, anomaly, variance = call(
        "recentre", last_kernel,
        (struct(planes, rows, columns), struct(members, fields, count), struct(fields, count)),
        operands,
        [
            plane_scratch,
            whole_scratch,
            pltpu.VMEM((members, fields, count), jnp.float32),
            pltpu.VMEM((fields, count), jnp.float32),
            pltpu.SemaphoreType.DMA((members * COPIES + 2,)),
        ],
        in_specs=[SMEM] + [VMEM] * 6 + [HBM],
        out_specs=(HBM, HBM, HBM),
        aliases={len(operands) - 1: 0},
    )
    return field.reshape(members, fields, levels, rows, columns), anomaly, variance


def solution(mesh):
    placed = (
        P("member", None, "level", None, "tile"),
        P(None, None, "tile"),
        P("tile"),
        P("tile"),
        P(("tile", "level")),
        P(None, ("tile", "level")),
    )

    return jax.shard_map(
        local,
        mesh=mesh,
        in_specs=placed,
        out_specs=(
            P("member", None, "level", None, "tile"),
            P("member", None, ("tile", "level")),
            P(None, ("tile", "level")),
        ),
        check_vma=False,
    )
```
